256 devices in a mesh: gx: 16 (over z, core), gy: 16 (over x, y).
Axes of the slice: x: 4, y: 4, z: 8, core: 2. Of those that a mesh axis runs over, the one named last changes fastest.
Arguments:
- particles: float32 [8, 2097152], P(None, ('gx', 'gy'))
- old_density: float32 [2097152], P(('gx', 'gy')), may hold values from 0.5 to 4
- active: int32 [2097152], P(('gx', 'gy')), may hold values 0 or 1
- send_rows: int32 [4, 524288], P(None, ('gx', 'gy')), may hold values from 0 to 8191, as said below
- send_count: int32 [4, 256], P(None, ('gx', 'gy')), may hold values from 682 to 2048, as said below
- export_rows: int32 [8, 262144], P(None, ('gx', 'gy')), may hold values from 0 to 8191
- pair_tiles: int32 [2, 131072], P(None, ('gx', 'gy')), may hold values from 0 to 255, as said below
- pair_count: int32 [256], P(('gx', 'gy')), may hold values from 128 to 512, as said below
Outputs:
- density: float32 [2097152], P(('gx', 'gy'))
- acceleration: float32 [3, 2097152], P(None, ('gx', 'gy'))
- heating: float32 [2097152], P(('gx', 'gy'))
The draws below stay inside these ranges and needn't reach their ends.
Inputs may be any that keep to these rules, and one draw needn't show every extreme that they name: `send_rows`: within one level and one device the 2048 offered rows are distinct local rows. `send_count`: the two devices that a level pairs have the same count; at every level some pair exchanges all 2048 offered rows. `pair_tiles`: a pair's source tile differs from its target tile; target tiles are below 128. `pair_count`: some device uses all 512 slots.
All inputs are finite; a program needn't handle non-finite values. No bound on the sum of `active` on one device may be relied on, other than what follows from the above.
Results may differ from the reference program's by a relative error of at most 0.0003.
Values sent between devices are 32-bit elements; how exact they have to be, the bound alone decides.
A program may use at most 64 MiB of HBM per device.

```python
import math
import jax
import jax.numpy as jnp
from jax import lax

ROWS = 8192
NPAIR = 512
LEVELS = 4
FIELDS = 8
TILE = 64
SEND = 2048
GHOSTS = 1024
NTILE = 128
POOLT = 256
PARTS_SIZE = 2097152
N_GX = 16
N_GY = 16


def draw_particles(key, part):
    keys = jax.random.split(key, 4)
    position = jax.random.uniform(keys[0], (3, PARTS_SIZE), jnp.float32)
    velocity = jax.random.normal(keys[1], (3, PARTS_SIZE), jnp.float32)
    smooth = jax.random.uniform(keys[2], (1, PARTS_SIZE), jnp.float32, 0.12, 0.25)
    energy = jnp.exp(jax.random.uniform(keys[3], (1, PARTS_SIZE), jnp.float32, jnp.log(0.5), jnp.log(2.0)))
    return jnp.concatenate([position, velocity, smooth, energy], axis=0)


def draw_send_rows(key, part):
    devices = N_GX * N_GY
    keys = jax.random.split(key, LEVELS * devices)
    chosen = jax.vmap(lambda k: jax.random.permutation(k, ROWS)[:SEND])(keys)
    return chosen.reshape(LEVELS, devices * SEND).astype(jnp.int32)


def draw_send_count(key, part):
    devices = N_GX * N_GY
    bits_x = N_GX.bit_length() - 1
    bits_y = N_GY.bit_length() - 1
    masks = (1 << bits_y + bits_x - 1, 1 << bits_y + bits_x - 2, 1 << bits_y - 1, 1 << bits_y - 2)
    raw = jax.random.randint(key, (LEVELS, devices), SEND // 3, SEND + 1, dtype=jnp.int32)
    raw = raw.at[:, 0].set(SEND)
    ranks = jnp.arange(devices, dtype=jnp.int32)
    result = []
    for section_level in range(LEVELS):
        lower = jnp.bitwise_and(ranks, devices - 1 - masks[section_level])
        result.append(raw[section_level][lower])
    return jnp.stack(result, axis=0)


def draw_pair_tiles(key, part):
    devices = N_GX * N_GY
    keys = jax.random.split(jax.random.fold_in(key, 11), 2)
    targets = jax.random.randint(keys[0], (devices * NPAIR,), 0, NTILE, dtype=jnp.int32)
    raw = jax.random.randint(keys[1], (devices * NPAIR,), 0, POOLT - 1, dtype=jnp.int32)
    sources = raw + (raw >= targets).astype(jnp.int32)
    return jnp.stack([targets, sources], axis=0)


def draw_pair_count(key, part):
    devices = N_GX * N_GY
    counts = jax.random.randint(jax.random.fold_in(key, 23), (devices,), NPAIR // 4, NPAIR + 1, dtype=jnp.int32)
    return counts.at[0].set(NPAIR)


def plant(values, own_key, smallest, high):
    shape = values.shape
    place = [jax.random.randint(jax.random.fold_in(own_key, axis), (), 0, shape[axis]) for axis in range(len(shape))]
    values = values.at[tuple(place)].set(smallest)
    longest = shape.index(max(shape))
    place[longest] = (place[longest] + 1) % shape[longest]
    return values.at[tuple(place)].set(high)


def shard_levels(key, shape, cuts, smallest, top_value):
    def one(axis_at, blocks):
        draws = jax.random.uniform(jax.random.fold_in(jax.random.fold_in(key, 6), axis_at), (blocks,), jnp.float32, smallest / len(cuts), top_value / len(cuts))
        return jnp.repeat(jnp.exp(draws), shape[axis_at] // blocks).reshape((-1,) + (1,) * (len(shape) - axis_at - 1))

    loudness = one(*cuts[0])
    for cut in cuts[1:]:
        loudness = loudness * one(*cut)
    return loudness


def setup_inputs(seed: int = 0) -> dict:
    key_list = jax.random.split(jax.random.key(seed), 9)
    return {
        "particles": draw_particles(jax.random.fold_in(key_list[8], 71), 0),
        "old_density": jnp.clip(jnp.exp(math.log(4.0) - 2.0794415 * jax.random.uniform(key_list[1], (PARTS_SIZE,), jnp.float32) ** shard_levels(key_list[1], (PARTS_SIZE,), ((0, 256),), -0.2, 0.2)), 0.5, 4.0),
        "active": plant((jax.random.randint(key_list[2], (PARTS_SIZE,), 0, 4) < 1).astype(jnp.int32), jax.random.fold_in(key_list[2], 1), 0, 1),
        "send_rows": draw_send_rows(jax.random.fold_in(key_list[8], 71), 0),
        "send_count": draw_send_count(jax.random.fold_in(key_list[8], 71), 0),
        "export_rows": plant(jax.random.randint(key_list[5], (8, GHOSTS * N_GX * N_GY), 0, ROWS), jax.random.fold_in(key_list[5], 1), 0, ROWS - 1).astype(jnp.int32),
        "pair_tiles": draw_pair_tiles(jax.random.fold_in(key_list[8], 71), 0),
        "pair_count": draw_pair_count(jax.random.fold_in(key_list[8], 71), 0),
    }


PARTICLE_MASS = 1.0 / 512.0
ADIABATIC = 5.0 / 3.0
directions = ((-1, -1), (-1, 0), (-1, 1), (0, -1), (0, 1), (1, -1), (1, 0), (1, 1))

def kernel_value(dist_sq, smooth):
    q = jnp.sqrt(dist_sq) / smooth
    inner_part = 1.0 - 1.5 * q * q + 0.75 * q * q * q
    outer_part = 0.25 * (2.0 - q) ** 3
    profile = jnp.where(q < 1.0, inner_part, jnp.where(q < 2.0, outer_part, 0.0))
    return profile / (jnp.pi * smooth * smooth * smooth)

def kernel_slope(dist_sq, smooth):
    q = jnp.sqrt(dist_sq) / smooth
    inner_part = -3.0 + 2.25 * q
    outer_part = -0.75 * (2.0 - q) ** 2 / jnp.maximum(q, 1.0)
    profile = jnp.where(q < 1.0, inner_part, jnp.where(q < 2.0, outer_part, 0.0))
    return profile / (jnp.pi * smooth ** 5)

def separation(target_rows, source_rows):
    offset = target_rows[0:3, :, :, None] - source_rows[0:3, :, None, :]
    offset = offset - jnp.floor(offset + 0.5)
    return (offset, lax.optimization_barrier(jnp.sum(offset * offset, axis=0)))

def tile_select(targets, in_list, tile_count):
    return ((targets[:, None] == jnp.arange(tile_count)[None, :]) & in_list[:, None]).astype(jnp.float32)

def density_block(tile_view, targets, sources, in_list, tile_count):
    target_rows = jnp.take(tile_view, targets, axis=1)
    source_rows = jnp.take(tile_view, sources, axis=1)
    offset, dist_sq = separation(target_rows, source_rows)
    terms = PARTICLE_MASS * lax.optimization_barrier(jnp.sum(kernel_value(dist_sq, target_rows[6][:, :, None]), axis=2))
    onehot = tile_select(targets, in_list, tile_count)
    return jnp.einsum('bt,br->tr', onehot, terms, precision=lax.Precision.HIGHEST)

def force_block(tile_view, press_view, targets, sources, in_list, tile_count):
    target_rows = jnp.take(tile_view, targets, axis=1)
    source_rows = jnp.take(tile_view, sources, axis=1)
    target_press = jnp.take(press_view, targets, axis=0)
    source_press = jnp.take(press_view, sources, axis=0)
    offset, dist_sq = separation(target_rows, source_rows)
    slope = 0.5 * (kernel_slope(dist_sq, target_rows[6][:, :, None]) + kernel_slope(dist_sq, source_rows[6][:, None, :]))
    weight_pair = PARTICLE_MASS * (target_press[:, :, None] + source_press[:, None, :]) * slope
    acceleration = -lax.optimization_barrier(jnp.sum(weight_pair[None] * offset, axis=3))
    velocity_gap = target_rows[3:6, :, :, None] - source_rows[3:6, :, None, :]
    heating = 0.5 * lax.optimization_barrier(jnp.sum(weight_pair * lax.optimization_barrier(jnp.sum(velocity_gap * offset, axis=0)), axis=2))
    terms = jnp.concatenate([acceleration, heating[None]], axis=0)
    onehot = tile_select(targets, in_list, tile_count)
    return jnp.einsum('bt,kbr->ktr', onehot, terms, precision=lax.Precision.HIGHEST)

def device_density(pooled, pair_lists, used):
    tile_view = pooled.reshape(FIELDS, -1, TILE)
    tile_count = ROWS // TILE
    block_size = math.gcd(NPAIR, 64)

    def advance(running, which):
        begin = which * block_size
        targets = lax.dynamic_slice_in_dim(pair_lists[0], begin, block_size)
        sources = lax.dynamic_slice_in_dim(pair_lists[1], begin, block_size)
        in_list = begin + jnp.arange(block_size) < used
        return (running + density_block(tile_view, targets, sources, in_list, tile_count), None)
    start = jnp.zeros((tile_count, TILE), jnp.float32)
    total, _ = lax.scan(advance, start, jnp.arange(NPAIR // block_size))
    return total.reshape(ROWS)

def device_force(pooled, press_pool, pair_lists, used):
    tile_view = pooled.reshape(FIELDS, -1, TILE)
    press_view = press_pool.reshape(-1, TILE)
    tile_count = ROWS // TILE
    block_size = math.gcd(NPAIR, 64)

    def advance(running, which):
        begin = which * block_size
        targets = lax.dynamic_slice_in_dim(pair_lists[0], begin, block_size)
        sources = lax.dynamic_slice_in_dim(pair_lists[1], begin, block_size)
        in_list = begin + jnp.arange(block_size) < used
        return (running + force_block(tile_view, press_view, targets, sources, in_list, tile_count), None)
    start = jnp.zeros((4, tile_count, TILE), jnp.float32)
    total, _ = lax.scan(advance, start, jnp.arange(NPAIR // block_size))
    return total.reshape(4, ROWS)

def reference(particles, old_density, active, send_rows, send_count, export_rows, pair_tiles, pair_count):
    size_x = N_GX
    size_y = N_GY
    devices = size_x * size_y
    fields = particles.reshape(FIELDS, size_x, size_y, ROWS).transpose(1, 2, 0, 3)
    density_rows = old_density.reshape(size_x, size_y, ROWS)
    active_rows = active.reshape(size_x, size_y, ROWS)
    bits_x = size_x.bit_length() - 1
    bits_y = size_y.bit_length() - 1
    bisections = ((0, bits_x - 1), (0, bits_x - 2), (1, bits_y - 1), (1, bits_y - 2))
    for section_level in range(LEVELS):
        which_axis, bit_number = bisections[section_level]
        slots = send_rows[section_level].reshape(size_x, size_y, SEND)
        offered = send_count[section_level].reshape(size_x, size_y)
        taken = jnp.arange(SEND)[None, None, :] < offered[:, :, None]
        out_fields = jnp.take_along_axis(fields, slots[:, :, None, :], axis=3)
        out_density = jnp.take_along_axis(density_rows, slots, axis=2)
        out_active = jnp.take_along_axis(active_rows, slots, axis=2)
        extent = size_x if which_axis == 0 else size_y
        partner = jnp.bitwise_xor(jnp.arange(extent, dtype=jnp.int32), 1 << bit_number)
        in_fields = jnp.take(out_fields, partner, axis=which_axis)
        in_density = jnp.take(out_density, partner, axis=which_axis)
        in_active = jnp.take(out_active, partner, axis=which_axis)
        new_fields = jnp.where(taken[:, :, None, :], in_fields, out_fields)
        new_density = jnp.where(taken, in_density, out_density)
        new_active = jnp.where(taken, in_active, out_active)
        fields = jax.vmap(jax.vmap(lambda a, i, v: a.at[:, i].set(v)))(fields, slots, new_fields)
        density_rows = jax.vmap(jax.vmap(lambda a, i, v: a.at[i].set(v)))(density_rows, slots, new_density)
        active_rows = jax.vmap(jax.vmap(lambda a, i, v: a.at[i].set(v)))(active_rows, slots, new_active)
    exports = export_rows.reshape(8, size_x, size_y, GHOSTS)
    ghost_blocks = []
    for number in range(8):
        step_x, step_y = directions[number]
        portion = jnp.take_along_axis(fields, exports[number][:, :, None, :], axis=3)
        ghost_blocks.append(jnp.roll(portion, (step_x, step_y), axis=(0, 1)))
    pooled = jnp.concatenate([fields] + ghost_blocks, axis=3).reshape(devices, FIELDS, -1)
    pair_lists = pair_tiles.reshape(2, devices, NPAIR).transpose(1, 0, 2)
    kernel_sums = lax.map(lambda item: device_density(item[0], item[1], item[2]), (pooled, pair_lists, pair_count))
    smooth = fields[:, :, 6, :].reshape(devices, ROWS)
    recomputed = PARTICLE_MASS * kernel_value(jnp.zeros_like(smooth), smooth) + kernel_sums
    flat_active = active_rows.reshape(devices, ROWS)
    density_new = jnp.where(flat_active == 1, recomputed, density_rows.reshape(devices, ROWS))
    density_grid = density_new.reshape(size_x, size_y, ROWS)
    ghost_density = []
    for number in range(8):
        step_x, step_y = directions[number]
        portion = jnp.take_along_axis(density_grid, exports[number], axis=2)
        ghost_density.append(jnp.roll(portion, (step_x, step_y), axis=(0, 1)))
    pool_density = jnp.concatenate([density_grid] + ghost_density, axis=2).reshape(devices, -1)
    press_pool = (ADIABATIC - 1.0) * pooled[:, 7, :] / pool_density
    forces = lax.map(lambda item: device_force(item[0], item[1], item[2], item[3]), (pooled, press_pool, pair_lists, pair_count))
    forces = forces * flat_active.astype(jnp.float32)[:, None, :]
    acceleration = forces[:, 0:3, :].transpose(1, 0, 2).reshape(3, devices * ROWS)
    heating = forces[:, 3, :].reshape(devices * ROWS)
    return (density_new.reshape(devices * ROWS), acceleration, heating)
```

```python
import functools
import math

import jax
import jax.numpy as jnp
from jax import lax
from jax.experimental import pallas as pl
from jax.experimental.pallas import tpu as pltpu
from jax.sharding import PartitionSpec as P

F32 = jnp.float32
BF16 = jnp.bfloat16
I32 = jnp.int32
MASS = 1.0 / 512.0
NEAR = 1e-30
FAR = 1e36
NT_DIMS = (((1,), (1,)), ((), ()))
COLS = 320
ITEMS = 2560
UNROLL = 8


def iota(shape, axis):
    return lax.broadcasted_iota(I32, shape, axis)


def split3(x):
    a = x.astype(BF16)
    r = x - a.astype(F32)
    b = r.astype(BF16)
    c = (r - b.astype(F32)).astype(BF16)
    return a, b, c


def dot(a, b):
    return jnp.dot(a, b, preferred_element_type=F32)


def dot_nt(a, b):
    return lax.dot_general(a, b, NT_DIMS, preferred_element_type=F32)


def swap_halves(x):
    return pltpu.roll(x, 64, x.ndim - 1)


def ranks_of(active):
    rows, cols = iota((256, 256), 0), iota((256, 256), 1)
    before = ((rows // 64 == cols // 64) & (rows < cols)).astype(F32).astype(BF16)
    rank = dot(active.astype(BF16), before)
    return jnp.where(active > 0.5, rank, -1.0)


def tile_groups(active):
    rows, cols = iota((256, 128), 0), iota((256, 128), 1)
    pick = (rows // 64 == cols % 4).astype(F32).astype(BF16)
    count = dot(active.astype(BF16), pick)
    own = iota((32, 128), 0) == iota((32, 128), 1) // 4
    total = jnp.sum(jnp.where(own, count, 0.0), axis=0, keepdims=True)
    return jnp.floor((total + 7.0) * 0.125)


def item_codes(pairs, used, groups):
    target, source = pairs[0:1], pairs[1:2]
    target_col = pairs.T[:, 0:1]
    count = pairs.shape[1]
    lane = iota((1, count), 1)
    used_row = lane < used
    q, p = iota((count, count), 0), iota((count, count), 1)
    same = (target_col == target) & (q < p) & (q < used)
    order = jnp.sum(jnp.where(same, 1.0, 0.0), axis=0, keepdims=True)
    at = (iota((128, count), 0).astype(F32) == target) & used_row
    at_f = jnp.where(at, 1.0, 0.0)
    number = jnp.sum(at_f, axis=1, keepdims=True)
    columns = jnp.floor((number + 1.0) * 0.5)
    below = (iota((128, 128), 0) > iota((128, 128), 1)).astype(F32).astype(BF16)
    first = dot(below, jnp.broadcast_to(columns, (128, 128)).astype(BF16))[:, 0:1]
    groups_row = dot(groups.astype(BF16), at_f.astype(BF16))
    first_row = jnp.sum(at_f * first, axis=0, keepdims=True)
    half = jnp.floor(order * 0.5)
    column = first_row + half
    second = jnp.where(order - 2.0 * half > 0.5, 1.0, 0.0)
    use = jnp.where(used_row, 1.0, 0.0)
    lead = use * (1.0 - second)
    trail = use * second
    values = jnp.concatenate(
        [target * lead, source * lead, source * trail, trail, groups_row * lead, lead * 0.0, lead * 0.0, lead * 0.0],
        axis=0,
    ).astype(BF16)
    match = jnp.where((iota((COLS, count), 0).astype(F32) == column) & used_row, 1.0, 0.0).astype(BF16)
    in_row = dot_nt(values, match)
    in_col = dot_nt(match, values)
    upper = (iota((COLS, COLS), 0) < iota((COLS, COLS), 1)).astype(F32).astype(BF16)
    lower = (iota((COLS, COLS), 0) > iota((COLS, COLS), 1)).astype(F32).astype(BF16)
    start_row = dot(in_row.astype(BF16), upper)[4:5]
    start_col = dot(lower, in_col.astype(BF16))[:, 4:5]
    size_col = in_col[:, 4:5]
    total = jnp.sum(size_col, axis=0, keepdims=True)
    high = jnp.floor(start_row * (1.0 / 256.0))
    second_source = in_row[2:3] + 256.0 * (1.0 - in_row[3:4])
    table = jnp.concatenate(
        [in_row[0:2], second_source, high, start_row - 256.0 * high, high * 0.0, high * 0.0, high * 0.0], axis=0
    ).astype(BF16)
    item = iota((1, ITEMS), 1).astype(F32)
    inside = jnp.where((item >= start_col) & (item < start_col + size_col), 1.0, 0.0).astype(BF16)
    found = dot(table, inside)
    beyond = item >= total
    group = item - 256.0 * found[3:4] - found[4:5]
    place = jnp.where(beyond, 0.0, group * 128.0 + found[0:1]).astype(I32)
    first_source = jnp.where(beyond, 256.0, found[1:2]).astype(I32)
    other = jnp.where(beyond, 256.0, found[2:3]).astype(I32)
    return place + first_source * 1024 + other * (1 << 19), total.astype(I32)


def put_sources(table, slot, chunk):
    left = iota(chunk.shape, 1) < 64
    other = swap_halves(chunk)
    table[slot] = jnp.where(left, chunk, other)
    table[slot + 1] = jnp.where(left, other, chunk)


def put_targets(columns, tile, chunk, rank):
    fields = chunk.shape[0]
    left = iota(chunk.shape, 1) < 64
    a, b, c = [v.astype(F32) for v in split3(chunk)]
    ar, br, cr = swap_halves(a), swap_halves(b), swap_halves(c)
    zero = jnp.zeros_like(a)
    wide = jnp.broadcast_to(rank, (8, 128))
    wide_other = swap_halves(wide)
    left8 = iota((8, 128), 1) < 64
    for half in range(2):
        if half == 0:
            right = jnp.concatenate([jnp.where(left, a, br), jnp.where(left, c, zero)], axis=1)
            own = jnp.where(left8, wide, wide_other)
        else:
            right = jnp.concatenate([jnp.where(left, ar, b), jnp.where(left, cr, zero)], axis=1)
            own = jnp.where(left8, wide_other, wide)
        sub = iota((8, 128), 0).astype(F32)
        pick = jnp.concatenate([jnp.where(own == sub + 8.0 * g, 1.0, 0.0) for g in range(8)], axis=0).astype(BF16)
        rows = dot_nt(jnp.concatenate([pick, pick], axis=1), right.astype(BF16))
        for g in range(8):
            columns[pl.ds(g * 1024 + (tile + half) * 8, 8), :] = rows[8 * g : 8 * g + 8]


def gather_sums(totals, tile, rank, highest):
    left = iota((8, 128), 1) < 64
    wide = jnp.broadcast_to(rank, (8, 128))
    sub = iota((8, 128), 0).astype(F32)
    out = [jnp.zeros((8, 128), F32) for _ in totals]
    for g in range(8):
        hit = wide == sub + 8.0 * g
        for n, total in enumerate(totals):
            one = jnp.sum(total[pl.ds(g * 1024 + tile * 8, 8), :], axis=1, keepdims=True)
            two = jnp.sum(total[pl.ds(g * 1024 + tile * 8 + 8, 8), :], axis=1, keepdims=True)
            out[n] = out[n] + jnp.where(hit, jnp.where(left, one, two), 0.0)
    return [jnp.sum(o, axis=0, keepdims=True) for o in out]


def wrapped(a, b):
    s = a - b
    return s - jnp.floor(s + 0.5)


def decode(code):
    return code & 1023, (code >> 10) & 511, code >> 19


def density_item(code, columns, sources, total):
    place, one, two = decode(code)
    row = pl.multiple_of(place * 8, 8)
    mine = columns[pl.ds(row, 8), :]
    left = iota((8, 128), 1) < 64
    other = jnp.where(left, sources[one], sources[two])
    dx = wrapped(mine[:, 0:1], other[0:1])
    dy = wrapped(mine[:, 1:2], other[1:2])
    dz = wrapped(mine[:, 2:3], other[2:3])
    rsq = jnp.maximum(dx * dx + dy * dy + dz * dz, other[3:4])
    q = rsq * lax.rsqrt(rsq) * mine[:, 3:4]
    t = jnp.maximum(2.0 - q, 0.0)
    u = jnp.maximum(1.0 - q, 0.0)
    w = t * t * t - 4.0 * (u * u * u)
    return row, w


def force_item(code, columns, sources):
    place, one, two = decode(code)
    row = pl.multiple_of(place * 8, 8)
    mine = columns[pl.ds(row, 8), :]
    left = iota((16, 128), 1) < 64
    other = jnp.where(left, sources[one], sources[two])
    dx = wrapped(mine[:, 0:1], other[0:1])
    dy = wrapped(mine[:, 1:2], other[1:2])
    dz = wrapped(mine[:, 2:3], other[2:3])
    rsq = jnp.maximum(dx * dx + dy * dy + dz * dz, other[10:11])
    inv = lax.rsqrt(rsq)
    r = rsq * inv

    def profile(h, hinv):
        q = r * hinv
        t = jnp.maximum(2.0 - q, 0.0)
        return jnp.where(q < 1.0, 4.0 - 3.0 * q, t * t * (h * inv))

    slope = profile(mine[:, 6:7], mine[:, 8:9]) * mine[:, 9:10] + profile(other[6:7], other[8:9]) * other[9:10]
    w = (mine[:, 7:8] + other[7:8]) * slope
    gap = (
        (mine[:, 3:4] - other[3:4]) * dx
        + (mine[:, 4:5] - other[4:5]) * dy
        + (mine[:, 5:6] - other[5:6]) * dz
    )
    return row, (w * dx, w * dy, w * dz, w * gap)


def density_kernel(count_ref, pairs_ref, own_ref, extra_ref, ghost_ref, dens_ref, code_ref, number_ref, rank_ref,
                   sources, columns, total, kept, codes_s, sem):
    extra = extra_ref[...].reshape(32, 2, 256)
    active = extra[:, 1, :]
    rank = ranks_of(active)
    for part in range(2):
        lanes = slice(128 * part, 128 * part + 128)
        rank_ref[pl.ds(part, 32, stride=2), :] = rank[:, lanes]
        kept[pl.ds(part, 32, stride=2), :] = extra[:, 0, lanes]
    pairs = jnp.concatenate([pairs_ref[...].astype(F32), jnp.zeros((6, 512), F32)], axis=0)
    codes, number = item_codes(pairs, count_ref[0], tile_groups(active))
    code_ref[...] = jnp.broadcast_to(codes, (8, ITEMS))
    code_ref[1:2, 0:128] = jnp.broadcast_to(number, (1, 128))
    copy = pltpu.make_async_copy(code_ref, codes_s, sem)
    copy.start()

    def fields(block):
        width = block.shape[1]
        keep = iota((8, width), 0) < 3
        floor = jnp.where(iota((8, width), 0) == 3, NEAR, 0.0)
        return jnp.where(keep, block, floor)

    def targets(block):
        hinv = 1.0 / block[6:7]
        sub = iota((8, block.shape[1]), 0)
        return jnp.where(sub < 3, block, jnp.where(sub == 3, hinv, 0.0))

    @pl.loop(0, 32)
    def _(hi):
        at = pl.multiple_of(hi * 256, 256)
        for part in range(2):
            rank = rank_ref[pl.ds(hi * 2 + part, 1), :]
            block = own_ref[:, pl.ds(at + 128 * part, 128)]
            tile = hi * 4 + 2 * part
            put_sources(sources, tile, fields(block))
            put_targets(columns, tile, targets(block), rank)
            put_sources(sources, tile + 128, fields(ghost_ref[:, pl.ds(at + 128 * part, 128)]))
            for g in range(8):
                total[pl.ds(g * 1024 + tile * 8, 16), :] = jnp.zeros((16, 128), F32)
    sources[256] = jnp.where(iota((8, 128), 0) == 3, FAR, 0.0)
    copy.wait()
    number_ref[0] = codes_s[1, 0]

    @pl.loop(0, (codes_s[1, 0] + UNROLL - 1) // UNROLL)
    def _(step):
        for u in range(UNROLL):
            row, w = density_item(codes_s[0, step * UNROLL + u], columns, sources, total)
            total[pl.ds(row, 8), :] += w

    @pl.loop(0, 32)
    def _(hi):
        at = pl.multiple_of(hi * 256, 256)
        for part in range(2):
            rank = rank_ref[pl.ds(hi * 2 + part, 1), :]
            (got,) = gather_sums([total], hi * 4 + 2 * part, rank, None)
            h = own_ref[6:7, pl.ds(at + 128 * part, 128)]
            fresh = MASS / math.pi / (h * h * h) * (1.0 + 0.25 * got)
            old = kept[pl.ds(hi * 2 + part, 1), :]
            dens_ref[pl.ds(hi * 2 + part, 1), :] = jnp.where(rank >= 0.0, fresh, old)


def force_kernel(number_ref, code_ref, own_ref, ghost_ref, dens_ref, gdens_ref, rank_ref, acc_ref, heat_ref,
                 sources, columns, ax, ay, az, heat):
    def fields(block, density):
        width = block.shape[1]
        h = block[6:7]
        press = (5.0 / 3.0 - 1.0) * block[7:8] / density
        hinv = 1.0 / h
        scale = (0.375 * MASS / math.pi) / (h * h * h * h * h)
        zero = jnp.zeros((5, width), F32)
        near = jnp.full((1, width), NEAR, F32)
        return jnp.concatenate([block[0:7], press, hinv, scale, near, zero], axis=0)

    @pl.loop(0, 32)
    def _(hi):
        at = pl.multiple_of(hi * 256, 256)
        for part in range(2):
            rank = rank_ref[pl.ds(hi * 2 + part, 1), :]
            tile = hi * 4 + 2 * part
            own = fields(own_ref[:, pl.ds(at + 128 * part, 128)], dens_ref[pl.ds(hi * 2 + part, 1), :])
            put_sources(sources, tile, own)
            put_targets(columns, tile, own, rank)
            put_sources(
                sources,
                tile + 128,
                fields(ghost_ref[:, pl.ds(at + 128 * part, 128)], gdens_ref[pl.ds(hi * 2 + part, 1), :]),
            )
            for g in range(8):
                for total in (ax, ay, az, heat):
                    total[pl.ds(g * 1024 + tile * 8, 16), :] = jnp.zeros((16, 128), F32)
    sub = iota((16, 128), 0)
    sources[256] = jnp.where(sub == 10, FAR, jnp.where((sub == 6) | (sub == 8), 1.0, 0.0))

    @pl.loop(0, (number_ref[0] + UNROLL - 1) // UNROLL)
    def _(step):
        for u in range(UNROLL):
            row, terms = force_item(code_ref[0, step * UNROLL + u], columns, sources)
            for total, term in zip((ax, ay, az, heat), terms):
                total[pl.ds(row, 8), :] += term

    @pl.loop(0, 32)
    def _(hi):
        at = pl.multiple_of(hi * 256, 256)
        for part in range(2):
            rank = rank_ref[pl.ds(hi * 2 + part, 1), :]
            got = gather_sums([ax, ay, az, heat], hi * 4 + 2 * part, rank, None)
            for n in range(3):
                acc_ref[n : n + 1, pl.ds(at + 128 * part, 128)] = got[n]
            heat_ref[pl.ds(hi * 2 + part, 1), :] = -0.5 * got[3]


VM = pl.BlockSpec(memory_space=pltpu.VMEM)
SM = pl.BlockSpec(memory_space=pltpu.SMEM)


def density_step(pair_count, pair_tiles, own, extra, ghost):
    return pl.pallas_call(
        density_kernel,
        name="density",
        out_shape=(
            jax.ShapeDtypeStruct((64, 128), F32),
            jax.ShapeDtypeStruct((8, ITEMS), I32),
            jax.ShapeDtypeStruct((1,), I32),
            jax.ShapeDtypeStruct((64, 128), F32),
        ),
        in_specs=[SM, VM, VM, VM, VM],
        out_specs=(VM, VM, SM, VM),
        scratch_shapes=[
            pltpu.VMEM((257, 8, 128), F32),
            pltpu.VMEM((8192, 8), F32),
            pltpu.VMEM((8192, 128), F32),
            pltpu.VMEM((64, 128), F32),
            pltpu.SMEM((8, ITEMS), I32),
            pltpu.SemaphoreType.DMA,
        ],
        compiler_params=pltpu.CompilerParams(vmem_limit_bytes=48 << 20),
    )(pair_count, pair_tiles, own, extra, ghost)


def force_step(number, codes, own, ghost, density, ghost_density, rank):
    return pl.pallas_call(
        force_kernel,
        name="force",
        out_shape=(jax.ShapeDtypeStruct((3, 8192), F32), jax.ShapeDtypeStruct((64, 128), F32)),
        in_specs=[SM, SM, VM, VM, VM, VM, VM],
        out_specs=(VM, VM),
        scratch_shapes=[pltpu.VMEM((257, 16, 128), F32), pltpu.VMEM((8192, 16), F32)]
        + [pltpu.VMEM((8192, 128), F32)] * 4,
        compiler_params=pltpu.CompilerParams(vmem_limit_bytes=48 << 20),
    )(number, codes, own, ghost, density, ghost_density, rank)


LEVELS = 4
SEND = 2048
PIECE = 512
PIECES = SEND // PIECE
GHOSTS = 1024
MESH = pl.DeviceIdType.MESH


def flipped(index, bit):
    step = 1 << bit
    return index + step - 2 * step * ((index // step) % 2)


def neighbour(number, sign, count_x, count_y):
    cell = number + number // 4
    i = (lax.axis_index("gx") + sign * (cell // 3 - 1) + count_x) % count_x
    j = (lax.axis_index("gy") + sign * (cell % 3 - 1) + count_y) % count_y
    return i, j


def one_hot(index_row):
    low = jnp.bitwise_and(index_row, 255)
    return jnp.where(iota((256, index_row.shape[1]), 0) == low, 1.0, 0.0).astype(BF16)


def put_parts(parts, row, value):
    for n, part in enumerate(split3(value)):
        parts[n, row : row + 16, :] = part


def spread_state(own, extra, parts):
    for h in range(0, 32, 2):
        pair = jnp.concatenate([own[:, h * 256 : h * 256 + 256], own[:, h * 256 + 256 : h * 256 + 512]], axis=0)
        put_parts(parts, h * 8, pair)
    if extra is not None:
        for a in range(4):
            put_parts(parts, 256 + a * 16, extra[16 * a : 16 * a + 16, :])


def pick(parts, rows, hot):
    return dot(parts[0, 0:rows, :], hot) + dot(parts[1, 0:rows, :], hot) + dot(parts[2, 0:rows, :], hot)


def by_block(found, high, blocks, first):
    out = found[first : first + 8]
    for h in range(1, blocks):
        out = jnp.where(high == h, found[first + 8 * h : first + 8 * h + 8], out)
    return out


def exchange_kernel(count_x, count_y, counts, particles, extra_in, rows, exports, own, extra, ghost,
                    hots, hots_x, exports_3, parts, placed, marks, send_main, send_extra, recv_main, recv_extra,
                    send_ghost, send_sems, recv_sems, ghost_send, ghost_recv):
    i, j = lax.axis_index("gx"), lax.axis_index("gy")
    bits_x, bits_y = count_x.bit_length() - 1, count_y.bit_length() - 1
    partners = [
        (flipped(i, bits_x - 1), j),
        (flipped(i, bits_x - 2), j),
        (i, flipped(j, bits_y - 1)),
        (i, flipped(j, bits_y - 2)),
    ]
    barrier = pltpu.get_barrier_semaphore()
    for partner in partners:
        pl.semaphore_signal(barrier, inc=1, device_id=partner, device_id_type=MESH)
    for number in range(8):
        pl.semaphore_signal(barrier, inc=1, device_id=neighbour(number, 1, count_x, count_y), device_id_type=MESH)

    def level_hot(level):
        for piece in range(PIECES):
            at = piece * PIECE
            hots[level, :, at : at + PIECE] = one_hot(rows[level : level + 1, at : at + PIECE])

    def export_hots():
        for number in range(8):
            exports_3[number] = exports[number : number + 1, :]

        @pl.loop(0, 8)
        def _(number):
            hots_x[number] = one_hot(exports_3[number])

    def main_copy(level, piece):
        lanes = pl.ds(piece * PIECE, PIECE)
        return pltpu.make_async_remote_copy(
            src_ref=send_main.at[level, :, lanes],
            dst_ref=recv_main.at[level, :, lanes],
            send_sem=send_sems.at[level, piece],
            recv_sem=recv_sems.at[level, piece],
            device_id=partners[level],
            device_id_type=MESH,
        )

    def extra_copy(level):
        return pltpu.make_async_remote_copy(
            src_ref=send_extra.at[level],
            dst_ref=recv_extra.at[level],
            send_sem=send_sems.at[level, PIECES],
            recv_sem=recv_sems.at[level, PIECES],
            device_id=partners[level],
            device_id_type=MESH,
        )

    def ghost_copy(number):
        lanes = pl.ds(pl.multiple_of(number * GHOSTS, GHOSTS), GHOSTS)
        return pltpu.make_async_remote_copy(
            src_ref=send_ghost.at[:, lanes],
            dst_ref=ghost.at[:, lanes],
            send_sem=ghost_send.at[number],
            recv_sem=ghost_recv.at[number],
            device_id=neighbour(number, 1, count_x, count_y),
            device_id_type=MESH,
        )

    own[...] = particles[...]
    extra[...] = extra_in[...]
    level_hot(0)
    sub8 = iota((8, PIECE), 0)

    for level in range(LEVELS):
        spread_state(own, extra, parts)
        for piece in range(PIECES):
            at = piece * PIECE
            high = jnp.broadcast_to(rows[level : level + 1, at : at + PIECE] // 256, (8, PIECE))
            found = pick(parts, 320, hots[level, :, at : at + PIECE])
            send_main[level, :, at : at + PIECE] = by_block(found, high, 32, 0)
            both = by_block(found, high // 4, 8, 256)
            both = jnp.where(sub8 // 2 == high % 4, both, 0.0)
            both = both + pltpu.roll(both, 4, 0)
            both = both + pltpu.roll(both, 2, 0)
            send_extra[level, 2 * piece : 2 * piece + 2, :] = both[0:2]
            if level == 0 and piece == 0:
                pl.semaphore_wait(barrier, 12)
            main_copy(level, piece).start()
        extra_copy(level).start()
        if level + 1 < LEVELS:
            level_hot(level + 1)
        else:
            export_hots()
        extra_copy(level).wait()
        for piece in range(PIECES):
            main_copy(level, piece).wait()
            at = piece * PIECE
            lanes = slice(at, at + PIECE)
            slot = iota((8, PIECE), 1) + at
            high = jnp.where(slot < counts[level, 0], jnp.broadcast_to(rows[level : level + 1, lanes] // 256, (8, PIECE)), 64)
            for n, part in enumerate(split3(recv_main[level, :, lanes])):
                part = part.astype(F32)
                for h in range(0, 32, 2):
                    placed[n, h * 8 : h * 8 + 16, lanes] = jnp.concatenate(
                        [jnp.where(high == h, part, 0.0), jnp.where(high == h + 1, part, 0.0)], axis=0
                    ).astype(BF16)
            both = recv_extra[level, 2 * piece : 2 * piece + 2, :]
            both = jnp.where(sub8 // 2 == high % 4, jnp.concatenate([both] * 4, axis=0), 0.0)
            for n, part in enumerate(split3(both)):
                part = part.astype(F32)
                for a in range(0, 8, 2):
                    placed[n, 256 + a * 8 : 272 + a * 8, lanes] = jnp.concatenate(
                        [jnp.where(high // 4 == a, part, 0.0), jnp.where(high // 4 == a + 1, part, 0.0)], axis=0
                    ).astype(BF16)
            for a in range(0, 8, 2):
                marks[a * 8 : a * 8 + 16, lanes] = jnp.concatenate(
                    [jnp.where(high == sub8 // 2 + 4 * a, 1.0, 0.0), jnp.where(high == sub8 // 2 + 4 * a + 4, 1.0, 0.0)],
                    axis=0,
                ).astype(BF16)
        hot = hots[level]
        fresh = dot_nt(placed[0], hot) + dot_nt(placed[1], hot) + dot_nt(placed[2], hot)
        hit = dot_nt(marks[...], hot)
        for h in range(32):
            lanes = slice(256 * h, 256 * h + 256)
            own[:, lanes] = jnp.where(hit[2 * h : 2 * h + 1] > 0.5, fresh[8 * h : 8 * h + 8], own[:, lanes])
        extra[...] = jnp.where(hit > 0.5, fresh[256:320], extra[...])

    spread_state(own, None, parts)

    @pl.loop(0, 8)
    def _(number):
        for piece in range(GHOSTS // PIECE):
            at = piece * PIECE
            high = jnp.broadcast_to(exports_3[number, :, at : at + PIECE] // 256, (8, PIECE))
            found = pick(parts, 256, hots_x[number, :, at : at + PIECE])
            send_ghost[:, pl.ds(pl.multiple_of(number * GHOSTS + at, PIECE), PIECE)] = by_block(found, high, 32, 0)
        ghost_copy(number).start()

    for number in range(8):
        ghost_copy(number).wait()


def exchange(mesh, send_count, particles, extra, send_rows, export_rows):
    count_x, count_y = mesh.shape["gx"], mesh.shape["gy"]
    return pl.pallas_call(
        functools.partial(exchange_kernel, count_x, count_y),
        name="exchange",
        out_shape=(
            jax.ShapeDtypeStruct((8, 8192), F32),
            jax.ShapeDtypeStruct((64, 256), F32),
            jax.ShapeDtypeStruct((8, 8192), F32),
        ),
        in_specs=[SM, VM, VM, VM, VM],
        out_specs=(VM, VM, VM),
        scratch_shapes=[
            pltpu.VMEM((LEVELS, 256, SEND), BF16),
            pltpu.VMEM((8, 256, GHOSTS), BF16),
            pltpu.VMEM((8, 1, GHOSTS), I32),
            pltpu.VMEM((3, 320, 256), BF16),
            pltpu.VMEM((3, 320, SEND), BF16),
            pltpu.VMEM((64, SEND), BF16),
            pltpu.VMEM((LEVELS, 8, SEND), F32),
            pltpu.VMEM((LEVELS, 8, PIECE), F32),
            pltpu.VMEM((LEVELS, 8, SEND), F32),
            pltpu.VMEM((LEVELS, 8, PIECE), F32),
            pltpu.VMEM((8, 8 * GHOSTS), F32),
            pltpu.SemaphoreType.DMA((LEVELS, PIECES + 1)),
            pltpu.SemaphoreType.DMA((LEVELS, PIECES + 1)),
            pltpu.SemaphoreType.DMA((8,)),
            pltpu.SemaphoreType.DMA((8,)),
        ],
        compiler_params=pltpu.CompilerParams(
            collective_id=0, has_side_effects=True, vmem_limit_bytes=48 << 20
        ),
    )(send_count, particles, extra, send_rows, export_rows)


def ghost_density_kernel(count_x, count_y, density, exports, out, exports_3, send, send_sems, recv_sems):
    barrier = pltpu.get_barrier_semaphore()
    for number in range(8):
        pl.semaphore_signal(barrier, inc=1, device_id=neighbour(number, 1, count_x, count_y), device_id_type=MESH)
    for number in range(8):
        exports_3[number] = exports[number : number + 1, :]
    table = jnp.concatenate([density[pl.ds(0, 32, stride=2), :], density[pl.ds(1, 32, stride=2), :]], axis=1)
    table = jnp.concatenate([part.astype(F32) for part in split3(table)], axis=0).astype(BF16)

    def copy(number):
        return pltpu.make_async_remote_copy(
            src_ref=send.at[number],
            dst_ref=out.at[number],
            send_sem=send_sems.at[number],
            recv_sem=recv_sems.at[number],
            device_id=neighbour(number, 1, count_x, count_y),
            device_id_type=MESH,
        )

    def gathered(number):
        index = exports_3[number]
        found = dot(table, one_hot(index))
        found = found[0:32] + found[32:64] + found[64:96]
        row = jnp.sum(jnp.where(iota((32, GHOSTS), 0) == index // 256, found, 0.0), axis=0, keepdims=True)
        for k in range(8):
            send[number, k : k + 1, :] = row[:, 128 * k : 128 * k + 128]

    gathered(0)
    pl.semaphore_wait(barrier, 8)
    copy(0).start()

    @pl.loop(1, 8)
    def _(number):
        gathered(number)
        copy(number).start()

    for number in range(8):
        copy(number).wait()


def ghost_density_step(mesh, density, export_rows):
    return pl.pallas_call(
        functools.partial(ghost_density_kernel, mesh.shape["gx"], mesh.shape["gy"]),
        name="ghost_density",
        out_shape=jax.ShapeDtypeStruct((8, 8, 128), F32),
        in_specs=[VM, VM],
        out_specs=VM,
        scratch_shapes=[
            pltpu.VMEM((8, 1, GHOSTS), I32),
            pltpu.VMEM((8, 8, 128), F32),
            pltpu.SemaphoreType.DMA((8,)),
            pltpu.SemaphoreType.DMA((8,)),
        ],
        compiler_params=pltpu.CompilerParams(collective_id=1, has_side_effects=True, vmem_limit_bytes=32 << 20),
    )(density, export_rows)


def on_device(
    mesh, particles, old_density, active, send_rows, send_count, export_rows, pair_tiles, pair_count
):
    extra = jnp.stack([old_density.reshape(32, 256), active.astype(F32).reshape(32, 256)], axis=1).reshape(64, 256)
    own, extra, ghost = exchange(mesh, send_count, particles, extra, send_rows, export_rows)
    density, codes, number, rank = density_step(pair_count, pair_tiles, own, extra, ghost)
    ghost_density = ghost_density_step(mesh, density, export_rows).reshape(64, 128)
    acceleration, heating = force_step(number, codes, own, ghost, density, ghost_density, rank)
    return density.reshape(8192), acceleration, heating.reshape(8192)


def solution(mesh):
    in_specs = (
        P(None, ("gx", "gy")),
        P(("gx", "gy")),
        P(("gx", "gy")),
        P(None, ("gx", "gy")),
        P(None, ("gx", "gy")),
        P(None, ("gx", "gy")),
        P(None, ("gx", "gy")),
        P(("gx", "gy")),
    )
    out_specs = (P(("gx", "gy")), P(None, ("gx", "gy")), P(("gx", "gy")))
    return jax.shard_map(
        functools.partial(on_device, mesh), mesh=mesh, in_specs=in_specs, out_specs=out_specs, check_vma=False
    )
```

```python
import functools
import math

import jax
import jax.numpy as jnp
from jax import lax
from jax.experimental import pallas as pl
from jax.experimental.pallas import tpu as pltpu
from jax.sharding import PartitionSpec as P

F32 = jnp.float32
BF16 = jnp.bfloat16
I32 = jnp.int32
MASS = 1.0 / 512.0
NEAR = 1e-30
FAR = 1e36
NT_DIMS = (((1,), (1,)), ((), ()))
COLS = 320
STEPS = 384
WAYS = 8
FEW = 4


def iota(shape, axis):
    return lax.broadcasted_iota(I32, shape, axis)


def split3(x):
    a = x.astype(BF16)
    r = x - a.astype(F32)
    b = r.astype(BF16)
    c = (r - b.astype(F32)).astype(BF16)
    return a, b, c


def dot(a, b):
    return jnp.dot(a, b, preferred_element_type=F32)


def dot_nt(a, b):
    return lax.dot_general(a, b, NT_DIMS, preferred_element_type=F32)


def swap_halves(x):
    return pltpu.roll(x, 64, x.ndim - 1)


def ranks_of(active):
    rows, cols = iota((128, 128), 0), iota((128, 128), 1)
    before = ((rows // 64 == cols // 64) & (rows < cols)).astype(F32).astype(BF16)
    rank = dot(active.astype(BF16), before)
    return jnp.where(active > 0.5, rank, -1.0)


def tile_groups(active):
    rows, cols = iota((128, 128), 0), iota((128, 128), 1)
    pick = (rows // 64 == cols % 2).astype(F32).astype(BF16)
    count = dot(active.astype(BF16), pick)
    own = iota((64, 128), 0) == iota((64, 128), 1) // 2
    total = jnp.sum(jnp.where(own, count, 0.0), axis=0, keepdims=True)
    return jnp.floor((total + 7.0) * 0.125)


def item_codes(pairs, used, groups):
    target, source = pairs[0:1], pairs[1:2]
    target_col = pairs.T[:, 0:1]
    count = pairs.shape[1]
    lane = iota((1, count), 1)
    used_row = lane < used
    q, p = iota((count, count), 0), iota((count, count), 1)
    same = (target_col == target) & (q < p) & (q < used)
    order = jnp.sum(jnp.where(same, 1.0, 0.0), axis=0, keepdims=True)
    at = (iota((128, count), 0).astype(F32) == target) & used_row
    at_f = jnp.where(at, 1.0, 0.0)
    number = jnp.sum(at_f, axis=1, keepdims=True)
    columns = jnp.floor((number + 1.0) * 0.5)
    below = (iota((128, 128), 0) > iota((128, 128), 1)).astype(F32).astype(BF16)
    first = dot(below, jnp.broadcast_to(columns, (128, 128)).astype(BF16))[:, 0:1]
    groups_row = dot(groups.astype(BF16), at_f.astype(BF16))
    first_row = jnp.sum(at_f * first, axis=0, keepdims=True)
    half = jnp.floor(order * 0.5)
    column = first_row + half
    second = jnp.where(order - 2.0 * half > 0.5, 1.0, 0.0)
    use = jnp.where(used_row, 1.0, 0.0)
    lead = use * (1.0 - second)
    trail = use * second
    values = jnp.concatenate(
        [target * lead, source * lead, source * trail, trail, groups_row * lead, lead * 0.0, lead * 0.0, lead * 0.0],
        axis=0,
    ).astype(BF16)
    match = jnp.where((iota((COLS, count), 0).astype(F32) == column) & used_row, 1.0, 0.0).astype(BF16)
    in_row = dot_nt(values, match)
    in_col = dot_nt(match, values)
    upper = (iota((COLS, COLS), 0) < iota((COLS, COLS), 1)).astype(F32).astype(BF16)
    lower = (iota((COLS, COLS), 0) > iota((COLS, COLS), 1)).astype(F32).astype(BF16)
    start_row = dot(in_row.astype(BF16), upper)[4:5]
    start_col = dot(lower, in_col.astype(BF16))[:, 4:5]
    size_col = in_col[:, 4:5]
    total = jnp.sum(size_col, axis=0, keepdims=True)
    high = jnp.floor(start_row * (1.0 / 256.0))
    second_source = in_row[2:3] + 256.0 * (1.0 - in_row[3:4])
    table = jnp.concatenate(
        [in_row[0:2], second_source, high, start_row - 256.0 * high, high * 0.0, high * 0.0, high * 0.0], axis=0
    )
    table = jnp.concatenate([table, jnp.zeros((8, 128 * ((COLS + 127) // 128) - COLS), F32)], axis=1)
    before = jnp.where(iota(table.shape, 1) == 0, 0.0, pltpu.roll(table, 1, 1))
    steps = (table - before)[:, 0:COLS].astype(BF16)
    at = iota((1, WAYS * STEPS), 1)
    item = (at % STEPS * WAYS + at // STEPS).astype(F32)
    found = dot(steps, jnp.where(item >= start_col, 1.0, 0.0).astype(BF16))
    beyond = item >= total
    group = item - 256.0 * found[3:4] - found[4:5]
    place = jnp.where(beyond, 0.0, group * 128.0 + found[0:1]).astype(I32)
    first_source = jnp.where(beyond, 256.0, found[1:2]).astype(I32)
    other = jnp.where(beyond, 256.0, found[2:3]).astype(I32)
    codes = place + first_source * 1024 + other * (1 << 19)
    codes = jnp.concatenate([codes[:, STEPS * w : STEPS * w + STEPS] for w in range(WAYS)], axis=0)
    most = jnp.max(groups, axis=1, keepdims=True).astype(I32)
    lane = iota(codes.shape, 1)
    return jnp.where(lane == STEPS - 1, total.astype(I32), jnp.where(lane == STEPS - 2, most, codes))


def put_sources(table, slot, chunk):
    left = iota(chunk.shape, 1) < 64
    other = swap_halves(chunk)
    table[slot] = jnp.where(left, chunk, other)
    table[slot + 1] = jnp.where(left, other, chunk)


def put_targets(columns, tile, chunk, rank, first, last):
    left = iota(chunk.shape, 1) < 64
    a, b, c = [v.astype(F32) for v in split3(chunk)]
    ar, br, cr = swap_halves(a), swap_halves(b), swap_halves(c)
    zero = jnp.zeros_like(a)
    wide = jnp.broadcast_to(rank, (8, 128))
    wide_other = swap_halves(wide)
    left8 = iota((8, 128), 1) < 64
    for half in range(2):
        if half == 0:
            right = jnp.concatenate([jnp.where(left, a, br), jnp.where(left, c, zero)], axis=1)
            own = jnp.where(left8, wide, wide_other)
        else:
            right = jnp.concatenate([jnp.where(left, ar, b), jnp.where(left, cr, zero)], axis=1)
            own = jnp.where(left8, wide_other, wide)
        sub = iota((8, 128), 0).astype(F32)
        pick = jnp.concatenate([jnp.where(own == sub + 8.0 * g, 1.0, 0.0) for g in range(first, last)], axis=0).astype(BF16)
        rows = dot_nt(jnp.concatenate([pick, pick], axis=1), right.astype(BF16))
        for g in range(first, last):
            columns[pl.ds(g * 1024 + (tile + half) * 8, 8), :] = rows[8 * (g - first) : 8 * (g - first) + 8]


def gather_sums(totals, tile, rank, first, last):
    left = iota((8, 128), 1) < 64
    wide = jnp.broadcast_to(rank, (8, 128))
    sub = iota((8, 128), 0).astype(F32)
    out = [jnp.zeros((8, 128), F32) for _ in totals]
    for g in range(first, last):
        hit = wide == sub + 8.0 * g
        for n, total in enumerate(totals):
            one = jnp.sum(total[pl.ds(g * 1024 + tile * 8, 8), :], axis=1, keepdims=True)
            two = jnp.sum(total[pl.ds(g * 1024 + tile * 8 + 8, 8), :], axis=1, keepdims=True)
            out[n] = out[n] + jnp.where(hit, jnp.where(left, one, two), 0.0)
    return [jnp.sum(o, axis=0, keepdims=True) for o in out]


def wrapped(a, b):
    s = a - b
    return s - jnp.floor(s + 0.5)


def decode(code):
    return code & 1023, (code >> 10) & 511, code >> 19


def density_item(code, columns, sources):
    place, one, two = decode(code)
    row = pl.multiple_of(place * 8, 8)
    mine = columns[pl.ds(row, 8), :]
    left = iota((8, 128), 1) < 64
    other = jnp.where(left, sources[one], sources[two])
    dx = wrapped(mine[:, 0:1], other[0:1])
    dy = wrapped(mine[:, 1:2], other[1:2])
    dz = wrapped(mine[:, 2:3], other[2:3])
    rsq = jnp.maximum(dx * dx + dy * dy + dz * dz, other[3:4])
    q = rsq * lax.rsqrt(rsq) * mine[:, 3:4]
    t = jnp.maximum(2.0 - q, 0.0)
    u = jnp.maximum(1.0 - q, 0.0)
    w = t * t * t - 4.0 * (u * u * u)
    return row, w


def force_item(code, columns, sources):
    place, one, two = decode(code)
    row = pl.multiple_of(place * 8, 8)
    mine = columns[pl.ds(row, 8), :]
    left = iota((16, 128), 1) < 64
    other = jnp.where(left, sources[one], sources[two])
    dx = wrapped(mine[:, 0:1], other[0:1])
    dy = wrapped(mine[:, 1:2], other[1:2])
    dz = wrapped(mine[:, 2:3], other[2:3])
    rsq = jnp.maximum(dx * dx + dy * dy + dz * dz, other[10:11])
    inv = lax.rsqrt(rsq)
    r = rsq * inv

    def profile(h, hinv):
        q = r * hinv
        t = jnp.maximum(2.0 - q, 0.0)
        return jnp.where(q < 1.0, 4.0 - 3.0 * q, t * t * (h * inv))

    slope = profile(mine[:, 6:7], mine[:, 8:9]) * mine[:, 9:10] + profile(other[6:7], other[8:9]) * other[9:10]
    w = (mine[:, 7:8] + other[7:8]) * slope
    gap = (
        (mine[:, 3:4] - other[3:4]) * dx
        + (mine[:, 4:5] - other[4:5]) * dy
        + (mine[:, 5:6] - other[5:6]) * dz
    )
    return row, (w * dx, w * dy, w * dz, w * gap)


def for_all_groups(most, body):
    body(0, FEW, False)

    @pl.when(most > FEW)
    def _():
        body(FEW, 8, True)


def run_items(number, codes, item):
    @pl.loop(0, (number + 2 * WAYS - 1) // (2 * WAYS))
    def _(pair):
        for late in range(2):
            for way in range(WAYS):
                item(codes[way, 2 * pair + late])


def density_kernel(count_ref, pairs_ref, own_ref, extra_ref, ghost_ref, dens_ref, code_ref, rank_ref,
                   sources, columns, total, sums, smooth, codes_s, sem):
    active = extra_ref[pl.ds(1, 64, stride=2), :]
    rank_ref[...] = ranks_of(active)
    pairs = jnp.concatenate([pairs_ref[...].astype(F32), jnp.zeros((6, 512), F32)], axis=0)
    code_ref[...] = item_codes(pairs, count_ref[0], tile_groups(active))
    copy = pltpu.make_async_copy(code_ref, codes_s, sem)
    copy.start()

    def fields(block):
        sub = iota((8, 128), 0)
        return jnp.where(sub < 3, block, jnp.where(sub == 3, NEAR, 0.0))

    def targets(block):
        sub = iota((8, 128), 0)
        return jnp.where(sub < 3, block, jnp.where(sub == 3, 1.0 / block[6:7], 0.0))

    @pl.loop(0, 16)
    def _(step):
        for part in range(4):
            chunk = step * 4 + part
            lanes = pl.ds(pl.multiple_of(step * 512, 512) + 128 * part, 128)
            block = own_ref[:, lanes]
            smooth[pl.ds(chunk, 1), :] = block[6:7]
            put_sources(sources, chunk * 2, fields(block))
            put_sources(sources, chunk * 2 + 128, fields(ghost_ref[:, lanes]))

    sources[256] = jnp.where(iota((8, 128), 0) == 3, FAR, 0.0)
    copy.wait()
    number, most = codes_s[0, STEPS - 1], codes_s[0, STEPS - 2]

    def prepare(first, last, again):
        @pl.loop(0, 16)
        def _(step):
            for part in range(4):
                chunk = step * 4 + part
                lanes = pl.ds(pl.multiple_of(step * 512, 512) + 128 * part, 128)
                put_targets(columns, chunk * 2, targets(own_ref[:, lanes]), rank_ref[pl.ds(chunk, 1), :], first, last)
                for g in range(first, last):
                    total[pl.ds(g * 1024 + chunk * 16, 16), :] = jnp.zeros((16, 128), F32)

    for_all_groups(most, prepare)

    def item(code):
        row, w = density_item(code, columns, sources)
        total[pl.ds(row, 8), :] += w

    run_items(number, codes_s, item)

    def collect(first, last, again):
        @pl.loop(0, 16)
        def _(step):
            for part in range(4):
                chunk = step * 4 + part
                (got,) = gather_sums([total], chunk * 2, rank_ref[pl.ds(chunk, 1), :], first, last)
                at = pl.ds(chunk, 1)
                sums[at, :] = sums[at, :] + got if again else got

    for_all_groups(most, collect)
    h = smooth[...]
    fresh = MASS / math.pi / (h * h * h) * (1.0 + 0.25 * sums[...])
    dens_ref[...] = jnp.where(rank_ref[...] >= 0.0, fresh, extra_ref[pl.ds(0, 64, stride=2), :])


def force_kernel(code_ref, own_ref, ghost_ref, dens_ref, gdens_ref, rank_ref, acc_ref, heat_ref,
                 sources, columns, ax, ay, az, heat):
    number, most = code_ref[0, STEPS - 1], code_ref[0, STEPS - 2]

    def fields(block, density):
        h = block[6:7]
        press = (5.0 / 3.0 - 1.0) * block[7:8] / density
        hinv = 1.0 / h
        scale = (0.375 * MASS / math.pi) / (h * h * h * h * h)
        near = jnp.full((1, 128), NEAR, F32)
        return jnp.concatenate([block[0:7], press, hinv, scale, near, jnp.zeros((5, 128), F32)], axis=0)

    def own_fields(step, part):
        lanes = pl.ds(pl.multiple_of(step * 512, 512) + 128 * part, 128)
        return fields(own_ref[:, lanes], dens_ref[pl.ds(step * 4 + part, 1), :])

    @pl.loop(0, 16)
    def _(step):
        for part in range(4):
            chunk = step * 4 + part
            lanes = pl.ds(pl.multiple_of(step * 512, 512) + 128 * part, 128)
            put_sources(sources, chunk * 2, own_fields(step, part))
            put_sources(sources, chunk * 2 + 128, fields(ghost_ref[:, lanes], gdens_ref[pl.ds(chunk, 1), :]))

    def prepare(first, last, again):
        @pl.loop(0, 16)
        def _(step):
            for part in range(4):
                chunk = step * 4 + part
                put_targets(columns, chunk * 2, own_fields(step, part), rank_ref[pl.ds(chunk, 1), :], first, last)
                for g in range(first, last):
                    for total in (ax, ay, az, heat):
                        total[pl.ds(g * 1024 + chunk * 16, 16), :] = jnp.zeros((16, 128), F32)

    for_all_groups(most, prepare)
    sub = iota((16, 128), 0)
    sources[256] = jnp.where(sub == 10, FAR, jnp.where((sub == 6) | (sub == 8), 1.0, 0.0))

    def item(code):
        row, terms = force_item(code, columns, sources)
        for total, term in zip((ax, ay, az, heat), terms):
            total[pl.ds(row, 8), :] += term

    run_items(number, code_ref, item)

    def collect(first, last, again):
        @pl.loop(0, 16)
        def _(step):
            for part in range(4):
                chunk = step * 4 + part
                got = gather_sums([ax, ay, az, heat], chunk * 2, rank_ref[pl.ds(chunk, 1), :], first, last)
                lanes = pl.ds(pl.multiple_of(step * 512, 512) + 128 * part, 128)
                at = pl.ds(chunk, 1)
                for n in range(3):
                    acc_ref[n : n + 1, lanes] = acc_ref[n : n + 1, lanes] + got[n] if again else got[n]
                heat_ref[at, :] = heat_ref[at, :] - 0.5 * got[3] if again else -0.5 * got[3]

    for_all_groups(most, collect)


VM = pl.BlockSpec(memory_space=pltpu.VMEM)
SM = pl.BlockSpec(memory_space=pltpu.SMEM)


def density_step(pair_count, pair_tiles, own, extra, ghost):
    return pl.pallas_call(
        density_kernel,
        name="density",
        out_shape=(
            jax.ShapeDtypeStruct((64, 128), F32),
            jax.ShapeDtypeStruct((WAYS, STEPS), I32),
            jax.ShapeDtypeStruct((64, 128), F32),
        ),
        in_specs=[SM, VM, VM, VM, VM],
        out_specs=(VM, VM, VM),
        scratch_shapes=[
            pltpu.VMEM((257, 8, 128), F32),
            pltpu.VMEM((8192, 8), F32),
            pltpu.VMEM((8192, 128), F32),
            pltpu.VMEM((64, 128), F32),
            pltpu.VMEM((64, 128), F32),
            pltpu.SMEM((WAYS, STEPS), I32),
            pltpu.SemaphoreType.DMA,
        ],
        compiler_params=pltpu.CompilerParams(vmem_limit_bytes=48 << 20),
    )(pair_count, pair_tiles, own, extra, ghost)


def force_step(codes, own, ghost, density, ghost_density, rank):
    return pl.pallas_call(
        force_kernel,
        name="force",
        out_shape=(jax.ShapeDtypeStruct((3, 8192), F32), jax.ShapeDtypeStruct((64, 128), F32)),
        in_specs=[SM, VM, VM, VM, VM, VM],
        out_specs=(VM, VM),
        scratch_shapes=[pltpu.VMEM((257, 16, 128), F32), pltpu.VMEM((8192, 16), F32)]
        + [pltpu.VMEM((8192, 128), F32)] * 4,
        compiler_params=pltpu.CompilerParams(vmem_limit_bytes=48 << 20),
    )(codes, own, ghost, density, ghost_density, rank)


LEVELS = 4
SEND = 2048
PIECE = 512
PIECES = SEND // PIECE
GHOSTS = 1024
MESH = pl.DeviceIdType.MESH


def flipped(index, bit):
    step = 1 << bit
    return index + step - 2 * step * ((index // step) % 2)


def neighbour(number, sign, count_x, count_y):
    cell = number + number // 4
    i = (lax.axis_index("gx") + sign * (cell // 3 - 1) + count_x) % count_x
    j = (lax.axis_index("gy") + sign * (cell % 3 - 1) + count_y) % count_y
    return i, j


def permuted(value, lanes):
    return jnp.take_along_axis(value, lanes, axis=1, mode="promise_in_bounds")


def one_hot(index_row):
    low = jnp.bitwise_and(index_row, 255)
    return jnp.where(iota((256, index_row.shape[1]), 0) == low, 1.0, 0.0).astype(BF16)


def chosen(read, bits, first, count):
    if count == 1:
        return read(first)
    half = count // 2
    low = chosen(read, bits, first, half)
    high = chosen(read, bits, first + half, half)
    return jnp.where(bits[half.bit_length() - 1], high, low)


def digits_of(value, count):
    return [jnp.bitwise_and(value, 1 << n) != 0 for n in range(count)]


def rows_at(state, index):
    index = jnp.broadcast_to(index, (8, 128))
    low = jnp.bitwise_and(index, 127)
    return chosen(lambda c: permuted(state[:, 128 * c : 128 * c + 128], low), digits_of(index >> 7, 6), 0, 64)


def pairs_at(extra, index, groups):
    index = jnp.broadcast_to(index, (8, 128))
    low = jnp.bitwise_and(index, 127)
    bits = digits_of(index >> 9, groups.bit_length() - 1)
    out = chosen(lambda g: permuted(extra[8 * g : 8 * g + 8, :], low), bits, 0, groups)
    out = jnp.where(iota((8, 128), 0) >> 1 == jnp.bitwise_and(index >> 7, 3), out, 0.0)
    out = out + pltpu.roll(out, 4, 0)
    return out + pltpu.roll(out, 2, 0)


def cells_at(table, index):
    index = jnp.broadcast_to(index, (8, 128))
    low, high = jnp.bitwise_and(index, 127), (index >> 7) - iota((8, 128), 0)
    out = jnp.zeros((8, 128), table.dtype)
    for v in range(8):
        out = jnp.where(high == 8 * v, permuted(table[8 * v : 8 * v + 8, :], low), out)
    return jnp.sum(out, axis=0, keepdims=True)


def landed(read, slot, old):
    low = jnp.bitwise_and(slot, 127)
    new = chosen(lambda c: permuted(read(c), low), digits_of(slot >> 7, 4), 0, 16)
    return jnp.where(slot >= 0, new, old)


def exchange_kernel(count_x, count_y, counts, particles, extra_in, rows, exports, own, extra, ghost,
                    hot, inverse, inverse_wide, slots, slots_x, exports_3, base_main, base_extra,
                    send_main, send_extra, recv_main, recv_extra, recv_wide,
                    send_ghost, send_sems, recv_sems, ghost_send, ghost_recv):
    i, j = lax.axis_index("gx"), lax.axis_index("gy")
    bits_x, bits_y = count_x.bit_length() - 1, count_y.bit_length() - 1
    partners = [
        (flipped(i, bits_x - 1), j),
        (flipped(i, bits_x - 2), j),
        (i, flipped(j, bits_y - 1)),
        (i, flipped(j, bits_y - 2)),
    ]
    barrier = pltpu.get_barrier_semaphore()
    for partner in partners:
        pl.semaphore_signal(barrier, inc=1, device_id=partner, device_id_type=MESH)
    for number in range(8):
        pl.semaphore_signal(barrier, inc=1, device_id=neighbour(number, 1, count_x, count_y), device_id_type=MESH)

    def invert(level):
        slot = iota((32, SEND), 1)
        index = rows[level : level + 1, :]
        high = jnp.where(slot < counts[level, 0], jnp.broadcast_to(index >> 8, (32, SEND)), 64)
        here = iota((32, SEND), 0) == high
        digits = jnp.concatenate(
            [
                jnp.where(here, ((slot >> 7) + 1).astype(F32), 0.0),
                jnp.where(here, jnp.bitwise_and(slot, 127).astype(F32), 0.0),
            ],
            axis=0,
        ).astype(BF16)
        for piece in range(PIECES):
            hot[:, piece * PIECE : piece * PIECE + PIECE] = one_hot(index[:, piece * PIECE : piece * PIECE + PIECE])
        found = dot_nt(digits, hot[...])
        found = (128.0 * (found[0:32] - 1.0) + found[32:64]).astype(I32)
        for part in range(2):
            value = found[:, 128 * part : 128 * part + 128]
            inverse[pl.ds(part, 32, stride=2), :] = value
            for field in range(2):
                inverse_wide[level, pl.ds(2 * part + field, 32, stride=4), :] = value

    def main_copy(level, piece):
        lanes = pl.ds(pl.multiple_of(piece * PIECE, PIECE), PIECE)
        return pltpu.make_async_remote_copy(
            src_ref=send_main.at[level, :, lanes],
            dst_ref=recv_main.at[level, :, lanes],
            send_sem=send_sems.at[level, piece],
            recv_sem=recv_sems.at[level, piece],
            device_id=partners[level],
            device_id_type=MESH,
        )

    def extra_copy(level):
        return pltpu.make_async_remote_copy(
            src_ref=send_extra.at[level],
            dst_ref=recv_extra.at[level],
            send_sem=send_sems.at[level, PIECES],
            recv_sem=recv_sems.at[level, PIECES],
            device_id=partners[level],
            device_id_type=MESH,
        )

    def ghost_copy(number):
        lanes = pl.ds(pl.multiple_of(number * GHOSTS, GHOSTS), GHOSTS)
        return pltpu.make_async_remote_copy(
            src_ref=send_ghost.at[:, lanes],
            dst_ref=ghost.at[:, lanes],
            send_sem=ghost_send.at[number],
            recv_sem=ghost_recv.at[number],
            device_id=neighbour(number, 1, count_x, count_y),
            device_id_type=MESH,
        )

    def gather(level, out):
        @pl.loop(0, PIECES)
        def _(piece):
            for k in range(PIECE // 128):
                at = pl.multiple_of(piece * PIECE + 128 * k, 128)
                index = rows[level : level + 1, pl.ds(at, 128)]
                out[:, pl.ds(at, 128)] = rows_at(own, index)
                base_extra[:, pl.ds(at, 128)] = pairs_at(extra, index, 16)

    def compose(level):
        @pl.loop(0, PIECES)
        def _(piece):
            for k in range(PIECE // 128):
                at = pl.multiple_of(piece * PIECE + 128 * k, 128)
                slots[:, pl.ds(at, 128)] = cells_at(inverse, rows[level : level + 1, pl.ds(at, 128)])

    def send(level):
        for piece in range(PIECES):
            for k in range(PIECE // 128):
                c = piece * (PIECE // 128) + k
                lanes = slice(128 * c, 128 * c + 128)
                both = base_extra[:, lanes]
                if level > 0:
                    slot = jnp.broadcast_to(slots[:, lanes], (8, 128))
                    send_main[level, :, lanes] = landed(
                        lambda n: recv_main[level - 1, :, 128 * n : 128 * n + 128], slot, base_main[:, lanes]
                    )
                    fresh = pairs_at(recv_extra.at[level - 1], jnp.maximum(slots[:, lanes], 0), 4)
                    both = jnp.where(slot >= 0, fresh, both)
                send_extra[level, 2 * c : 2 * c + 2, :] = both[0:2]
            main_copy(level, piece).start()
        extra_copy(level).start()

    def arrive(level):
        extra_copy(level).wait()
        for piece in range(PIECES):
            main_copy(level, piece).wait()

    def settle(level):
        for c in range(16):
            wide = jnp.concatenate([recv_extra[level, 2 * c : 2 * c + 2, :]] * 4, axis=0)
            recv_wide[:, 128 * c : 128 * c + 128] = wide

        @pl.loop(0, 16)
        def _(g):
            at = pl.multiple_of(g * 8, 8)
            slot = inverse_wide[level, pl.ds(at, 8), :]
            extra[pl.ds(at, 8), :] = landed(lambda c: recv_wide[:, 128 * c : 128 * c + 128], slot, extra[pl.ds(at, 8), :])
            for b in range(4):
                lanes = pl.ds(pl.multiple_of(g * 512, 512) + 128 * b, 128)
                slot_b = jnp.broadcast_to(slot[2 * b : 2 * b + 1], (8, 128))
                own[:, lanes] = landed(
                    lambda c: recv_main[level, :, 128 * c : 128 * c + 128], slot_b, own[:, lanes]
                )

    own[...] = particles[...]
    extra[...] = extra_in[...]
    for number in range(8):
        exports_3[number] = exports[number : number + 1, :]
    gather(0, send_main.at[0])
    pl.semaphore_wait(barrier, 12)

    for level in range(LEVELS):
        send(level)
        invert(level)
        if level > 0:
            settle(level - 1)
        if level + 1 < LEVELS:
            compose(level + 1)
            gather(level + 1, base_main)
        else:

            @pl.loop(0, 16)
            def _(block):
                number, part = block // 2, block % 2
                for k in range(4):
                    lanes = pl.multiple_of(part * 512 + 128 * k, 128)
                    index = exports_3[number, :, pl.ds(lanes, 128)]
                    slots_x[number, :, pl.ds(lanes, 128)] = cells_at(inverse, index)
                    send_ghost[:, pl.ds(pl.multiple_of(number * GHOSTS + lanes, 128), 128)] = rows_at(own, index)

        arrive(level)

    @pl.loop(0, 8)
    def _(number):
        for k in range(8):
            lanes = pl.ds(pl.multiple_of(number * GHOSTS, GHOSTS) + 128 * k, 128)
            slot = jnp.broadcast_to(slots_x[number, :, 128 * k : 128 * k + 128], (8, 128))
            send_ghost[:, lanes] = landed(
                lambda n: recv_main[LEVELS - 1, :, 128 * n : 128 * n + 128], slot, send_ghost[:, lanes]
            )
        ghost_copy(number).start()

    settle(LEVELS - 1)
    for number in range(8):
        ghost_copy(number).wait()


def exchange(mesh, send_count, particles, extra, send_rows, export_rows):
    count_x, count_y = mesh.shape["gx"], mesh.shape["gy"]
    return pl.pallas_call(
        functools.partial(exchange_kernel, count_x, count_y),
        name="exchange",
        out_shape=(
            jax.ShapeDtypeStruct((8, 8192), F32),
            jax.ShapeDtypeStruct((128, 128), F32),
            jax.ShapeDtypeStruct((8, 8192), F32),
        ),
        in_specs=[SM, VM, VM, VM, VM],
        out_specs=(VM, VM, VM),
        scratch_shapes=[
            pltpu.VMEM((256, SEND), BF16),
            pltpu.VMEM((64, 128), I32),
            pltpu.VMEM((LEVELS, 128, 128), I32),
            pltpu.VMEM((1, SEND), I32),
            pltpu.VMEM((8, 1, GHOSTS), I32),
            pltpu.VMEM((8, 1, GHOSTS), I32),
            pltpu.VMEM((8, SEND), F32),
            pltpu.VMEM((8, SEND), F32),
            pltpu.VMEM((LEVELS, 8, SEND), F32),
            pltpu.VMEM((LEVELS, 32, 128), F32),
            pltpu.VMEM((LEVELS, 8, SEND), F32),
            pltpu.VMEM((LEVELS, 32, 128), F32),
            pltpu.VMEM((8, SEND), F32),
            pltpu.VMEM((8, 8 * GHOSTS), F32),
            pltpu.SemaphoreType.DMA((LEVELS, PIECES + 1)),
            pltpu.SemaphoreType.DMA((LEVELS, PIECES + 1)),
            pltpu.SemaphoreType.DMA((8,)),
            pltpu.SemaphoreType.DMA((8,)),
        ],
        compiler_params=pltpu.CompilerParams(
            collective_id=0, has_side_effects=True, vmem_limit_bytes=48 << 20
        ),
    )(send_count, particles, extra, send_rows, export_rows)


def ghost_density_kernel(count_x, count_y, density, exports, out, exports_3, send, send_sems, recv_sems):
    barrier = pltpu.get_barrier_semaphore()
    for number in range(8):
        pl.semaphore_signal(barrier, inc=1, device_id=neighbour(number, 1, count_x, count_y), device_id_type=MESH)
    for number in range(8):
        exports_3[number] = exports[number : number + 1, :]
    def copy(number):
        return pltpu.make_async_remote_copy(
            src_ref=send.at[number],
            dst_ref=out.at[number],
            send_sem=send_sems.at[number],
            recv_sem=recv_sems.at[number],
            device_id=neighbour(number, 1, count_x, count_y),
            device_id_type=MESH,
        )

    def gathered(number):
        for k in range(8):
            send[number, k : k + 1, :] = cells_at(density, exports_3[number, :, 128 * k : 128 * k + 128])

    gathered(0)
    pl.semaphore_wait(barrier, 8)
    copy(0).start()

    @pl.loop(1, 8)
    def _(number):
        gathered(number)
        copy(number).start()

    for number in range(8):
        copy(number).wait()


def ghost_density_step(mesh, density, export_rows):
    return pl.pallas_call(
        functools.partial(ghost_density_kernel, mesh.shape["gx"], mesh.shape["gy"]),
        name="ghost_density",
        out_shape=jax.ShapeDtypeStruct((8, 8, 128), F32),
        in_specs=[VM, VM],
        out_specs=VM,
        scratch_shapes=[
            pltpu.VMEM((8, 1, GHOSTS), I32),
            pltpu.VMEM((8, 8, 128), F32),
            pltpu.SemaphoreType.DMA((8,)),
            pltpu.SemaphoreType.DMA((8,)),
        ],
        compiler_params=pltpu.CompilerParams(collective_id=1, has_side_effects=True, vmem_limit_bytes=32 << 20),
    )(density, export_rows)


def on_device(
    mesh, particles, old_density, active, send_rows, send_count, export_rows, pair_tiles, pair_count
):
    extra = jnp.stack([old_density.reshape(64, 128), active.astype(F32).reshape(64, 128)], axis=1).reshape(128, 128)
    own, extra, ghost = exchange(mesh, send_count, particles, extra, send_rows, export_rows)
    density, codes, rank = density_step(pair_count, pair_tiles, own, extra, ghost)
    ghost_density = ghost_density_step(mesh, density, export_rows).reshape(64, 128)
    acceleration, heating = force_step(codes, own, ghost, density, ghost_density, rank)
    return density.reshape(8192), acceleration, heating.reshape(8192)


def solution(mesh):
    in_specs = (
        P(None, ("gx", "gy")),
        P(("gx", "gy")),
        P(("gx", "gy")),
        P(None, ("gx", "gy")),
        P(None, ("gx", "gy")),
        P(None, ("gx", "gy")),
        P(None, ("gx", "gy")),
        P(("gx", "gy")),
    )
    out_specs = (P(("gx", "gy")), P(None, ("gx", "gy")), P(("gx", "gy")))
    return jax.shard_map(
        functools.partial(on_device, mesh), mesh=mesh, in_specs=in_specs, out_specs=out_specs, check_vma=False
    )
```

```python
import functools
import math

import jax
import jax.numpy as jnp
from jax import lax
from jax.experimental import pallas as pl
from jax.experimental.pallas import tpu as pltpu
from jax.sharding import PartitionSpec as P

F32 = jnp.float32
BF16 = jnp.bfloat16
I32 = jnp.int32
MASS = 1.0 / 512.0
NEAR = 1e-30
FAR = 1e36
NT_DIMS = (((1,), (1,)), ((), ()))
COLS = 320
STEPS = 384
WAYS = 8
FEW = 4


def iota(shape, axis):
    return lax.broadcasted_iota(I32, shape, axis)


def split3(x):
    a = x.astype(BF16)
    r = x - a.astype(F32)
    b = r.astype(BF16)
    c = (r - b.astype(F32)).astype(BF16)
    return a, b, c


def dot(a, b):
    return jnp.dot(a, b, preferred_element_type=F32)


def dot_nt(a, b):
    return lax.dot_general(a, b, NT_DIMS, preferred_element_type=F32)


def swap_halves(x):
    return pltpu.roll(x, 64, x.ndim - 1)


def ranks_of(active):
    rows, cols = iota((128, 128), 0), iota((128, 128), 1)
    before = ((rows // 64 == cols // 64) & (rows < cols)).astype(F32).astype(BF16)
    rank = dot(active.astype(BF16), before)
    return jnp.where(active > 0.5, rank, -1.0)


def tile_groups(active):
    rows, cols = iota((128, 128), 0), iota((128, 128), 1)
    pick = (rows // 64 == cols % 2).astype(F32).astype(BF16)
    count = dot(active.astype(BF16), pick)
    own = iota((64, 128), 0) == iota((64, 128), 1) // 2
    total = jnp.sum(jnp.where(own, count, 0.0), axis=0, keepdims=True)
    return jnp.floor((total + 7.0) * 0.125)


def pair_columns(pairs, used):
    target, source = pairs[0:1], pairs[1:2]
    count = pairs.shape[1]
    target_col = jnp.broadcast_to(target, (8, count)).T[:, 0:1]
    used_row = iota((1, count), 1) < used
    q, p = iota((count, count), 0), iota((count, count), 1)
    same = (target_col == target) & (q < p) & (q < used)
    order = jnp.sum(jnp.where(same, 1.0, 0.0), axis=0, keepdims=True)
    at = (iota((128, count), 0).astype(F32) == target) & used_row
    at_f = jnp.where(at, 1.0, 0.0)
    number = jnp.sum(at_f, axis=1, keepdims=True)
    columns = jnp.floor((number + 1.0) * 0.5)
    below = (iota((128, 128), 0) > iota((128, 128), 1)).astype(F32).astype(BF16)
    first = dot(below, jnp.broadcast_to(columns, (128, 128)).astype(BF16))[:, 0:1]
    first_row = jnp.sum(at_f * first, axis=0, keepdims=True)
    half = jnp.floor(order * 0.5)
    column = first_row + half
    second = jnp.where(order - 2.0 * half > 0.5, 1.0, 0.0)
    use = jnp.where(used_row, 1.0, 0.0)
    lead = use * (1.0 - second)
    trail = use * second
    zero = lead * 0.0
    values = jnp.concatenate(
        [target * lead, source * lead, source * trail, lead, trail, zero, zero, zero], axis=0
    ).astype(BF16)
    match = jnp.where((iota((COLS, count), 0).astype(F32) == column) & used_row, 1.0, 0.0).astype(BF16)
    found = dot_nt(values, match)
    alone = 256.0 * (1.0 - found[4:5])
    return jnp.where(iota(found.shape, 0) == 2, found + alone, found)


def item_codes(in_row, groups):
    tile = jnp.where(iota((128, COLS), 0).astype(F32) == in_row[0:1], 1.0, 0.0).astype(BF16)
    size = dot(jnp.broadcast_to(groups, (8, 128)).astype(BF16), tile) * in_row[3:4]
    upper = (iota((COLS, COLS), 0) < iota((COLS, COLS), 1)).astype(F32).astype(BF16)
    lower = (iota((COLS, COLS), 0) > iota((COLS, COLS), 1)).astype(F32).astype(BF16)
    start_row = dot(size.astype(BF16), upper)[0:1]
    start_col = dot_nt(lower, size.astype(BF16))[:, 0:1]
    total = jnp.sum(size[0:1], axis=1, keepdims=True)
    high = jnp.floor(start_row * (1.0 / 256.0))
    table = jnp.concatenate(
        [in_row[0:3], high, start_row - 256.0 * high, high * 0.0, high * 0.0, high * 0.0], axis=0
    )
    table = jnp.concatenate([table, jnp.zeros((8, 128 * ((COLS + 127) // 128) - COLS), F32)], axis=1)
    before = jnp.where(iota(table.shape, 1) == 0, 0.0, pltpu.roll(table, 1, 1))
    steps = (table - before)[:, 0:COLS].astype(BF16)
    at = iota((1, WAYS * STEPS), 1)
    item = (at % STEPS * WAYS + at // STEPS).astype(F32)
    found = dot(steps, jnp.where(item >= start_col, 1.0, 0.0).astype(BF16))
    beyond = item >= total
    group = item - 256.0 * found[3:4] - found[4:5]
    place = jnp.where(beyond, 0.0, group * 128.0 + found[0:1]).astype(I32)
    first_source = jnp.where(beyond, 256.0, found[1:2]).astype(I32)
    other = jnp.where(beyond, 256.0, found[2:3]).astype(I32)
    codes = place + first_source * 1024 + other * (1 << 19)
    codes = jnp.concatenate([codes[:, STEPS * w : STEPS * w + STEPS] for w in range(WAYS)], axis=0)
    most = jnp.max(groups, axis=1, keepdims=True).astype(I32)
    lane = iota(codes.shape, 1)
    return jnp.where(lane == STEPS - 1, total.astype(I32), jnp.where(lane == STEPS - 2, most, codes))


def put_sources(table, slot, chunk):
    left = iota(chunk.shape, 1) < 64
    other = swap_halves(chunk)
    table[slot] = jnp.where(left, chunk, other)
    table[slot + 1] = jnp.where(left, other, chunk)


def put_targets(columns, tile, chunk, rank, first, last):
    left = iota(chunk.shape, 1) < 64
    a, b, c = [v.astype(F32) for v in split3(chunk)]
    ar, br, cr = swap_halves(a), swap_halves(b), swap_halves(c)
    zero = jnp.zeros_like(a)
    wide = jnp.broadcast_to(rank, (8, 128))
    wide_other = swap_halves(wide)
    left8 = iota((8, 128), 1) < 64
    for half in range(2):
        if half == 0:
            right = jnp.concatenate([jnp.where(left, a, br), jnp.where(left, c, zero)], axis=1)
            own = jnp.where(left8, wide, wide_other)
        else:
            right = jnp.concatenate([jnp.where(left, ar, b), jnp.where(left, cr, zero)], axis=1)
            own = jnp.where(left8, wide_other, wide)
        sub = iota((8, 128), 0).astype(F32)
        pick = jnp.concatenate([jnp.where(own == sub + 8.0 * g, 1.0, 0.0) for g in range(first, last)], axis=0).astype(BF16)
        rows = dot_nt(jnp.concatenate([pick, pick], axis=1), right.astype(BF16))
        for g in range(first, last):
            columns[pl.ds(g * 1024 + (tile + half) * 8, 8), :] = rows[8 * (g - first) : 8 * (g - first) + 8]


def gather_sums(totals, tile, rank, first, last):
    left = iota((8, 128), 1) < 64
    wide = jnp.broadcast_to(rank, (8, 128))
    sub = iota((8, 128), 0).astype(F32)
    out = [jnp.zeros((8, 128), F32) for _ in totals]
    for g in range(first, last):
        hit = wide == sub + 8.0 * g
        for n, total in enumerate(totals):
            one = jnp.sum(total[pl.ds(g * 1024 + tile * 8, 8), :], axis=1, keepdims=True)
            two = jnp.sum(total[pl.ds(g * 1024 + tile * 8 + 8, 8), :], axis=1, keepdims=True)
            out[n] = out[n] + jnp.where(hit, jnp.where(left, one, two), 0.0)
    return [jnp.sum(o, axis=0, keepdims=True) for o in out]


def wrapped(a, b):
    s = a - b
    return s - jnp.floor(s + 0.5)


def decode(code):
    return code & 1023, (code >> 10) & 511, code >> 19


def density_item(code, columns, sources):
    place, one, two = decode(code)
    row = pl.multiple_of(place * 8, 8)
    mine = columns[pl.ds(row, 8), :]
    left = iota((8, 128), 1) < 64
    other = jnp.where(left, sources[one], sources[two])
    dx = wrapped(mine[:, 0:1], other[0:1])
    dy = wrapped(mine[:, 1:2], other[1:2])
    dz = wrapped(mine[:, 2:3], other[2:3])
    rsq = jnp.maximum(dx * dx + dy * dy + dz * dz, other[3:4])
    q = rsq * lax.rsqrt(rsq) * mine[:, 3:4]
    t = jnp.maximum(2.0 - q, 0.0)
    u = jnp.maximum(1.0 - q, 0.0)
    w = t * t * t - 4.0 * (u * u * u)
    return row, w


def force_item(code, columns, sources):
    place, one, two = decode(code)
    row = pl.multiple_of(place * 8, 8)
    mine = columns[pl.ds(row, 8), :]
    left = iota((16, 128), 1) < 64
    other = jnp.where(left, sources[one], sources[two])
    dx = wrapped(mine[:, 0:1], other[0:1])
    dy = wrapped(mine[:, 1:2], other[1:2])
    dz = wrapped(mine[:, 2:3], other[2:3])
    rsq = jnp.maximum(dx * dx + dy * dy + dz * dz, other[10:11])
    inv = lax.rsqrt(rsq)
    r = rsq * inv

    def profile(h, hinv):
        q = r * hinv
        t = jnp.maximum(2.0 - q, 0.0)
        return jnp.where(q < 1.0, 4.0 - 3.0 * q, t * t * (h * inv))

    slope = profile(mine[:, 6:7], mine[:, 8:9]) * mine[:, 9:10] + profile(other[6:7], other[8:9]) * other[9:10]
    w = (mine[:, 7:8] + other[7:8]) * slope
    gap = (
        (mine[:, 3:4] - other[3:4]) * dx
        + (mine[:, 4:5] - other[4:5]) * dy
        + (mine[:, 5:6] - other[5:6]) * dz
    )
    return row, (w * dx, w * dy, w * dz, w * gap)


def for_all_groups(most, body):
    body(0, FEW, False)

    @pl.when(most > FEW)
    def _():
        body(FEW, 8, True)


def run_items(number, codes, item):
    @pl.loop(0, (number + 2 * WAYS - 1) // (2 * WAYS))
    def _(pair):
        for late in range(2):
            for way in range(WAYS):
                item(codes[way, 2 * pair + late])


def density_kernel(cols_ref, own_ref, extra_ref, ghost_ref, result_ref, dens_ref, code_ref, rank_ref,
                   sources, columns, total, sums, smooth, codes_s, sem):
    active = extra_ref[pl.ds(1, 64, stride=2), :]
    rank_ref[...] = ranks_of(active)
    code_ref[...] = item_codes(cols_ref[...], tile_groups(active))
    copy = pltpu.make_async_copy(code_ref, codes_s, sem)
    copy.start()

    def fields(block):
        sub = iota((8, 128), 0)
        return jnp.where(sub < 3, block, jnp.where(sub == 3, NEAR, 0.0))

    def targets(block):
        sub = iota((8, 128), 0)
        return jnp.where(sub < 3, block, jnp.where(sub == 3, 1.0 / block[6:7], 0.0))

    @pl.loop(0, 16)
    def _(step):
        for part in range(4):
            chunk = step * 4 + part
            lanes = pl.ds(pl.multiple_of(step * 512, 512) + 128 * part, 128)
            block = own_ref[:, lanes]
            smooth[pl.ds(chunk, 1), :] = block[6:7]
            put_sources(sources, chunk * 2, fields(block))
            put_sources(sources, chunk * 2 + 128, fields(ghost_ref[:, lanes]))

    sources[256] = jnp.where(iota((8, 128), 0) == 3, FAR, 0.0)
    copy.wait()
    number, most = codes_s[0, STEPS - 1], codes_s[0, STEPS - 2]

    def prepare(first, last, again):
        @pl.loop(0, 16)
        def _(step):
            for part in range(4):
                chunk = step * 4 + part
                lanes = pl.ds(pl.multiple_of(step * 512, 512) + 128 * part, 128)
                put_targets(columns, chunk * 2, targets(own_ref[:, lanes]), rank_ref[pl.ds(chunk, 1), :], first, last)
                for g in range(first, last):
                    total[pl.ds(g * 1024 + chunk * 16, 16), :] = jnp.zeros((16, 128), F32)

    for_all_groups(most, prepare)

    def item(code):
        row, w = density_item(code, columns, sources)
        total[pl.ds(row, 8), :] += w

    run_items(number, codes_s, item)

    def collect(first, last, again):
        @pl.loop(0, 16)
        def _(step):
            for part in range(4):
                chunk = step * 4 + part
                (got,) = gather_sums([total], chunk * 2, rank_ref[pl.ds(chunk, 1), :], first, last)
                at = pl.ds(chunk, 1)
                sums[at, :] = sums[at, :] + got if again else got

    for_all_groups(most, collect)
    h = smooth[...]
    fresh = MASS / math.pi / (h * h * h) * (1.0 + 0.25 * sums[...])
    fresh = jnp.where(rank_ref[...] >= 0.0, fresh, extra_ref[pl.ds(0, 64, stride=2), :])
    dens_ref[...] = fresh
    result_ref[...] = fresh


def force_kernel(code_ref, own_ref, ghost_ref, dens_ref, gdens_ref, rank_ref, acc_ref, heat_ref,
                 sources, columns, ax, ay, az, heat):
    number, most = code_ref[0, STEPS - 1], code_ref[0, STEPS - 2]

    def fields(block, density):
        h = block[6:7]
        press = (5.0 / 3.0 - 1.0) * block[7:8] / density
        hinv = 1.0 / h
        scale = (0.375 * MASS / math.pi) / (h * h * h * h * h)
        near = jnp.full((1, 128), NEAR, F32)
        return jnp.concatenate([block[0:7], press, hinv, scale, near, jnp.zeros((5, 128), F32)], axis=0)

    def own_fields(step, part):
        lanes = pl.ds(pl.multiple_of(step * 512, 512) + 128 * part, 128)
        return fields(own_ref[:, lanes], dens_ref[pl.ds(step * 4 + part, 1), :])

    @pl.loop(0, 16)
    def _(step):
        for part in range(4):
            chunk = step * 4 + part
            lanes = pl.ds(pl.multiple_of(step * 512, 512) + 128 * part, 128)
            put_sources(sources, chunk * 2, own_fields(step, part))
            put_sources(sources, chunk * 2 + 128, fields(ghost_ref[:, lanes], gdens_ref[pl.ds(chunk, 1), :]))

    def prepare(first, last, again):
        @pl.loop(0, 16)
        def _(step):
            for part in range(4):
                chunk = step * 4 + part
                put_targets(columns, chunk * 2, own_fields(step, part), rank_ref[pl.ds(chunk, 1), :], first, last)
                for g in range(first, last):
                    for total in (ax, ay, az, heat):
                        total[pl.ds(g * 1024 + chunk * 16, 16), :] = jnp.zeros((16, 128), F32)

    for_all_groups(most, prepare)
    sub = iota((16, 128), 0)
    sources[256] = jnp.where(sub == 10, FAR, jnp.where((sub == 6) | (sub == 8), 1.0, 0.0))

    def item(code):
        row, terms = force_item(code, columns, sources)
        for total, term in zip((ax, ay, az, heat), terms):
            total[pl.ds(row, 8), :] += term

    run_items(number, code_ref, item)

    def collect(first, last, again):
        @pl.loop(0, 16)
        def _(step):
            for part in range(4):
                chunk = step * 4 + part
                got = gather_sums([ax, ay, az, heat], chunk * 2, rank_ref[pl.ds(chunk, 1), :], first, last)
                lanes = pl.ds(pl.multiple_of(step * 512, 512) + 128 * part, 128)
                at = pl.ds(chunk, 1)
                for n in range(3):
                    acc_ref[n : n + 1, lanes] = acc_ref[n : n + 1, lanes] + got[n] if again else got[n]
                heat_ref[at, :] = heat_ref[at, :] - 0.5 * got[3] if again else -0.5 * got[3]

    for_all_groups(most, collect)


VM = pl.BlockSpec(memory_space=pltpu.VMEM)
SM = pl.BlockSpec(memory_space=pltpu.SMEM)


def density_step(columns, own, extra, ghost):
    return pl.pallas_call(
        density_kernel,
        name="density",
        out_shape=(
            jax.ShapeDtypeStruct((64, 128), F32),
            jax.ShapeDtypeStruct((64, 128), F32),
            jax.ShapeDtypeStruct((WAYS, STEPS), I32),
            jax.ShapeDtypeStruct((64, 128), F32),
        ),
        in_specs=[VM, VM, VM, VM],
        out_specs=(VM, VM, VM, VM),
        scratch_shapes=[
            pltpu.VMEM((257, 8, 128), F32),
            pltpu.VMEM((8192, 8), F32),
            pltpu.VMEM((8192, 128), F32),
            pltpu.VMEM((64, 128), F32),
            pltpu.VMEM((64, 128), F32),
            pltpu.SMEM((WAYS, STEPS), I32),
            pltpu.SemaphoreType.DMA,
        ],
        compiler_params=pltpu.CompilerParams(vmem_limit_bytes=24 << 20),
    )(columns, own, extra, ghost)


def force_step(codes, own, ghost, density, ghost_density, rank):
    return pl.pallas_call(
        force_kernel,
        name="force",
        out_shape=(jax.ShapeDtypeStruct((3, 8192), F32), jax.ShapeDtypeStruct((64, 128), F32)),
        in_specs=[SM, VM, VM, VM, VM, VM],
        out_specs=(VM, VM),
        scratch_shapes=[pltpu.VMEM((257, 16, 128), F32), pltpu.VMEM((8192, 16), F32)]
        + [pltpu.VMEM((8192, 128), F32)] * 4,
        compiler_params=pltpu.CompilerParams(vmem_limit_bytes=40 << 20),
    )(codes, own, ghost, density, ghost_density, rank)


LEVELS = 4
SEND = 2048
PIECE = 512
BLOCK = 1024
DENSE = 512
DENSE_X = 512
PIECES = SEND // PIECE
GHOSTS = 1024
MESH = pl.DeviceIdType.MESH


def flipped(index, bit):
    step = 1 << bit
    return index + step - 2 * step * ((index // step) % 2)


def neighbour(number, sign, count_x, count_y):
    cell = number + number // 4
    i = (lax.axis_index("gx") + sign * (cell // 3 - 1) + count_x) % count_x
    j = (lax.axis_index("gy") + sign * (cell % 3 - 1) + count_y) % count_y
    return i, j


def spread_state(own, parts):
    for h in range(0, 32, 2):
        pair = jnp.concatenate([own[:, h * 256 : h * 256 + 256], own[:, h * 256 + 256 : h * 256 + 512]], axis=0)
        for n, part in enumerate(split3(pair)):
            parts[n, h * 8 : h * 8 + 16, :] = part


def permuted(value, lanes):
    return jnp.take_along_axis(value, lanes, axis=1, mode="promise_in_bounds")


def one_hot(index_row):
    low = jnp.bitwise_and(index_row, 255)
    return jnp.where(iota((256, index_row.shape[1]), 0) == low, 1.0, 0.0).astype(BF16)


def chosen(read, bits, first, count):
    if count == 1:
        return read(first)
    half = count // 2
    low = chosen(read, bits, first, half)
    high = chosen(read, bits, first + half, half)
    return jnp.where(bits[half.bit_length() - 1], high, low)


def digits_of(value, count):
    return [jnp.bitwise_and(value, 1 << n) != 0 for n in range(count)]


def rows_at(state, index):
    index = jnp.broadcast_to(index, (8, 128))
    low = jnp.bitwise_and(index, 127)
    return chosen(lambda c: permuted(state[:, 128 * c : 128 * c + 128], low), digits_of(index >> 7, 6), 0, 64)


def rows_by_matmul(parts, index):
    hot = one_hot(index)
    found = dot(parts[2], hot) + dot(parts[1], hot) + dot(parts[0], hot)
    bits = digits_of(jnp.broadcast_to(index, (8, 256)) >> 8, 5)
    return chosen(lambda h: found[8 * h : 8 * h + 8], bits, 0, 32)


def pairs_at(extra, index, groups):
    index = jnp.broadcast_to(index, (8, 128))
    low = jnp.bitwise_and(index, 127)
    bits = digits_of(index >> 9, groups.bit_length() - 1)
    out = chosen(lambda g: permuted(extra[8 * g : 8 * g + 8, :], low), bits, 0, groups)
    out = jnp.where(iota((8, 128), 0) >> 1 == jnp.bitwise_and(index >> 7, 3), out, 0.0)
    out = out + pltpu.roll(out, 4, 0)
    return out + pltpu.roll(out, 2, 0)


def cells_at(table, index):
    index = jnp.broadcast_to(index, (8, 128))
    low, high = jnp.bitwise_and(index, 127), (index >> 7) - iota((8, 128), 0)
    out = jnp.zeros((8, 128), table.dtype)
    for v in range(8):
        out = jnp.where(high == 8 * v, permuted(table[8 * v : 8 * v + 8, :], low), out)
    return jnp.sum(out, axis=0, keepdims=True)


def landed(read, slot, old):
    low = jnp.bitwise_and(slot, 127)
    new = chosen(lambda c: permuted(read(c), low), digits_of(slot >> 7, 4), 0, 16)
    return jnp.where(slot >= 0, new, old)


def exchange_kernel(count_x, count_y, counts, used, particles_h, old_h, active_h, rows_h, exports_h, pairs_h,
                    own, extra, ghost, columns, exports_3,
                    loads, old, active, rows, exports, pairs, parts, hot, inverse, inverse_wide, slots, slots_x, base_main, base_extra,
                    send_main, send_extra, recv_main, recv_extra, recv_wide,
                    send_ghost, send_sems, recv_sems, ghost_send, ghost_recv):
    i, j = lax.axis_index("gx"), lax.axis_index("gy")
    bits_x, bits_y = count_x.bit_length() - 1, count_y.bit_length() - 1
    partners = [
        (flipped(i, bits_x - 1), j),
        (flipped(i, bits_x - 2), j),
        (i, flipped(j, bits_y - 1)),
        (i, flipped(j, bits_y - 2)),
    ]
    copies = [
        pltpu.make_async_copy(source, target, loads.at[n])
        for n, (source, target) in enumerate(
            ((rows_h, rows), (particles_h, own), (old_h, old), (active_h, active), (exports_h, exports), (pairs_h, pairs))
        )
    ]
    for copy in copies:
        copy.start()
    barrier = pltpu.get_barrier_semaphore()
    for partner in partners:
        pl.semaphore_signal(barrier, inc=1, device_id=partner, device_id_type=MESH)
    for number in range(8):
        pl.semaphore_signal(barrier, inc=1, device_id=neighbour(number, 1, count_x, count_y), device_id_type=MESH)

    def invert(level):
        slot = iota((32, SEND), 1)
        index = rows[level : level + 1, :]
        high = jnp.where(slot < counts[0, level], jnp.broadcast_to(index >> 8, (32, SEND)), 64)
        here = iota((32, SEND), 0) == high
        digits = jnp.concatenate(
            [
                jnp.where(here, ((slot >> 7) + 1).astype(F32), 0.0),
                jnp.where(here, jnp.bitwise_and(slot, 127).astype(F32), 0.0),
            ],
            axis=0,
        ).astype(BF16)
        for piece in range(PIECES):
            hot[:, piece * PIECE : piece * PIECE + PIECE] = one_hot(index[:, piece * PIECE : piece * PIECE + PIECE])
        found = dot_nt(digits, hot[...])
        found = (128.0 * (found[0:32] - 1.0) + found[32:64]).astype(I32)
        for part in range(2):
            value = found[:, 128 * part : 128 * part + 128]
            inverse[pl.ds(part, 32, stride=2), :] = value
            for field in range(2):
                inverse_wide[level, pl.ds(2 * part + field, 32, stride=4), :] = value

    def main_copy(level, piece):
        lanes = pl.ds(pl.multiple_of(piece * PIECE, PIECE), PIECE)
        return pltpu.make_async_remote_copy(
            src_ref=send_main.at[level, :, lanes],
            dst_ref=recv_main.at[level, :, lanes],
            send_sem=send_sems.at[level, piece],
            recv_sem=recv_sems.at[level, piece],
            device_id=partners[level],
            device_id_type=MESH,
        )

    def extra_copy(level):
        return pltpu.make_async_remote_copy(
            src_ref=send_extra.at[level],
            dst_ref=recv_extra.at[level],
            send_sem=send_sems.at[level, PIECES],
            recv_sem=recv_sems.at[level, PIECES],
            device_id=partners[level],
            device_id_type=MESH,
        )

    def ghost_copy(number):
        lanes = pl.ds(pl.multiple_of(number * GHOSTS, GHOSTS), GHOSTS)
        return pltpu.make_async_remote_copy(
            src_ref=send_ghost.at[:, lanes],
            dst_ref=ghost.at[:, lanes],
            send_sem=ghost_send.at[number],
            recv_sem=ghost_recv.at[number],
            device_id=neighbour(number, 1, count_x, count_y),
            device_id_type=MESH,
        )

    def gather(level, out):
        spread_state(own, parts)

        @pl.loop(0, SEND // BLOCK)
        def _(block):
            at = pl.multiple_of(block * BLOCK, BLOCK)
            for k in range(0, DENSE, 256):
                out[:, pl.ds(at + k, 256)] = rows_by_matmul(parts, rows[level : level + 1, pl.ds(at + k, 256)])
            for k in range(0, BLOCK, 128):
                index = rows[level : level + 1, pl.ds(at + k, 128)]
                base_extra[:, pl.ds(at + k, 128)] = pairs_at(extra, index, 16)
                if k >= DENSE:
                    out[:, pl.ds(at + k, 128)] = rows_at(own, index)

    def compose(level):
        @pl.loop(0, PIECES)
        def _(piece):
            for k in range(PIECE // 128):
                at = pl.multiple_of(piece * PIECE + 128 * k, 128)
                slots[:, pl.ds(at, 128)] = cells_at(inverse, rows[level : level + 1, pl.ds(at, 128)])

    def send(level):
        for piece in range(PIECES):
            for k in range(PIECE // 128):
                c = piece * (PIECE // 128) + k
                lanes = slice(128 * c, 128 * c + 128)
                both = base_extra[:, lanes]
                if level > 0:
                    slot = jnp.broadcast_to(slots[:, lanes], (8, 128))
                    send_main[level, :, lanes] = landed(
                        lambda n: recv_main[level - 1, :, 128 * n : 128 * n + 128], slot, base_main[:, lanes]
                    )
                    fresh = pairs_at(recv_extra.at[level - 1], jnp.maximum(slots[:, lanes], 0), 4)
                    both = jnp.where(slot >= 0, fresh, both)
                send_extra[level, 2 * c : 2 * c + 2, :] = both[0:2]
            main_copy(level, piece).start()
        extra_copy(level).start()

    def arrive(level):
        extra_copy(level).wait()
        for piece in range(PIECES):
            main_copy(level, piece).wait()

    def settle(level):
        for c in range(16):
            wide = jnp.concatenate([recv_extra[level, 2 * c : 2 * c + 2, :]] * 4, axis=0)
            recv_wide[:, 128 * c : 128 * c + 128] = wide

        @pl.loop(0, 8)
        def _(step):
            for late in range(2):
                g = step * 2 + late
                at = pl.multiple_of(g * 8, 8)
                slot = inverse_wide[level, pl.ds(at, 8), :]
                extra[pl.ds(at, 8), :] = landed(
                    lambda c: recv_wide[:, 128 * c : 128 * c + 128], slot, extra[pl.ds(at, 8), :]
                )
                for b in range(4):
                    lanes = pl.ds(pl.multiple_of(g * 512, 512) + 128 * b, 128)
                    slot_b = jnp.broadcast_to(slot[2 * b : 2 * b + 1], (8, 128))
                    own[:, lanes] = landed(
                        lambda c: recv_main[level, :, 128 * c : 128 * c + 128], slot_b, own[:, lanes]
                    )

    for copy in copies:
        copy.wait()
    extra[pl.ds(0, 64, stride=2), :] = old[...]
    extra[pl.ds(1, 64, stride=2), :] = active[...].astype(F32)
    for number in range(8):
        exports_3[number] = exports[number : number + 1, :]
    gather(0, send_main.at[0])
    pl.semaphore_wait(barrier, 12)

    for level in range(LEVELS):
        send(level)
        if level == 0:
            columns[...] = pair_columns(pairs[...].astype(F32), used[0])
        invert(level)
        if level > 0:
            settle(level - 1)
        if level + 1 < LEVELS:
            compose(level + 1)
            gather(level + 1, base_main)
        else:

            spread_state(own, parts)

            @pl.loop(0, 8)
            def _(number):
                at = pl.multiple_of(number * GHOSTS, GHOSTS)
                for k in range(0, DENSE_X, 256):
                    send_ghost[:, pl.ds(at + k, 256)] = rows_by_matmul(parts, exports_3[number, :, k : k + 256])
                for k in range(0, GHOSTS, 128):
                    index = exports_3[number, :, k : k + 128]
                    slots_x[number, :, k : k + 128] = cells_at(inverse, index)
                    if k >= DENSE_X:
                        send_ghost[:, pl.ds(at + k, 128)] = rows_at(own, index)

        arrive(level)

    @pl.loop(0, 8)
    def _(number):
        for k in range(8):
            lanes = pl.ds(pl.multiple_of(number * GHOSTS, GHOSTS) + 128 * k, 128)
            slot = jnp.broadcast_to(slots_x[number, :, 128 * k : 128 * k + 128], (8, 128))
            send_ghost[:, lanes] = landed(
                lambda n: recv_main[LEVELS - 1, :, 128 * n : 128 * n + 128], slot, send_ghost[:, lanes]
            )
        ghost_copy(number).start()

    settle(LEVELS - 1)
    for number in range(8):
        ghost_copy(number).wait()


HB = pl.BlockSpec(memory_space=pltpu.HBM)


def exchange(mesh, send_count, pair_count, particles, old, active, send_rows, export_rows, pair_tiles):
    count_x, count_y = mesh.shape["gx"], mesh.shape["gy"]
    return pl.pallas_call(
        functools.partial(exchange_kernel, count_x, count_y),
        name="exchange",
        out_shape=(
            jax.ShapeDtypeStruct((8, 8192), F32),
            jax.ShapeDtypeStruct((128, 128), F32),
            jax.ShapeDtypeStruct((8, 8192), F32),
            jax.ShapeDtypeStruct((8, COLS), F32),
            jax.ShapeDtypeStruct((8, 1, GHOSTS), I32),
        ),
        in_specs=[SM, SM, HB, HB, HB, HB, HB, HB],
        out_specs=(VM, VM, VM, VM, VM),
        scratch_shapes=[
            pltpu.SemaphoreType.DMA((6,)),
            pltpu.VMEM((64, 128), F32),
            pltpu.VMEM((64, 128), I32),
            pltpu.VMEM((LEVELS, SEND), I32),
            pltpu.VMEM((8, GHOSTS), I32),
            pltpu.VMEM((2, 512), I32),
            pltpu.VMEM((3, 256, 256), BF16),
            pltpu.VMEM((256, SEND), BF16),
            pltpu.VMEM((64, 128), I32),
            pltpu.VMEM((LEVELS, 128, 128), I32),
            pltpu.VMEM((1, SEND), I32),
            pltpu.VMEM((8, 1, GHOSTS), I32),
            pltpu.VMEM((8, SEND), F32),
            pltpu.VMEM((8, SEND), F32),
            pltpu.VMEM((LEVELS, 8, SEND), F32),
            pltpu.VMEM((LEVELS, 32, 128), F32),
            pltpu.VMEM((LEVELS, 8, SEND), F32),
            pltpu.VMEM((LEVELS, 32, 128), F32),
            pltpu.VMEM((8, SEND), F32),
            pltpu.VMEM((8, 8 * GHOSTS), F32),
            pltpu.SemaphoreType.DMA((LEVELS, PIECES + 1)),
            pltpu.SemaphoreType.DMA((LEVELS, PIECES + 1)),
            pltpu.SemaphoreType.DMA((8,)),
            pltpu.SemaphoreType.DMA((8,)),
        ],
        compiler_params=pltpu.CompilerParams(
            collective_id=0, has_side_effects=True, vmem_limit_bytes=24 << 20
        ),
    )(send_count, pair_count, particles, old, active, send_rows, export_rows, pair_tiles)


def ghost_density_kernel(count_x, count_y, density, exports_3, out, send, send_sems, recv_sems):
    barrier = pltpu.get_barrier_semaphore()
    for number in range(8):
        pl.semaphore_signal(barrier, inc=1, device_id=neighbour(number, 1, count_x, count_y), device_id_type=MESH)

    def copy(number):
        return pltpu.make_async_remote_copy(
            src_ref=send.at[number],
            dst_ref=out.at[number],
            send_sem=send_sems.at[number],
            recv_sem=recv_sems.at[number],
            device_id=neighbour(number, 1, count_x, count_y),
            device_id_type=MESH,
        )

    def gathered(number):
        for k in range(8):
            send[number, k : k + 1, :] = cells_at(density, exports_3[number, :, 128 * k : 128 * k + 128])

    gathered(0)
    pl.semaphore_wait(barrier, 8)
    copy(0).start()

    @pl.loop(1, 8)
    def _(number):
        gathered(number)
        copy(number).start()

    for number in range(8):
        copy(number).wait()


def ghost_density_step(mesh, density, export_rows):
    return pl.pallas_call(
        functools.partial(ghost_density_kernel, mesh.shape["gx"], mesh.shape["gy"]),
        name="ghost_density",
        out_shape=jax.ShapeDtypeStruct((8, 8, 128), F32),
        in_specs=[VM, VM],
        out_specs=VM,
        scratch_shapes=[
            pltpu.VMEM((8, 8, 128), F32),
            pltpu.SemaphoreType.DMA((8,)),
            pltpu.SemaphoreType.DMA((8,)),
        ],
        compiler_params=pltpu.CompilerParams(collective_id=1, has_side_effects=True, vmem_limit_bytes=8 << 20),
    )(density, export_rows)


def on_device(
    mesh, particles, old_density, active, send_rows, send_count, export_rows, pair_tiles, pair_count
):
    own, extra, ghost, columns, exports = exchange(
        mesh,
        send_count.T,
        pair_count,
        particles,
        old_density.reshape(64, 128),
        active.reshape(64, 128),
        send_rows,
        export_rows,
        pair_tiles,
    )
    result, density, codes, rank = density_step(columns, own, extra, ghost)
    ghost_density = ghost_density_step(mesh, density, exports).reshape(64, 128)
    acceleration, heating = force_step(codes, own, ghost, density, ghost_density, rank)
    return result.reshape(8192), acceleration, heating.reshape(8192)


def solution(mesh):
    in_specs = (
        P(None, ("gx", "gy")),
        P(("gx", "gy")),
        P(("gx", "gy")),
        P(None, ("gx", "gy")),
        P(None, ("gx", "gy")),
        P(None, ("gx", "gy")),
        P(None, ("gx", "gy")),
        P(("gx", "gy")),
    )
    out_specs = (P(("gx", "gy")), P(None, ("gx", "gy")), P(("gx", "gy")))
    return jax.shard_map(
        functools.partial(on_device, mesh), mesh=mesh, in_specs=in_specs, out_specs=out_specs, check_vma=False
    )
```

```python
import functools
import math

import jax
import jax.numpy as jnp
from jax import lax
from jax.experimental import pallas as pl
from jax.experimental.pallas import tpu as pltpu
from jax.sharding import PartitionSpec as P

F32 = jnp.float32
BF16 = jnp.bfloat16
I32 = jnp.int32
MASS = 1.0 / 512.0
NEAR = 1e-30
FAR = 1e36
NT_DIMS = (((1,), (1,)), ((), ()))
COLS = 320
STEPS = 384
WAYS = 8
SPAN = 8
FEW = 4


def iota(shape, axis):
    return lax.broadcasted_iota(I32, shape, axis)


def split3(x):
    a = x.astype(BF16)
    r = x - a.astype(F32)
    b = r.astype(BF16)
    c = (r - b.astype(F32)).astype(BF16)
    return a, b, c


def dot(a, b):
    return jnp.dot(a, b, preferred_element_type=F32)


def dot_nt(a, b):
    return lax.dot_general(a, b, NT_DIMS, preferred_element_type=F32)


def swap_halves(x):
    return pltpu.roll(x, 64, x.ndim - 1)


def ranks_of(active):
    rows, cols = iota((128, 128), 0), iota((128, 128), 1)
    before = ((rows // 64 == cols // 64) & (rows < cols)).astype(F32).astype(BF16)
    rank = dot(active.astype(BF16), before)
    return jnp.where(active > 0.5, rank, -1.0)


def tile_groups(active):
    rows, cols = iota((128, 128), 0), iota((128, 128), 1)
    pick = (rows // 64 == cols % 2).astype(F32).astype(BF16)
    count = dot(active.astype(BF16), pick)
    own = iota((64, 128), 0) == iota((64, 128), 1) // 2
    total = jnp.sum(jnp.where(own, count, 0.0), axis=0, keepdims=True)
    return jnp.floor((total + 7.0) * 0.125)


def pair_columns(pairs, used):
    target, source = pairs[0:1], pairs[1:2]
    count = pairs.shape[1]
    target_col = jnp.broadcast_to(target, (8, count)).T[:, 0:1]
    used_row = iota((1, count), 1) < used
    q, p = iota((count, count), 0), iota((count, count), 1)
    same = (target_col == target) & (q < p) & (q < used)
    order = jnp.sum(jnp.where(same, 1.0, 0.0), axis=0, keepdims=True)
    at = (iota((128, count), 0).astype(F32) == target) & used_row
    at_f = jnp.where(at, 1.0, 0.0)
    number = jnp.sum(at_f, axis=1, keepdims=True)
    columns = jnp.floor((number + 1.0) * 0.5)
    below = (iota((128, 128), 0) > iota((128, 128), 1)).astype(F32).astype(BF16)
    first = dot(below, jnp.broadcast_to(columns, (128, 128)).astype(BF16))[:, 0:1]
    first_row = jnp.sum(at_f * first, axis=0, keepdims=True)
    half = jnp.floor(order * 0.5)
    column = first_row + half
    second = jnp.where(order - 2.0 * half > 0.5, 1.0, 0.0)
    use = jnp.where(used_row, 1.0, 0.0)
    lead = use * (1.0 - second)
    trail = use * second
    zero = lead * 0.0
    values = jnp.concatenate(
        [target * lead, source * lead, source * trail, lead, trail, zero, zero, zero], axis=0
    ).astype(BF16)
    match = jnp.where((iota((COLS, count), 0).astype(F32) == column) & used_row, 1.0, 0.0).astype(BF16)
    found = dot_nt(values, match)
    alone = 256.0 * (1.0 - found[4:5])
    return jnp.where(iota(found.shape, 0) == 2, found + alone, found)


def item_codes(in_row, groups):
    tile = jnp.where(iota((128, COLS), 0).astype(F32) == in_row[0:1], 1.0, 0.0).astype(BF16)
    size = dot(jnp.broadcast_to(groups, (8, 128)).astype(BF16), tile) * in_row[3:4]
    upper = (iota((COLS, COLS), 0) < iota((COLS, COLS), 1)).astype(F32).astype(BF16)
    lower = (iota((COLS, COLS), 0) > iota((COLS, COLS), 1)).astype(F32).astype(BF16)
    start_row = dot(size.astype(BF16), upper)[0:1]
    start_col = dot_nt(lower, size.astype(BF16))[:, 0:1]
    total = jnp.sum(size[0:1], axis=1, keepdims=True)
    high = jnp.floor(start_row * (1.0 / 256.0))
    table = jnp.concatenate(
        [in_row[0:3], high, start_row - 256.0 * high, high * 0.0, high * 0.0, high * 0.0], axis=0
    )
    table = jnp.concatenate([table, jnp.zeros((8, 128 * ((COLS + 127) // 128) - COLS), F32)], axis=1)
    before = jnp.where(iota(table.shape, 1) == 0, 0.0, pltpu.roll(table, 1, 1))
    steps = (table - before)[:, 0:COLS].astype(BF16)
    at = iota((1, WAYS * STEPS), 1)
    item = (at % STEPS * WAYS + at // STEPS).astype(F32)
    found = dot(steps, jnp.where(item >= start_col, 1.0, 0.0).astype(BF16))
    beyond = item >= total
    group = item - 256.0 * found[3:4] - found[4:5]
    place = jnp.where(beyond, 0.0, group * 128.0 + found[0:1]).astype(I32)
    first_source = jnp.where(beyond, 256.0, found[1:2]).astype(I32)
    other = jnp.where(beyond, 256.0, found[2:3]).astype(I32)
    codes = place + first_source * 1024 + other * (1 << 19)
    codes = jnp.concatenate([codes[:, STEPS * w : STEPS * w + STEPS] for w in range(WAYS)], axis=0)
    most = jnp.max(groups, axis=1, keepdims=True).astype(I32)
    lane = iota(codes.shape, 1)
    return jnp.where(lane == STEPS - 1, total.astype(I32), jnp.where(lane == STEPS - 2, most, codes))


def put_sources(table, slot, chunk):
    left = iota(chunk.shape, 1) < 64
    other = swap_halves(chunk)
    table[slot] = jnp.where(left, chunk, other)
    table[slot + 1] = jnp.where(left, other, chunk)


def put_targets(columns, chunk, fields, rank, first, last):
    parts = jnp.concatenate([part.astype(F32) for part in split3(fields)], axis=0)
    parts = jnp.concatenate([parts, jnp.zeros((128 - parts.shape[0], 128), F32)], axis=0).astype(BF16)
    wide = jnp.broadcast_to(rank, (8, 128))
    left = iota((8, 128), 1) < 64
    sub = iota((8, 128), 0).astype(F32)
    ours = jnp.where(left, wide, -1.0), jnp.where(left, -1.0, wide)
    pick = jnp.concatenate(
        [jnp.where(our == sub + 8.0 * g, 1.0, 0.0) for g in range(first, last) for our in ours], axis=0
    ).astype(BF16)
    rows = dot_nt(pick, parts)
    for g in range(first, last):
        columns[pl.ds(g * 1024 + chunk * 16, 16), :] = rows[16 * (g - first) : 16 * (g - first) + 16]


def widener(fields, stride):
    k, n = iota((128, 128 * fields), 0), iota((128, 128 * fields), 1)
    return ((k % stride == n // 128) & (k < 3 * stride)).astype(F32).astype(BF16)


def gather_sums(totals, tile, rank, first, last):
    left = iota((8, 128), 1) < 64
    wide = jnp.broadcast_to(rank, (8, 128))
    sub = iota((8, 128), 0).astype(F32)
    out = [jnp.zeros((8, 128), F32) for _ in totals]
    for g in range(first, last):
        hit = wide == sub + 8.0 * g
        for n, total in enumerate(totals):
            one = jnp.sum(total[pl.ds(g * 1024 + tile * 8, 8), :], axis=1, keepdims=True)
            two = jnp.sum(total[pl.ds(g * 1024 + tile * 8 + 8, 8), :], axis=1, keepdims=True)
            out[n] = out[n] + jnp.where(hit, jnp.where(left, one, two), 0.0)
    return [jnp.sum(o, axis=0, keepdims=True) for o in out]


def wrapped(a, b):
    s = a - b
    return s - jnp.floor(s + 0.5)


def decode(code):
    return code & 1023, (code >> 10) & 511, code >> 19


def density_item(mine, other):
    dx = wrapped(mine[0], other[0:1])
    dy = wrapped(mine[1], other[1:2])
    dz = wrapped(mine[2], other[2:3])
    rsq = jnp.maximum(dx * dx + dy * dy + dz * dz, other[3:4])
    q = rsq * lax.rsqrt(rsq) * mine[3]
    t = jnp.maximum(2.0 - q, 0.0)
    u = jnp.maximum(1.0 - q, 0.0)
    return (t * t * t - 4.0 * (u * u * u),)


def force_item(mine, other):
    dx = wrapped(mine[0], other[0:1])
    dy = wrapped(mine[1], other[1:2])
    dz = wrapped(mine[2], other[2:3])
    rsq = jnp.maximum(dx * dx + dy * dy + dz * dz, other[10:11])
    inv = lax.rsqrt(rsq)
    r = rsq * inv

    def profile(h, hinv):
        q = r * hinv
        t = jnp.maximum(2.0 - q, 0.0)
        return jnp.where(q < 1.0, 4.0 - 3.0 * q, t * t * (h * inv))

    slope = profile(mine[6], mine[8]) * mine[9] + profile(other[6:7], other[8:9]) * other[9:10]
    w = (mine[7] + other[7:8]) * slope
    gap = (mine[3] - other[3:4]) * dx + (mine[4] - other[4:5]) * dy + (mine[5] - other[5:6]) * dz
    return (w * dx, w * dy, w * dz, w * gap)


def for_all_groups(most, body):
    body(0, FEW, False)

    @pl.when(most > FEW)
    def _():
        body(FEW, 8, True)


def run_items(number, codes, columns, sources, spread, fields, item, totals):
    @pl.loop(0, (number + SPAN * WAYS - 1) // (SPAN * WAYS))
    def _(span):
        for late in range(0, SPAN, 2):
            places = [decode(codes[way, SPAN * span + late + n]) for n in range(2) for way in range(WAYS)]
            rows = [pl.multiple_of(place * 8, 8) for place, _, _ in places]
            mine = jnp.concatenate([columns[pl.ds(row, 8), :] for row in rows], axis=0).astype(BF16)
            wide = dot(mine, spread[...])
            for n, (_, one, two) in enumerate(places):
                first, second = sources[one], sources[two]
                other = jnp.where(iota(first.shape, 1) < 64, first, second)
                own = [wide[8 * n : 8 * n + 8, 128 * f : 128 * f + 128] for f in range(fields)]
                for total, term in zip(totals, item(own, other)):
                    total[pl.ds(rows[n], 8), :] += term


def density_kernel(cols_ref, own_ref, extra_ref, ghost_ref, result_ref, dens_ref, code_ref, rank_ref,
                   sources, columns, spread, total, sums, smooth, codes_s, sem):
    active = extra_ref[pl.ds(1, 64, stride=2), :]
    spread[...] = widener(4, 8)
    rank_ref[...] = ranks_of(active)
    code_ref[...] = item_codes(cols_ref[...], tile_groups(active))
    copy = pltpu.make_async_copy(code_ref, codes_s, sem)
    copy.start()

    def fields(block):
        sub = iota((8, 128), 0)
        return jnp.where(sub < 3, block, jnp.where(sub == 3, NEAR, 0.0))

    def targets(block):
        sub = iota((8, 128), 0)
        return jnp.where(sub < 3, block, jnp.where(sub == 3, 1.0 / block[6:7], 0.0))

    @pl.loop(0, 16)
    def _(step):
        for part in range(4):
            chunk = step * 4 + part
            lanes = pl.ds(pl.multiple_of(step * 512, 512) + 128 * part, 128)
            block = own_ref[:, lanes]
            smooth[pl.ds(chunk, 1), :] = block[6:7]
            put_sources(sources, chunk * 2, fields(block))
            put_sources(sources, chunk * 2 + 128, fields(ghost_ref[:, lanes]))

    sources[256] = jnp.where(iota((8, 128), 0) == 3, FAR, 0.0)
    copy.wait()
    number, most = codes_s[0, STEPS - 1], codes_s[0, STEPS - 2]

    def prepare(first, last, again):
        @pl.loop(0, 16)
        def _(step):
            for part in range(4):
                chunk = step * 4 + part
                lanes = pl.ds(pl.multiple_of(step * 512, 512) + 128 * part, 128)
                put_targets(columns, chunk, targets(own_ref[:, lanes]), rank_ref[pl.ds(chunk, 1), :], first, last)
                for g in range(first, last):
                    total[pl.ds(g * 1024 + chunk * 16, 16), :] = jnp.zeros((16, 128), F32)

    for_all_groups(most, prepare)

    run_items(number, codes_s, columns, sources, spread, 4, density_item, (total,))

    def collect(first, last, again):
        @pl.loop(0, 16)
        def _(step):
            for part in range(4):
                chunk = step * 4 + part
                (got,) = gather_sums([total], chunk * 2, rank_ref[pl.ds(chunk, 1), :], first, last)
                at = pl.ds(chunk, 1)
                sums[at, :] = sums[at, :] + got if again else got

    for_all_groups(most, collect)
    h = smooth[...]
    fresh = MASS / math.pi / (h * h * h) * (1.0 + 0.25 * sums[...])
    fresh = jnp.where(rank_ref[...] >= 0.0, fresh, extra_ref[pl.ds(0, 64, stride=2), :])
    dens_ref[...] = fresh
    result_ref[...] = fresh


def force_kernel(code_ref, own_ref, ghost_ref, dens_ref, gdens_ref, rank_ref, acc_ref, heat_ref,
                 sources, columns, spread, ax, ay, az, heat):
    number, most = code_ref[0, STEPS - 1], code_ref[0, STEPS - 2]
    spread[...] = widener(10, 16)

    def fields(block, density):
        h = block[6:7]
        press = (5.0 / 3.0 - 1.0) * block[7:8] / density
        hinv = 1.0 / h
        scale = (0.375 * MASS / math.pi) / (h * h * h * h * h)
        near = jnp.full((1, 128), NEAR, F32)
        return jnp.concatenate([block[0:7], press, hinv, scale, near, jnp.zeros((5, 128), F32)], axis=0)

    def own_fields(step, part):
        lanes = pl.ds(pl.multiple_of(step * 512, 512) + 128 * part, 128)
        return fields(own_ref[:, lanes], dens_ref[pl.ds(step * 4 + part, 1), :])

    @pl.loop(0, 16)
    def _(step):
        for part in range(4):
            chunk = step * 4 + part
            lanes = pl.ds(pl.multiple_of(step * 512, 512) + 128 * part, 128)
            put_sources(sources, chunk * 2, own_fields(step, part))
            put_sources(sources, chunk * 2 + 128, fields(ghost_ref[:, lanes], gdens_ref[pl.ds(chunk, 1), :]))

    def prepare(first, last, again):
        @pl.loop(0, 16)
        def _(step):
            for part in range(4):
                chunk = step * 4 + part
                put_targets(columns, chunk, own_fields(step, part), rank_ref[pl.ds(chunk, 1), :], first, last)
                for g in range(first, last):
                    for total in (ax, ay, az, heat):
                        total[pl.ds(g * 1024 + chunk * 16, 16), :] = jnp.zeros((16, 128), F32)

    for_all_groups(most, prepare)
    sub = iota((16, 128), 0)
    sources[256] = jnp.where(sub == 10, FAR, jnp.where((sub == 6) | (sub == 8), 1.0, 0.0))

    run_items(number, code_ref, columns, sources, spread, 10, force_item, (ax, ay, az, heat))

    def collect(first, last, again):
        @pl.loop(0, 16)
        def _(step):
            for part in range(4):
                chunk = step * 4 + part
                got = gather_sums([ax, ay, az, heat], chunk * 2, rank_ref[pl.ds(chunk, 1), :], first, last)
                lanes = pl.ds(pl.multiple_of(step * 512, 512) + 128 * part, 128)
                at = pl.ds(chunk, 1)
                for n in range(3):
                    acc_ref[n : n + 1, lanes] = acc_ref[n : n + 1, lanes] + got[n] if again else got[n]
                heat_ref[at, :] = heat_ref[at, :] - 0.5 * got[3] if again else -0.5 * got[3]

    for_all_groups(most, collect)


VM = pl.BlockSpec(memory_space=pltpu.VMEM)
SM = pl.BlockSpec(memory_space=pltpu.SMEM)


def density_step(columns, own, extra, ghost):
    return pl.pallas_call(
        density_kernel,
        name="density",
        out_shape=(
            jax.ShapeDtypeStruct((64, 128), F32),
            jax.ShapeDtypeStruct((64, 128), F32),
            jax.ShapeDtypeStruct((WAYS, STEPS), I32),
            jax.ShapeDtypeStruct((64, 128), F32),
        ),
        in_specs=[VM, VM, VM, VM],
        out_specs=(VM, VM, VM, VM),
        scratch_shapes=[
            pltpu.VMEM((257, 8, 128), F32),
            pltpu.VMEM((8192, 128), F32),
            pltpu.VMEM((128, 512), BF16),
            pltpu.VMEM((8192, 128), F32),
            pltpu.VMEM((64, 128), F32),
            pltpu.VMEM((64, 128), F32),
            pltpu.SMEM((WAYS, STEPS), I32),
            pltpu.SemaphoreType.DMA,
        ],
        compiler_params=pltpu.CompilerParams(vmem_limit_bytes=24 << 20),
    )(columns, own, extra, ghost)


def force_step(codes, own, ghost, density, ghost_density, rank):
    return pl.pallas_call(
        force_kernel,
        name="force",
        out_shape=(jax.ShapeDtypeStruct((3, 8192), F32), jax.ShapeDtypeStruct((64, 128), F32)),
        in_specs=[SM, VM, VM, VM, VM, VM],
        out_specs=(VM, VM),
        scratch_shapes=[pltpu.VMEM((257, 16, 128), F32), pltpu.VMEM((8192, 128), F32), pltpu.VMEM((128, 1280), BF16)]
        + [pltpu.VMEM((8192, 128), F32)] * 4,
        compiler_params=pltpu.CompilerParams(vmem_limit_bytes=40 << 20),
    )(codes, own, ghost, density, ghost_density, rank)


LEVELS = 4
SEND = 2048
PIECE = 512
BLOCK = 1024
DENSE = 512
DENSE_X = 512
PIECES = SEND // PIECE
GHOSTS = 1024
MESH = pl.DeviceIdType.MESH


def flipped(index, bit):
    step = 1 << bit
    return index + step - 2 * step * ((index // step) % 2)


def neighbour(number, sign, count_x, count_y):
    cell = number + number // 4
    i = (lax.axis_index("gx") + sign * (cell // 3 - 1) + count_x) % count_x
    j = (lax.axis_index("gy") + sign * (cell % 3 - 1) + count_y) % count_y
    return i, j


def spread_state(own, parts):
    for h in range(0, 32, 2):
        pair = jnp.concatenate([own[:, h * 256 : h * 256 + 256], own[:, h * 256 + 256 : h * 256 + 512]], axis=0)
        for n, part in enumerate(split3(pair)):
            parts[n, h * 8 : h * 8 + 16, :] = part


def permuted(value, lanes):
    return jnp.take_along_axis(value, lanes, axis=1, mode="promise_in_bounds")


def one_hot(index_row):
    low = jnp.bitwise_and(index_row, 255)
    return jnp.where(iota((256, index_row.shape[1]), 0) == low, 1.0, 0.0).astype(BF16)


def chosen(read, bits, first, count):
    if count == 1:
        return read(first)
    half = count // 2
    low = chosen(read, bits, first, half)
    high = chosen(read, bits, first + half, half)
    return jnp.where(bits[half.bit_length() - 1], high, low)


def digits_of(value, count):
    return [jnp.bitwise_and(value, 1 << n) != 0 for n in range(count)]


def rows_at(state, index):
    index = jnp.broadcast_to(index, (8, 128))
    low = jnp.bitwise_and(index, 127)
    return chosen(lambda c: permuted(state[:, 128 * c : 128 * c + 128], low), digits_of(index >> 7, 6), 0, 64)


def rows_by_matmul(parts, index):
    hot = one_hot(index)
    found = dot(parts[2], hot) + dot(parts[1], hot) + dot(parts[0], hot)
    bits = digits_of(jnp.broadcast_to(index, (8, 256)) >> 8, 5)
    return chosen(lambda h: found[8 * h : 8 * h + 8], bits, 0, 32)


def pairs_at(extra, index, groups):
    index = jnp.broadcast_to(index, (8, 128))
    low = jnp.bitwise_and(index, 127)
    bits = digits_of(index >> 9, groups.bit_length() - 1)
    out = chosen(lambda g: permuted(extra[8 * g : 8 * g + 8, :], low), bits, 0, groups)
    out = jnp.where(iota((8, 128), 0) >> 1 == jnp.bitwise_and(index >> 7, 3), out, 0.0)
    out = out + pltpu.roll(out, 4, 0)
    return out + pltpu.roll(out, 2, 0)


def cells_at(table, index):
    index = jnp.broadcast_to(index, (8, 128))
    low, high = jnp.bitwise_and(index, 127), (index >> 7) - iota((8, 128), 0)
    out = jnp.zeros((8, 128), table.dtype)
    for v in range(8):
        out = jnp.where(high == 8 * v, permuted(table[8 * v : 8 * v + 8, :], low), out)
    return jnp.sum(out, axis=0, keepdims=True)


def landed(read, slot, old):
    low = jnp.bitwise_and(slot, 127)
    new = chosen(lambda c: permuted(read(c), low), digits_of(slot >> 7, 4), 0, 16)
    return jnp.where(slot >= 0, new, old)


def exchange_kernel(count_x, count_y, used, counts_h, particles_h, old_h, active_h, rows_h, exports_h, pairs_h,
                    own, extra, ghost, columns, exports_3,
                    loads, counts, old, active, rows, exports, pairs, parts, hot, inverse, inverse_wide, slots, slots_x, base_main, base_extra,
                    send_main, send_extra, recv_main, recv_extra, recv_wide,
                    send_ghost, send_sems, recv_sems, ghost_send, ghost_recv):
    i, j = lax.axis_index("gx"), lax.axis_index("gy")
    bits_x, bits_y = count_x.bit_length() - 1, count_y.bit_length() - 1
    partners = [
        (flipped(i, bits_x - 1), j),
        (flipped(i, bits_x - 2), j),
        (i, flipped(j, bits_y - 1)),
        (i, flipped(j, bits_y - 2)),
    ]
    copies = [
        pltpu.make_async_copy(source, target, loads.at[n])
        for n, (source, target) in enumerate(
            ((rows_h, rows), (counts_h, counts), (particles_h, own), (old_h, old), (active_h, active), (exports_h, exports), (pairs_h, pairs))
        )
    ]
    for copy in copies:
        copy.start()
    barrier = pltpu.get_barrier_semaphore()
    for partner in partners:
        pl.semaphore_signal(barrier, inc=1, device_id=partner, device_id_type=MESH)
    for number in range(8):
        pl.semaphore_signal(barrier, inc=1, device_id=neighbour(number, 1, count_x, count_y), device_id_type=MESH)

    def invert(level):
        slot = iota((32, SEND), 1)
        index = rows[level : level + 1, :]
        high = jnp.where(slot < counts[0:1, level : level + 1], jnp.broadcast_to(index >> 8, (32, SEND)), 64)
        here = iota((32, SEND), 0) == high
        digits = jnp.concatenate(
            [
                jnp.where(here, ((slot >> 7) + 1).astype(F32), 0.0),
                jnp.where(here, jnp.bitwise_and(slot, 127).astype(F32), 0.0),
            ],
            axis=0,
        ).astype(BF16)
        for piece in range(PIECES):
            hot[:, piece * PIECE : piece * PIECE + PIECE] = one_hot(index[:, piece * PIECE : piece * PIECE + PIECE])
        found = dot_nt(digits, hot[...])
        found = (128.0 * (found[0:32] - 1.0) + found[32:64]).astype(I32)
        for part in range(2):
            value = found[:, 128 * part : 128 * part + 128]
            inverse[pl.ds(part, 32, stride=2), :] = value
            for field in range(2):
                inverse_wide[level, pl.ds(2 * part + field, 32, stride=4), :] = value

    def main_copy(level, piece):
        lanes = pl.ds(pl.multiple_of(piece * PIECE, PIECE), PIECE)
        return pltpu.make_async_remote_copy(
            src_ref=send_main.at[level, :, lanes],
            dst_ref=recv_main.at[level, :, lanes],
            send_sem=send_sems.at[level, piece],
            recv_sem=recv_sems.at[level, piece],
            device_id=partners[level],
            device_id_type=MESH,
        )

    def extra_copy(level):
        return pltpu.make_async_remote_copy(
            src_ref=send_extra.at[level],
            dst_ref=recv_extra.at[level],
            send_sem=send_sems.at[level, PIECES],
            recv_sem=recv_sems.at[level, PIECES],
            device_id=partners[level],
            device_id_type=MESH,
        )

    def ghost_copy(number):
        lanes = pl.ds(pl.multiple_of(number * GHOSTS, GHOSTS), GHOSTS)
        return pltpu.make_async_remote_copy(
            src_ref=send_ghost.at[:, lanes],
            dst_ref=ghost.at[:, lanes],
            send_sem=ghost_send.at[number],
            recv_sem=ghost_recv.at[number],
            device_id=neighbour(number, 1, count_x, count_y),
            device_id_type=MESH,
        )

    def gather(level, out):
        spread_state(own, parts)

        @pl.loop(0, SEND // BLOCK)
        def _(block):
            at = pl.multiple_of(block * BLOCK, BLOCK)
            for k in range(0, DENSE, 256):
                out[:, pl.ds(at + k, 256)] = rows_by_matmul(parts, rows[level : level + 1, pl.ds(at + k, 256)])
            for k in range(0, BLOCK, 128):
                index = rows[level : level + 1, pl.ds(at + k, 128)]
                base_extra[:, pl.ds(at + k, 128)] = pairs_at(extra, index, 16)
                if k >= DENSE:
                    out[:, pl.ds(at + k, 128)] = rows_at(own, index)

    def compose(level):
        @pl.loop(0, PIECES)
        def _(piece):
            for k in range(PIECE // 128):
                at = pl.multiple_of(piece * PIECE + 128 * k, 128)
                slots[:, pl.ds(at, 128)] = cells_at(inverse, rows[level : level + 1, pl.ds(at, 128)])

    def send(level):
        for piece in range(PIECES):
            for k in range(PIECE // 128):
                c = piece * (PIECE // 128) + k
                lanes = slice(128 * c, 128 * c + 128)
                both = base_extra[:, lanes]
                if level > 0:
                    slot = jnp.broadcast_to(slots[:, lanes], (8, 128))
                    send_main[level, :, lanes] = landed(
                        lambda n: recv_main[level - 1, :, 128 * n : 128 * n + 128], slot, base_main[:, lanes]
                    )
                    fresh = pairs_at(recv_extra.at[level - 1], jnp.maximum(slots[:, lanes], 0), 4)
                    both = jnp.where(slot >= 0, fresh, both)
                send_extra[level, 2 * c : 2 * c + 2, :] = both[0:2]
            main_copy(level, piece).start()
        extra_copy(level).start()

    def arrive(level):
        extra_copy(level).wait()
        for piece in range(PIECES):
            main_copy(level, piece).wait()

    def settle(level):
        for c in range(16):
            wide = jnp.concatenate([recv_extra[level, 2 * c : 2 * c + 2, :]] * 4, axis=0)
            recv_wide[:, 128 * c : 128 * c + 128] = wide

        @pl.loop(0, 8)
        def _(step):
            for late in range(2):
                g = step * 2 + late
                at = pl.multiple_of(g * 8, 8)
                slot = inverse_wide[level, pl.ds(at, 8), :]
                extra[pl.ds(at, 8), :] = landed(
                    lambda c: recv_wide[:, 128 * c : 128 * c + 128], slot, extra[pl.ds(at, 8), :]
                )
                for b in range(4):
                    lanes = pl.ds(pl.multiple_of(g * 512, 512) + 128 * b, 128)
                    slot_b = jnp.broadcast_to(slot[2 * b : 2 * b + 1], (8, 128))
                    own[:, lanes] = landed(
                        lambda c: recv_main[level, :, 128 * c : 128 * c + 128], slot_b, own[:, lanes]
                    )

    for copy in copies:
        copy.wait()
    extra[pl.ds(0, 64, stride=2), :] = old[...]
    extra[pl.ds(1, 64, stride=2), :] = active[...].astype(F32)
    for number in range(8):
        exports_3[number] = exports[number : number + 1, :]
    gather(0, send_main.at[0])
    pl.semaphore_wait(barrier, 12)

    for level in range(LEVELS):
        send(level)
        if level == 0:
            columns[...] = pair_columns(pairs[...].astype(F32), used[0])
        invert(level)
        if level > 0:
            settle(level - 1)
        if level + 1 < LEVELS:
            compose(level + 1)
            gather(level + 1, base_main)
        else:

            spread_state(own, parts)

            @pl.loop(0, 8)
            def _(number):
                at = pl.multiple_of(number * GHOSTS, GHOSTS)
                for k in range(0, DENSE_X, 256):
                    send_ghost[:, pl.ds(at + k, 256)] = rows_by_matmul(parts, exports_3[number, :, k : k + 256])
                for k in range(0, GHOSTS, 128):
                    index = exports_3[number, :, k : k + 128]
                    slots_x[number, :, k : k + 128] = cells_at(inverse, index)
                    if k >= DENSE_X:
                        send_ghost[:, pl.ds(at + k, 128)] = rows_at(own, index)

        arrive(level)

    @pl.loop(0, 8)
    def _(number):
        for k in range(8):
            lanes = pl.ds(pl.multiple_of(number * GHOSTS, GHOSTS) + 128 * k, 128)
            slot = jnp.broadcast_to(slots_x[number, :, 128 * k : 128 * k + 128], (8, 128))
            send_ghost[:, lanes] = landed(
                lambda n: recv_main[LEVELS - 1, :, 128 * n : 128 * n + 128], slot, send_ghost[:, lanes]
            )
        ghost_copy(number).start()

    settle(LEVELS - 1)
    for number in range(8):
        ghost_copy(number).wait()


HB = pl.BlockSpec(memory_space=pltpu.HBM)


def exchange(mesh, send_count, pair_count, particles, old, active, send_rows, export_rows, pair_tiles):
    count_x, count_y = mesh.shape["gx"], mesh.shape["gy"]
    return pl.pallas_call(
        functools.partial(exchange_kernel, count_x, count_y),
        name="exchange",
        out_shape=(
            jax.ShapeDtypeStruct((8, 8192), F32),
            jax.ShapeDtypeStruct((128, 128), F32),
            jax.ShapeDtypeStruct((8, 8192), F32),
            jax.ShapeDtypeStruct((8, COLS), F32),
            jax.ShapeDtypeStruct((8, 1, GHOSTS), I32),
        ),
        in_specs=[SM, HB, HB, HB, HB, HB, HB, HB],
        out_specs=(VM, VM, VM, VM, VM),
        scratch_shapes=[
            pltpu.SemaphoreType.DMA((7,)),
            pltpu.VMEM((1, 4), I32),
            pltpu.VMEM((64, 128), F32),
            pltpu.VMEM((64, 128), I32),
            pltpu.VMEM((LEVELS, SEND), I32),
            pltpu.VMEM((8, GHOSTS), I32),
            pltpu.VMEM((2, 512), I32),
            pltpu.VMEM((3, 256, 256), BF16),
            pltpu.VMEM((256, SEND), BF16),
            pltpu.VMEM((64, 128), I32),
            pltpu.VMEM((LEVELS, 128, 128), I32),
            pltpu.VMEM((1, SEND), I32),
            pltpu.VMEM((8, 1, GHOSTS), I32),
            pltpu.VMEM((8, SEND), F32),
            pltpu.VMEM((8, SEND), F32),
            pltpu.VMEM((LEVELS, 8, SEND), F32),
            pltpu.VMEM((LEVELS, 32, 128), F32),
            pltpu.VMEM((LEVELS, 8, SEND), F32),
            pltpu.VMEM((LEVELS, 32, 128), F32),
            pltpu.VMEM((8, SEND), F32),
            pltpu.VMEM((8, 8 * GHOSTS), F32),
            pltpu.SemaphoreType.DMA((LEVELS, PIECES + 1)),
            pltpu.SemaphoreType.DMA((LEVELS, PIECES + 1)),
            pltpu.SemaphoreType.DMA((8,)),
            pltpu.SemaphoreType.DMA((8,)),
        ],
        compiler_params=pltpu.CompilerParams(
            collective_id=0, has_side_effects=True, vmem_limit_bytes=24 << 20
        ),
    )(
        pair_count,
        *[
            pltpu.with_memory_space_constraint(x, pltpu.HBM)
            for x in (send_count, particles, old, active, send_rows, export_rows, pair_tiles)
        ],
    )


def ghost_density_kernel(count_x, count_y, density, exports_3, out, send, send_sems, recv_sems):
    barrier = pltpu.get_barrier_semaphore()
    for number in range(8):
        pl.semaphore_signal(barrier, inc=1, device_id=neighbour(number, 1, count_x, count_y), device_id_type=MESH)

    def copy(number):
        return pltpu.make_async_remote_copy(
            src_ref=send.at[number],
            dst_ref=out.at[number],
            send_sem=send_sems.at[number],
            recv_sem=recv_sems.at[number],
            device_id=neighbour(number, 1, count_x, count_y),
            device_id_type=MESH,
        )

    def gathered(number):
        for k in range(8):
            send[number, k : k + 1, :] = cells_at(density, exports_3[number, :, 128 * k : 128 * k + 128])

    gathered(0)
    pl.semaphore_wait(barrier, 8)
    copy(0).start()

    @pl.loop(1, 8)
    def _(number):
        gathered(number)
        copy(number).start()

    for number in range(8):
        copy(number).wait()


def ghost_density_step(mesh, density, export_rows):
    return pl.pallas_call(
        functools.partial(ghost_density_kernel, mesh.shape["gx"], mesh.shape["gy"]),
        name="ghost_density",
        out_shape=jax.ShapeDtypeStruct((8, 8, 128), F32),
        in_specs=[VM, VM],
        out_specs=VM,
        scratch_shapes=[
            pltpu.VMEM((8, 8, 128), F32),
            pltpu.SemaphoreType.DMA((8,)),
            pltpu.SemaphoreType.DMA((8,)),
        ],
        compiler_params=pltpu.CompilerParams(collective_id=1, has_side_effects=True, vmem_limit_bytes=8 << 20),
    )(density, export_rows)


def on_device(
    mesh, particles, old_density, active, send_rows, send_count, export_rows, pair_tiles, pair_count
):
    own, extra, ghost, columns, exports = exchange(
        mesh,
        send_count.T,
        pair_count,
        particles,
        old_density.reshape(64, 128),
        active.reshape(64, 128),
        send_rows,
        export_rows,
        pair_tiles,
    )
    result, density, codes, rank = density_step(columns, own, extra, ghost)
    ghost_density = ghost_density_step(mesh, density, exports).reshape(64, 128)
    acceleration, heating = force_step(codes, own, ghost, density, ghost_density, rank)
    return result.reshape(8192), acceleration, heating.reshape(8192)


def solution(mesh):
    in_specs = (
        P(None, ("gx", "gy")),
        P(("gx", "gy")),
        P(("gx", "gy")),
        P(None, ("gx", "gy")),
        P(None, ("gx", "gy")),
        P(None, ("gx", "gy")),
        P(None, ("gx", "gy")),
        P(("gx", "gy")),
    )
    out_specs = (P(("gx", "gy")), P(None, ("gx", "gy")), P(("gx", "gy")))
    return jax.shard_map(
        functools.partial(on_device, mesh), mesh=mesh, in_specs=in_specs, out_specs=out_specs, check_vma=False
    )
```

```python
import functools
import math

import jax
import jax.numpy as jnp
from jax import lax
from jax.experimental import pallas as pl
from jax.experimental.pallas import tpu as pltpu
from jax.sharding import PartitionSpec as P

F32 = jnp.float32
BF16 = jnp.bfloat16
I32 = jnp.int32
MASS = 1.0 / 512.0
NEAR = 1e-30
FAR = 1e36
NT_DIMS = (((1,), (1,)), ((), ()))
COLS = 320
STEPS = 384
WAYS = 8
SPAN = 16
TAIL = 4
FEW = 4


def iota(shape, axis):
    return lax.broadcasted_iota(I32, shape, axis)


def split3(x):
    a = x.astype(BF16)
    r = x - a.astype(F32)
    b = r.astype(BF16)
    c = (r - b.astype(F32)).astype(BF16)
    return a, b, c


def dot(a, b):
    return jnp.dot(a, b, preferred_element_type=F32)


def dot_nt(a, b):
    return lax.dot_general(a, b, NT_DIMS, preferred_element_type=F32)


def swap_halves(x):
    return pltpu.roll(x, 64, x.ndim - 1)


def ranks_of(active):
    rows, cols = iota((128, 128), 0), iota((128, 128), 1)
    before = ((rows // 64 == cols // 64) & (rows < cols)).astype(F32).astype(BF16)
    rank = dot(active.astype(BF16), before)
    return jnp.where(active > 0.5, rank, -1.0)


def tile_groups(active):
    rows, cols = iota((128, 128), 0), iota((128, 128), 1)
    pick = (rows // 64 == cols % 2).astype(F32).astype(BF16)
    count = dot(active.astype(BF16), pick)
    own = iota((64, 128), 0) == iota((64, 128), 1) // 2
    total = jnp.sum(jnp.where(own, count, 0.0), axis=0, keepdims=True)
    return jnp.floor((total + 7.0) * 0.125)


def pair_columns(pairs, used):
    target, source = pairs[0:1], pairs[1:2]
    count = pairs.shape[1]
    target_col = jnp.broadcast_to(target, (8, count)).T[:, 0:1]
    used_row = iota((1, count), 1) < used
    q, p = iota((count, count), 0), iota((count, count), 1)
    same = (target_col == target) & (q < p) & (q < used)
    order = jnp.sum(jnp.where(same, 1.0, 0.0), axis=0, keepdims=True)
    at = (iota((128, count), 0).astype(F32) == target) & used_row
    at_f = jnp.where(at, 1.0, 0.0)
    number = jnp.sum(at_f, axis=1, keepdims=True)
    columns = jnp.floor((number + 1.0) * 0.5)
    below = (iota((128, 128), 0) > iota((128, 128), 1)).astype(F32).astype(BF16)
    first = dot(below, jnp.broadcast_to(columns, (128, 128)).astype(BF16))[:, 0:1]
    first_row = jnp.sum(at_f * first, axis=0, keepdims=True)
    half = jnp.floor(order * 0.5)
    column = first_row + half
    second = jnp.where(order - 2.0 * half > 0.5, 1.0, 0.0)
    use = jnp.where(used_row, 1.0, 0.0)
    lead = use * (1.0 - second)
    trail = use * second
    zero = lead * 0.0
    values = jnp.concatenate(
        [target * lead, source * lead, source * trail, lead, trail, zero, zero, zero], axis=0
    ).astype(BF16)
    match = jnp.where((iota((COLS, count), 0).astype(F32) == column) & used_row, 1.0, 0.0).astype(BF16)
    found = dot_nt(values, match)
    alone = 256.0 * (1.0 - found[4:5])
    return jnp.where(iota(found.shape, 0) == 2, found + alone, found)


def item_codes(in_row, groups):
    tile = jnp.where(iota((128, COLS), 0).astype(F32) == in_row[0:1], 1.0, 0.0).astype(BF16)
    size = dot(jnp.broadcast_to(groups, (8, 128)).astype(BF16), tile) * in_row[3:4]
    upper = (iota((COLS, COLS), 0) < iota((COLS, COLS), 1)).astype(F32).astype(BF16)
    lower = (iota((COLS, COLS), 0) > iota((COLS, COLS), 1)).astype(F32).astype(BF16)
    start_row = dot(size.astype(BF16), upper)[0:1]
    start_col = dot_nt(lower, size.astype(BF16))[:, 0:1]
    total = jnp.sum(size[0:1], axis=1, keepdims=True)
    high = jnp.floor(start_row * (1.0 / 256.0))
    table = jnp.concatenate(
        [in_row[0:3], high, start_row - 256.0 * high, high * 0.0, high * 0.0, high * 0.0], axis=0
    )
    table = jnp.concatenate([table, jnp.zeros((8, 128 * ((COLS + 127) // 128) - COLS), F32)], axis=1)
    before = jnp.where(iota(table.shape, 1) == 0, 0.0, pltpu.roll(table, 1, 1))
    steps = (table - before)[:, 0:COLS].astype(BF16)
    at = iota((1, WAYS * STEPS), 1)
    item = (at % STEPS * WAYS + at // STEPS).astype(F32)
    found = dot(steps, jnp.where(item >= start_col, 1.0, 0.0).astype(BF16))
    beyond = item >= total
    group = item - 256.0 * found[3:4] - found[4:5]
    place = jnp.where(beyond, 0.0, group * 128.0 + found[0:1]).astype(I32)
    first_source = jnp.where(beyond, 256.0, found[1:2]).astype(I32)
    other = jnp.where(beyond, 256.0, found[2:3]).astype(I32)
    codes = place + first_source * 1024 + other * (1 << 19)
    codes = jnp.concatenate([codes[:, STEPS * w : STEPS * w + STEPS] for w in range(WAYS)], axis=0)
    most = jnp.max(groups, axis=1, keepdims=True).astype(I32)
    lane = iota(codes.shape, 1)
    return jnp.where(lane == STEPS - 1, total.astype(I32), jnp.where(lane == STEPS - 2, most, codes))


def put_sources(table, slot, chunk):
    left = iota(chunk.shape, 1) < 64
    other = swap_halves(chunk)
    table[slot] = jnp.where(left, chunk, other)
    table[slot + 1] = jnp.where(left, other, chunk)


def put_targets(columns, chunk, fields, rank, first, last):
    parts = jnp.concatenate([part.astype(F32) for part in split3(fields)], axis=0)
    parts = jnp.concatenate([parts, jnp.zeros((128 - parts.shape[0], 128), F32)], axis=0).astype(BF16)
    wide = jnp.broadcast_to(rank, (8, 128))
    left = iota((8, 128), 1) < 64
    sub = iota((8, 128), 0).astype(F32)
    ours = jnp.where(left, wide, -1.0), jnp.where(left, -1.0, wide)
    pick = jnp.concatenate(
        [jnp.where(our == sub + 8.0 * g, 1.0, 0.0) for g in range(first, last) for our in ours], axis=0
    ).astype(BF16)
    rows = dot_nt(pick, parts)
    for g in range(first, last):
        columns[pl.ds(g * 1024 + chunk * 16, 16), :] = rows[16 * (g - first) : 16 * (g - first) + 16]


def widener(fields, stride):
    k, n = iota((128, 128 * fields), 0), iota((128, 128 * fields), 1)
    return ((k % stride == n // 128) & (k < 3 * stride)).astype(F32).astype(BF16)


def gather_sums(totals, tile, rank, first, last):
    left = iota((8, 128), 1) < 64
    wide = jnp.broadcast_to(rank, (8, 128))
    sub = iota((8, 128), 0).astype(F32)
    out = [jnp.zeros((8, 128), F32) for _ in totals]
    for g in range(first, last):
        hit = wide == sub + 8.0 * g
        for n, total in enumerate(totals):
            one = jnp.sum(total[pl.ds(g * 1024 + tile * 8, 8), :], axis=1, keepdims=True)
            two = jnp.sum(total[pl.ds(g * 1024 + tile * 8 + 8, 8), :], axis=1, keepdims=True)
            out[n] = out[n] + jnp.where(hit, jnp.where(left, one, two), 0.0)
    return [jnp.sum(o, axis=0, keepdims=True) for o in out]


def wrapped(a, b):
    s = a - b
    return s - jnp.floor(s + 0.5)


def decode(code):
    return code & 1023, (code >> 10) & 511, code >> 19


def density_item(mine, other):
    dx = wrapped(mine[0], other[0:1])
    dy = wrapped(mine[1], other[1:2])
    dz = wrapped(mine[2], other[2:3])
    rsq = jnp.maximum(dx * dx + dy * dy + dz * dz, other[3:4])
    q = rsq * lax.rsqrt(rsq) * mine[3]
    t = jnp.maximum(2.0 - q, 0.0)
    u = jnp.maximum(1.0 - q, 0.0)
    return (t * t * t - 4.0 * (u * u * u),)


def force_item(mine, other):
    dx = wrapped(mine[0], other[0:1])
    dy = wrapped(mine[1], other[1:2])
    dz = wrapped(mine[2], other[2:3])
    rsq = jnp.maximum(dx * dx + dy * dy + dz * dz, other[10:11])
    inv = lax.rsqrt(rsq)
    r = rsq * inv

    def profile(h, hinv):
        q = r * hinv
        t = jnp.maximum(2.0 - q, 0.0)
        return jnp.where(q < 1.0, 4.0 - 3.0 * q, t * t * (h * inv))

    slope = profile(mine[6], mine[8]) * mine[9] + profile(other[6:7], other[8:9]) * other[9:10]
    w = (mine[7] + other[7:8]) * slope
    gap = (mine[3] - other[3:4]) * dx + (mine[4] - other[4:5]) * dy + (mine[5] - other[5:6]) * dz
    return (w * dx, w * dy, w * dz, w * gap)


def for_all_groups(most, body):
    body(0, FEW, False)

    @pl.when(most > FEW)
    def _():
        body(FEW, 8, True)


def run_items(number, codes, columns, sources, spread, fields, item, totals):
    def steps(first, count):
        for late in range(0, count, 2):
            places = [decode(codes[way, first + late + n]) for n in range(2) for way in range(WAYS)]
            rows = [pl.multiple_of(place * 8, 8) for place, _, _ in places]
            mine = jnp.concatenate([columns[pl.ds(row, 8), :] for row in rows], axis=0).astype(BF16)
            wide = dot(mine, spread[...])
            for n, (_, one, two) in enumerate(places):
                first_tile, second_tile = sources[one], sources[two]
                other = jnp.where(iota(first_tile.shape, 1) < 64, first_tile, second_tile)
                own = [wide[8 * n : 8 * n + 8, 128 * f : 128 * f + 128] for f in range(fields)]
                for total, term in zip(totals, item(own, other)):
                    total[pl.ds(rows[n], 8), :] += term

    spans = number // (SPAN * WAYS)

    @pl.loop(0, spans)
    def _(span):
        steps(SPAN * span, SPAN)

    rest = number - spans * (SPAN * WAYS)

    @pl.loop(0, (rest + TAIL * WAYS - 1) // (TAIL * WAYS))
    def _(tail):
        steps(SPAN * spans + TAIL * tail, TAIL)


def density_kernel(cols_ref, own_ref, extra_ref, ghost_ref, result_ref, dens_ref, code_ref, rank_ref,
                   sources, columns, spread, total, sums, smooth, codes_s, sem):
    active = extra_ref[pl.ds(1, 64, stride=2), :]
    spread[...] = widener(4, 8)
    rank_ref[...] = ranks_of(active)
    code_ref[...] = item_codes(cols_ref[...], tile_groups(active))
    copy = pltpu.make_async_copy(code_ref, codes_s, sem)
    copy.start()

    def fields(block):
        sub = iota((8, 128), 0)
        return jnp.where(sub < 3, block, jnp.where(sub == 3, NEAR, 0.0))

    def targets(block):
        sub = iota((8, 128), 0)
        return jnp.where(sub < 3, block, jnp.where(sub == 3, 1.0 / block[6:7], 0.0))

    @pl.loop(0, 16)
    def _(step):
        for part in range(4):
            chunk = step * 4 + part
            lanes = pl.ds(pl.multiple_of(step * 512, 512) + 128 * part, 128)
            block = own_ref[:, lanes]
            smooth[pl.ds(chunk, 1), :] = block[6:7]
            put_sources(sources, chunk * 2, fields(block))
            put_sources(sources, chunk * 2 + 128, fields(ghost_ref[:, lanes]))

    sources[256] = jnp.where(iota((8, 128), 0) == 3, FAR, 0.0)
    copy.wait()
    number, most = codes_s[0, STEPS - 1], codes_s[0, STEPS - 2]

    def prepare(first, last, again):
        @pl.loop(0, 16)
        def _(step):
            for part in range(4):
                chunk = step * 4 + part
                lanes = pl.ds(pl.multiple_of(step * 512, 512) + 128 * part, 128)
                put_targets(columns, chunk, targets(own_ref[:, lanes]), rank_ref[pl.ds(chunk, 1), :], first, last)
                for g in range(first, last):
                    total[pl.ds(g * 1024 + chunk * 16, 16), :] = jnp.zeros((16, 128), F32)

    for_all_groups(most, prepare)

    run_items(number, codes_s, columns, sources, spread, 4, density_item, (total,))

    def collect(first, last, again):
        @pl.loop(0, 16)
        def _(step):
            for part in range(4):
                chunk = step * 4 + part
                (got,) = gather_sums([total], chunk * 2, rank_ref[pl.ds(chunk, 1), :], first, last)
                at = pl.ds(chunk, 1)
                sums[at, :] = sums[at, :] + got if again else got

    for_all_groups(most, collect)
    h = smooth[...]
    fresh = MASS / math.pi / (h * h * h) * (1.0 + 0.25 * sums[...])
    fresh = jnp.where(rank_ref[...] >= 0.0, fresh, extra_ref[pl.ds(0, 64, stride=2), :])
    dens_ref[...] = fresh
    result_ref[...] = fresh


def force_kernel(code_ref, own_ref, ghost_ref, dens_ref, gdens_ref, rank_ref, acc_ref, heat_ref,
                 sources, columns, spread, ax, ay, az, heat):
    number, most = code_ref[0, STEPS - 1], code_ref[0, STEPS - 2]
    spread[...] = widener(10, 16)

    def fields(block, density):
        h = block[6:7]
        press = (5.0 / 3.0 - 1.0) * block[7:8] / density
        hinv = 1.0 / h
        scale = (0.375 * MASS / math.pi) / (h * h * h * h * h)
        near = jnp.full((1, 128), NEAR, F32)
        return jnp.concatenate([block[0:7], press, hinv, scale, near, jnp.zeros((5, 128), F32)], axis=0)

    def own_fields(step, part):
        lanes = pl.ds(pl.multiple_of(step * 512, 512) + 128 * part, 128)
        return fields(own_ref[:, lanes], dens_ref[pl.ds(step * 4 + part, 1), :])

    @pl.loop(0, 16)
    def _(step):
        for part in range(4):
            chunk = step * 4 + part
            lanes = pl.ds(pl.multiple_of(step * 512, 512) + 128 * part, 128)
            put_sources(sources, chunk * 2, own_fields(step, part))
            put_sources(sources, chunk * 2 + 128, fields(ghost_ref[:, lanes], gdens_ref[pl.ds(chunk, 1), :]))

    def prepare(first, last, again):
        @pl.loop(0, 16)
        def _(step):
            for part in range(4):
                chunk = step * 4 + part
                put_targets(columns, chunk, own_fields(step, part), rank_ref[pl.ds(chunk, 1), :], first, last)
                for g in range(first, last):
                    for total in (ax, ay, az, heat):
                        total[pl.ds(g * 1024 + chunk * 16, 16), :] = jnp.zeros((16, 128), F32)

    for_all_groups(most, prepare)
    sub = iota((16, 128), 0)
    sources[256] = jnp.where(sub == 10, FAR, jnp.where((sub == 6) | (sub == 8), 1.0, 0.0))

    run_items(number, code_ref, columns, sources, spread, 10, force_item, (ax, ay, az, heat))

    def collect(first, last, again):
        @pl.loop(0, 16)
        def _(step):
            for part in range(4):
                chunk = step * 4 + part
                got = gather_sums([ax, ay, az, heat], chunk * 2, rank_ref[pl.ds(chunk, 1), :], first, last)
                lanes = pl.ds(pl.multiple_of(step * 512, 512) + 128 * part, 128)
                at = pl.ds(chunk, 1)
                for n in range(3):
                    acc_ref[n : n + 1, lanes] = acc_ref[n : n + 1, lanes] + got[n] if again else got[n]
                heat_ref[at, :] = heat_ref[at, :] - 0.5 * got[3] if again else -0.5 * got[3]

    for_all_groups(most, collect)


VM = pl.BlockSpec(memory_space=pltpu.VMEM)
SM = pl.BlockSpec(memory_space=pltpu.SMEM)


def density_step(columns, own, extra, ghost):
    return pl.pallas_call(
        density_kernel,
        name="density",
        out_shape=(
            jax.ShapeDtypeStruct((64, 128), F32),
            jax.ShapeDtypeStruct((64, 128), F32),
            jax.ShapeDtypeStruct((WAYS, STEPS), I32),
            jax.ShapeDtypeStruct((64, 128), F32),
        ),
        in_specs=[VM, VM, VM, VM],
        out_specs=(VM, VM, VM, VM),
        scratch_shapes=[
            pltpu.VMEM((257, 8, 128), F32),
            pltpu.VMEM((8192, 128), F32),
            pltpu.VMEM((128, 512), BF16),
            pltpu.VMEM((8192, 128), F32),
            pltpu.VMEM((64, 128), F32),
            pltpu.VMEM((64, 128), F32),
            pltpu.SMEM((WAYS, STEPS), I32),
            pltpu.SemaphoreType.DMA,
        ],
        compiler_params=pltpu.CompilerParams(vmem_limit_bytes=24 << 20),
    )(columns, own, extra, ghost)


def force_step(codes, own, ghost, density, ghost_density, rank):
    return pl.pallas_call(
        force_kernel,
        name="force",
        out_shape=(jax.ShapeDtypeStruct((3, 8192), F32), jax.ShapeDtypeStruct((64, 128), F32)),
        in_specs=[SM, VM, VM, VM, VM, VM],
        out_specs=(VM, VM),
        scratch_shapes=[pltpu.VMEM((257, 16, 128), F32), pltpu.VMEM((8192, 128), F32), pltpu.VMEM((128, 1280), BF16)]
        + [pltpu.VMEM((8192, 128), F32)] * 4,
        compiler_params=pltpu.CompilerParams(vmem_limit_bytes=40 << 20),
    )(codes, own, ghost, density, ghost_density, rank)


LEVELS = 4
SEND = 2048
PIECE = 512
BLOCK = 1024
DENSE = 512
DENSE_X = 512
PIECES = SEND // PIECE
GHOSTS = 1024
MESH = pl.DeviceIdType.MESH


def flipped(index, bit):
    step = 1 << bit
    return index + step - 2 * step * ((index // step) % 2)


def neighbour(number, sign, count_x, count_y):
    cell = number + number // 4
    i = (lax.axis_index("gx") + sign * (cell // 3 - 1) + count_x) % count_x
    j = (lax.axis_index("gy") + sign * (cell % 3 - 1) + count_y) % count_y
    return i, j


def spread_state(own, parts):
    for h in range(0, own.shape[1] // 256, 2):
        pair = jnp.concatenate([own[:, h * 256 : h * 256 + 256], own[:, h * 256 + 256 : h * 256 + 512]], axis=0)
        for n, part in enumerate(split3(pair)):
            parts[n, h * 8 : h * 8 + 16, :] = part


def permuted(value, lanes):
    return jnp.take_along_axis(value, lanes, axis=1, mode="promise_in_bounds")


def one_hot(index_row):
    low = jnp.bitwise_and(index_row, 255)
    return jnp.where(iota((256, index_row.shape[1]), 0) == low, 1.0, 0.0).astype(BF16)


def chosen(read, bits, first, count):
    if count == 1:
        return read(first)
    half = count // 2
    low = chosen(read, bits, first, half)
    high = chosen(read, bits, first + half, half)
    return jnp.where(bits[half.bit_length() - 1], high, low)


def digits_of(value, count):
    return [jnp.bitwise_and(value, 1 << n) != 0 for n in range(count)]


def rows_at(state, index):
    index = jnp.broadcast_to(index, (8, 128))
    low = jnp.bitwise_and(index, 127)
    return chosen(lambda c: permuted(state[:, 128 * c : 128 * c + 128], low), digits_of(index >> 7, 6), 0, 64)


def rows_by_matmul(parts, index):
    blocks = parts.shape[1] // 8
    hot = one_hot(index)
    found = dot(parts[2], hot) + dot(parts[1], hot) + dot(parts[0], hot)
    bits = digits_of(jnp.broadcast_to(index, (8, 256)) >> 8, blocks.bit_length() - 1)
    return chosen(lambda h: found[8 * h : 8 * h + 8], bits, 0, blocks)


def pairs_at(extra, index, groups):
    index = jnp.broadcast_to(index, (8, 128))
    low = jnp.bitwise_and(index, 127)
    bits = digits_of(index >> 9, groups.bit_length() - 1)
    out = chosen(lambda g: permuted(extra[8 * g : 8 * g + 8, :], low), bits, 0, groups)
    out = jnp.where(iota((8, 128), 0) >> 1 == jnp.bitwise_and(index >> 7, 3), out, 0.0)
    out = out + pltpu.roll(out, 4, 0)
    return out + pltpu.roll(out, 2, 0)


def cells_at(table, index):
    index = jnp.broadcast_to(index, (8, 128))
    low, high = jnp.bitwise_and(index, 127), (index >> 7) - iota((8, 128), 0)
    out = jnp.zeros((8, 128), table.dtype)
    for v in range(8):
        out = jnp.where(high == 8 * v, permuted(table[8 * v : 8 * v + 8, :], low), out)
    return jnp.sum(out, axis=0, keepdims=True)


def landed(read, slot, old):
    low = jnp.bitwise_and(slot, 127)
    new = chosen(lambda c: permuted(read(c), low), digits_of(slot >> 7, 4), 0, 16)
    return jnp.where(slot >= 0, new, old)


def exchange_kernel(count_x, count_y, used, counts_h, particles_h, old_h, active_h, rows_h, exports_h, pairs_h,
                    own, extra, ghost, columns, exports_3,
                    loads, counts, old, active, rows, exports, pairs, parts, parts_in, hot, inverse, inverse_wide, slots, slots_x, base_main, base_extra,
                    send_main, send_extra, recv_main, recv_extra, recv_wide,
                    send_ghost, send_sems, recv_sems, ghost_send, ghost_recv):
    i, j = lax.axis_index("gx"), lax.axis_index("gy")
    bits_x, bits_y = count_x.bit_length() - 1, count_y.bit_length() - 1
    partners = [
        (flipped(i, bits_x - 1), j),
        (flipped(i, bits_x - 2), j),
        (i, flipped(j, bits_y - 1)),
        (i, flipped(j, bits_y - 2)),
    ]
    copies = [
        pltpu.make_async_copy(source, target, loads.at[n])
        for n, (source, target) in enumerate(
            ((rows_h, rows), (counts_h, counts), (particles_h, own), (old_h, old), (active_h, active), (exports_h, exports), (pairs_h, pairs))
        )
    ]
    for copy in copies:
        copy.start()
    barrier = pltpu.get_barrier_semaphore()
    for partner in partners:
        pl.semaphore_signal(barrier, inc=1, device_id=partner, device_id_type=MESH)
    for number in range(8):
        pl.semaphore_signal(barrier, inc=1, device_id=neighbour(number, 1, count_x, count_y), device_id_type=MESH)

    def invert(level):
        slot = iota((32, SEND), 1)
        index = rows[level : level + 1, :]
        high = jnp.where(slot < counts[0:1, level : level + 1], jnp.broadcast_to(index >> 8, (32, SEND)), 64)
        here = iota((32, SEND), 0) == high
        digits = jnp.concatenate(
            [
                jnp.where(here, ((slot >> 7) + 1).astype(F32), 0.0),
                jnp.where(here, jnp.bitwise_and(slot, 127).astype(F32), 0.0),
            ],
            axis=0,
        ).astype(BF16)
        for piece in range(PIECES):
            hot[:, piece * PIECE : piece * PIECE + PIECE] = one_hot(index[:, piece * PIECE : piece * PIECE + PIECE])
        found = dot_nt(digits, hot[...])
        found = (128.0 * (found[0:32] - 1.0) + found[32:64]).astype(I32)
        for part in range(2):
            value = found[:, 128 * part : 128 * part + 128]
            inverse[pl.ds(part, 32, stride=2), :] = value
            for field in range(2):
                inverse_wide[level, pl.ds(2 * part + field, 32, stride=4), :] = value

    def main_copy(level, piece):
        lanes = pl.ds(pl.multiple_of(piece * PIECE, PIECE), PIECE)
        return pltpu.make_async_remote_copy(
            src_ref=send_main.at[level, :, lanes],
            dst_ref=recv_main.at[level, :, lanes],
            send_sem=send_sems.at[level, piece],
            recv_sem=recv_sems.at[level, piece],
            device_id=partners[level],
            device_id_type=MESH,
        )

    def extra_copy(level):
        return pltpu.make_async_remote_copy(
            src_ref=send_extra.at[level],
            dst_ref=recv_extra.at[level],
            send_sem=send_sems.at[level, PIECES],
            recv_sem=recv_sems.at[level, PIECES],
            device_id=partners[level],
            device_id_type=MESH,
        )

    def ghost_copy(number):
        lanes = pl.ds(pl.multiple_of(number * GHOSTS, GHOSTS), GHOSTS)
        return pltpu.make_async_remote_copy(
            src_ref=send_ghost.at[:, lanes],
            dst_ref=ghost.at[:, lanes],
            send_sem=ghost_send.at[number],
            recv_sem=ghost_recv.at[number],
            device_id=neighbour(number, 1, count_x, count_y),
            device_id_type=MESH,
        )

    def gather(level, out):
        spread_state(own, parts)

        @pl.loop(0, SEND // BLOCK)
        def _(block):
            at = pl.multiple_of(block * BLOCK, BLOCK)
            for k in range(0, DENSE, 256):
                out[:, pl.ds(at + k, 256)] = rows_by_matmul(parts, rows[level : level + 1, pl.ds(at + k, 256)])
            for k in range(0, BLOCK, 128):
                index = rows[level : level + 1, pl.ds(at + k, 128)]
                base_extra[:, pl.ds(at + k, 128)] = pairs_at(extra, index, 16)
                if k >= DENSE:
                    out[:, pl.ds(at + k, 128)] = rows_at(own, index)

    def compose(level):
        @pl.loop(0, PIECES)
        def _(piece):
            for k in range(PIECE // 128):
                at = pl.multiple_of(piece * PIECE + 128 * k, 128)
                slots[:, pl.ds(at, 128)] = cells_at(inverse, rows[level : level + 1, pl.ds(at, 128)])

    def send(level):
        for piece in range(PIECES):
            for k in range(PIECE // 128):
                c = piece * (PIECE // 128) + k
                lanes = slice(128 * c, 128 * c + 128)
                both = base_extra[:, lanes]
                if level > 0:
                    slot = jnp.broadcast_to(slots[:, lanes], (8, 128))
                    send_main[level, :, lanes] = landed(
                        lambda n: recv_main[level - 1, :, 128 * n : 128 * n + 128], slot, base_main[:, lanes]
                    )
                    fresh = pairs_at(recv_extra.at[level - 1], jnp.maximum(slots[:, lanes], 0), 4)
                    both = jnp.where(slot >= 0, fresh, both)
                send_extra[level, 2 * c : 2 * c + 2, :] = both[0:2]
            main_copy(level, piece).start()
        extra_copy(level).start()

    def arrive(level):
        extra_copy(level).wait()
        for piece in range(PIECES):
            main_copy(level, piece).wait()

    def settle(level):
        spread_state(recv_main.at[level], parts_in)
        for c in range(16):
            wide = jnp.concatenate([recv_extra[level, 2 * c : 2 * c + 2, :]] * 4, axis=0)
            recv_wide[:, 128 * c : 128 * c + 128] = wide

        @pl.loop(0, 4)
        def _(step):
            for late in range(4):
                g = step * 4 + late
                at = pl.multiple_of(g * 8, 8)
                slot = inverse_wide[level, pl.ds(at, 8), :]
                extra[pl.ds(at, 8), :] = landed(
                    lambda c: recv_wide[:, 128 * c : 128 * c + 128], slot, extra[pl.ds(at, 8), :]
                )
                first = pl.multiple_of(g * 512, 512)
                for b in range(0, 2):
                    lanes = pl.ds(first + 128 * b, 128)
                    slot_b = jnp.broadcast_to(slot[2 * b : 2 * b + 1], (8, 128))
                    own[:, lanes] = landed(
                        lambda c: recv_main[level, :, 128 * c : 128 * c + 128], slot_b, own[:, lanes]
                    )
                lanes = pl.ds(first + 256, 256)
                slot_row = jnp.concatenate([slot[4:5], slot[6:7]], axis=1)
                fresh = rows_by_matmul(parts_in, slot_row)
                own[:, lanes] = jnp.where(jnp.broadcast_to(slot_row, (8, 256)) >= 0, fresh, own[:, lanes])

    for copy in copies:
        copy.wait()
    extra[pl.ds(0, 64, stride=2), :] = old[...]
    extra[pl.ds(1, 64, stride=2), :] = active[...].astype(F32)
    for number in range(8):
        exports_3[number] = exports[number : number + 1, :]
    gather(0, send_main.at[0])
    pl.semaphore_wait(barrier, 12)

    for level in range(LEVELS):
        send(level)
        if level == 0:
            columns[...] = pair_columns(pairs[...].astype(F32), used[0])
        invert(level)
        if level > 0:
            settle(level - 1)
        if level + 1 < LEVELS:
            compose(level + 1)
            gather(level + 1, base_main)
        else:

            spread_state(own, parts)

            @pl.loop(0, 8)
            def _(number):
                at = pl.multiple_of(number * GHOSTS, GHOSTS)
                for k in range(0, DENSE_X, 256):
                    send_ghost[:, pl.ds(at + k, 256)] = rows_by_matmul(parts, exports_3[number, :, k : k + 256])
                for k in range(0, GHOSTS, 128):
                    index = exports_3[number, :, k : k + 128]
                    slots_x[number, :, k : k + 128] = cells_at(inverse, index)
                    if k >= DENSE_X:
                        send_ghost[:, pl.ds(at + k, 128)] = rows_at(own, index)

        arrive(level)

    @pl.loop(0, 8)
    def _(number):
        for k in range(8):
            lanes = pl.ds(pl.multiple_of(number * GHOSTS, GHOSTS) + 128 * k, 128)
            slot = jnp.broadcast_to(slots_x[number, :, 128 * k : 128 * k + 128], (8, 128))
            send_ghost[:, lanes] = landed(
                lambda n: recv_main[LEVELS - 1, :, 128 * n : 128 * n + 128], slot, send_ghost[:, lanes]
            )
        ghost_copy(number).start()

    settle(LEVELS - 1)
    for number in range(8):
        ghost_copy(number).wait()


HB = pl.BlockSpec(memory_space=pltpu.HBM)


def exchange(mesh, send_count, pair_count, particles, old, active, send_rows, export_rows, pair_tiles):
    count_x, count_y = mesh.shape["gx"], mesh.shape["gy"]
    return pl.pallas_call(
        functools.partial(exchange_kernel, count_x, count_y),
        name="exchange",
        out_shape=(
            jax.ShapeDtypeStruct((8, 8192), F32),
            jax.ShapeDtypeStruct((128, 128), F32),
            jax.ShapeDtypeStruct((8, 8192), F32),
            jax.ShapeDtypeStruct((8, COLS), F32),
            jax.ShapeDtypeStruct((8, 1, GHOSTS), I32),
        ),
        in_specs=[SM, HB, HB, HB, HB, HB, HB, HB],
        out_specs=(VM, VM, VM, VM, VM),
        scratch_shapes=[
            pltpu.SemaphoreType.DMA((7,)),
            pltpu.VMEM((1, 4), I32),
            pltpu.VMEM((64, 128), F32),
            pltpu.VMEM((64, 128), I32),
            pltpu.VMEM((LEVELS, SEND), I32),
            pltpu.VMEM((8, GHOSTS), I32),
            pltpu.VMEM((2, 512), I32),
            pltpu.VMEM((3, 256, 256), BF16),
            pltpu.VMEM((3, SEND // 32, 256), BF16),
            pltpu.VMEM((256, SEND), BF16),
            pltpu.VMEM((64, 128), I32),
            pltpu.VMEM((LEVELS, 128, 128), I32),
            pltpu.VMEM((1, SEND), I32),
            pltpu.VMEM((8, 1, GHOSTS), I32),
            pltpu.VMEM((8, SEND), F32),
            pltpu.VMEM((8, SEND), F32),
            pltpu.VMEM((LEVELS, 8, SEND), F32),
            pltpu.VMEM((LEVELS, 32, 128), F32),
            pltpu.VMEM((LEVELS, 8, SEND), F32),
            pltpu.VMEM((LEVELS, 32, 128), F32),
            pltpu.VMEM((8, SEND), F32),
            pltpu.VMEM((8, 8 * GHOSTS), F32),
            pltpu.SemaphoreType.DMA((LEVELS, PIECES + 1)),
            pltpu.SemaphoreType.DMA((LEVELS, PIECES + 1)),
            pltpu.SemaphoreType.DMA((8,)),
            pltpu.SemaphoreType.DMA((8,)),
        ],
        compiler_params=pltpu.CompilerParams(
            collective_id=0, has_side_effects=True, vmem_limit_bytes=24 << 20
        ),
    )(
        pair_count,
        *[
            pltpu.with_memory_space_constraint(x, pltpu.HBM)
            for x in (send_count, particles, old, active, send_rows, export_rows, pair_tiles)
        ],
    )


def ghost_density_kernel(count_x, count_y, density, exports_3, out, send, send_sems, recv_sems):
    barrier = pltpu.get_barrier_semaphore()
    for number in range(8):
        pl.semaphore_signal(barrier, inc=1, device_id=neighbour(number, 1, count_x, count_y), device_id_type=MESH)

    def copy(number):
        return pltpu.make_async_remote_copy(
            src_ref=send.at[number],
            dst_ref=out.at[number],
            send_sem=send_sems.at[number],
            recv_sem=recv_sems.at[number],
            device_id=neighbour(number, 1, count_x, count_y),
            device_id_type=MESH,
        )

    def gathered(number):
        for k in range(8):
            send[number, k : k + 1, :] = cells_at(density, exports_3[number, :, 128 * k : 128 * k + 128])

    @pl.loop(0, 2)
    def _(half):
        for n in range(4):
            gathered(half * 4 + n)

    pl.semaphore_wait(barrier, 8)
    for number in range(8):
        copy(number).start()

    for number in range(8):
        copy(number).wait()


def ghost_density_step(mesh, density, export_rows):
    return pl.pallas_call(
        functools.partial(ghost_density_kernel, mesh.shape["gx"], mesh.shape["gy"]),
        name="ghost_density",
        out_shape=jax.ShapeDtypeStruct((8, 8, 128), F32),
        in_specs=[VM, VM],
        out_specs=VM,
        scratch_shapes=[
            pltpu.VMEM((8, 8, 128), F32),
            pltpu.SemaphoreType.DMA((8,)),
            pltpu.SemaphoreType.DMA((8,)),
        ],
        compiler_params=pltpu.CompilerParams(collective_id=1, has_side_effects=True, vmem_limit_bytes=8 << 20),
    )(density, export_rows)


def on_device(
    mesh, particles, old_density, active, send_rows, send_count, export_rows, pair_tiles, pair_count
):
    own, extra, ghost, columns, exports = exchange(
        mesh,
        send_count.T,
        pair_count,
        particles,
        old_density.reshape(64, 128),
        active.reshape(64, 128),
        send_rows,
        export_rows,
        pair_tiles,
    )
    result, density, codes, rank = density_step(columns, own, extra, ghost)
    ghost_density = ghost_density_step(mesh, density, exports).reshape(64, 128)
    acceleration, heating = force_step(codes, own, ghost, density, ghost_density, rank)
    return result.reshape(8192), acceleration, heating.reshape(8192)


def solution(mesh):
    in_specs = (
        P(None, ("gx", "gy")),
        P(("gx", "gy")),
        P(("gx", "gy")),
        P(None, ("gx", "gy")),
        P(None, ("gx", "gy")),
        P(None, ("gx", "gy")),
        P(None, ("gx", "gy")),
        P(("gx", "gy")),
    )
    out_specs = (P(("gx", "gy")), P(None, ("gx", "gy")), P(("gx", "gy")))
    return jax.shard_map(
        functools.partial(on_device, mesh), mesh=mesh, in_specs=in_specs, out_specs=out_specs, check_vma=False
    )
```

```python
import functools
import math

import jax
import jax.numpy as jnp
from jax import lax
from jax.experimental import pallas as pl
from jax.experimental.pallas import tpu as pltpu
from jax.sharding import PartitionSpec as P

F32 = jnp.float32
BF16 = jnp.bfloat16
I32 = jnp.int32
MASS = 1.0 / 512.0
NEAR = 1e-30
FAR = 1e36
NT_DIMS = (((1,), (1,)), ((), ()))
COLS = 320
STEPS = 384
WAYS = 8
SPAN = 16
TAIL = 4
FEW = 4


def iota(shape, axis):
    return lax.broadcasted_iota(I32, shape, axis)


def split3(x):
    a = x.astype(BF16)
    r = x - a.astype(F32)
    b = r.astype(BF16)
    c = (r - b.astype(F32)).astype(BF16)
    return a, b, c


def dot(a, b):
    return jnp.dot(a, b, preferred_element_type=F32)


def dot_nt(a, b):
    return lax.dot_general(a, b, NT_DIMS, preferred_element_type=F32)


def swap_halves(x):
    return pltpu.roll(x, 64, x.ndim - 1)


def ranks_of(active):
    rows, cols = iota((128, 128), 0), iota((128, 128), 1)
    before = ((rows // 64 == cols // 64) & (rows < cols)).astype(F32).astype(BF16)
    rank = dot(active.astype(BF16), before)
    return jnp.where(active > 0.5, rank, -1.0)


def tile_groups(active):
    rows, cols = iota((128, 128), 0), iota((128, 128), 1)
    pick = (rows // 64 == cols % 2).astype(F32).astype(BF16)
    count = dot(active.astype(BF16), pick)
    own = iota((64, 128), 0) == iota((64, 128), 1) // 2
    total = jnp.sum(jnp.where(own, count, 0.0), axis=0, keepdims=True)
    return jnp.floor((total + 7.0) * 0.125)


def pair_columns(pairs, used):
    target, source = pairs[0:1], pairs[1:2]
    count = pairs.shape[1]
    target_col = jnp.broadcast_to(target, (8, count)).T[:, 0:1]
    used_row = iota((1, count), 1) < used
    q, p = iota((count, count), 0), iota((count, count), 1)
    same = (target_col == target) & (q < p) & (q < used)
    order = jnp.sum(jnp.where(same, 1.0, 0.0), axis=0, keepdims=True)
    at = (iota((128, count), 0).astype(F32) == target) & used_row
    at_f = jnp.where(at, 1.0, 0.0)
    number = jnp.sum(at_f, axis=1, keepdims=True)
    columns = jnp.floor((number + 1.0) * 0.5)
    below = (iota((128, 128), 0) > iota((128, 128), 1)).astype(F32).astype(BF16)
    first = dot(below, jnp.broadcast_to(columns, (128, 128)).astype(BF16))[:, 0:1]
    first_row = jnp.sum(at_f * first, axis=0, keepdims=True)
    half = jnp.floor(order * 0.5)
    column = first_row + half
    second = jnp.where(order - 2.0 * half > 0.5, 1.0, 0.0)
    use = jnp.where(used_row, 1.0, 0.0)
    lead = use * (1.0 - second)
    trail = use * second
    zero = lead * 0.0
    values = jnp.concatenate(
        [target * lead, source * lead, source * trail, lead, trail, zero, zero, zero], axis=0
    ).astype(BF16)
    match = jnp.where((iota((COLS, count), 0).astype(F32) == column) & used_row, 1.0, 0.0).astype(BF16)
    found = dot_nt(values, match)
    alone = 256.0 * (1.0 - found[4:5])
    return jnp.where(iota(found.shape, 0) == 2, found + alone, found)


def item_codes(in_row, groups):
    tile = jnp.where(iota((128, COLS), 0).astype(F32) == in_row[0:1], 1.0, 0.0).astype(BF16)
    size = dot(jnp.broadcast_to(groups, (8, 128)).astype(BF16), tile) * in_row[3:4]
    upper = (iota((COLS, COLS), 0) < iota((COLS, COLS), 1)).astype(F32).astype(BF16)
    lower = (iota((COLS, COLS), 0) > iota((COLS, COLS), 1)).astype(F32).astype(BF16)
    start_row = dot(size.astype(BF16), upper)[0:1]
    start_col = dot_nt(lower, size.astype(BF16))[:, 0:1]
    total = jnp.sum(size[0:1], axis=1, keepdims=True)
    high = jnp.floor(start_row * (1.0 / 256.0))
    table = jnp.concatenate(
        [in_row[0:3], high, start_row - 256.0 * high, high * 0.0, high * 0.0, high * 0.0], axis=0
    )
    table = jnp.concatenate([table, jnp.zeros((8, 128 * ((COLS + 127) // 128) - COLS), F32)], axis=1)
    before = jnp.where(iota(table.shape, 1) == 0, 0.0, pltpu.roll(table, 1, 1))
    steps = (table - before)[:, 0:COLS].astype(BF16)
    at = iota((1, WAYS * STEPS), 1)
    item = (at % STEPS * WAYS + at // STEPS).astype(F32)
    found = dot(steps, jnp.where(item >= start_col, 1.0, 0.0).astype(BF16))
    beyond = item >= total
    group = item - 256.0 * found[3:4] - found[4:5]
    place = jnp.where(beyond, 0.0, group * 128.0 + found[0:1]).astype(I32)
    first_source = jnp.where(beyond, 256.0, found[1:2]).astype(I32)
    other = jnp.where(beyond, 256.0, found[2:3]).astype(I32)
    codes = place + first_source * 1024 + other * (1 << 19)
    codes = jnp.concatenate([codes[:, STEPS * w : STEPS * w + STEPS] for w in range(WAYS)], axis=0)
    most = jnp.max(groups, axis=1, keepdims=True).astype(I32)
    lane = iota(codes.shape, 1)
    return jnp.where(lane == STEPS - 1, total.astype(I32), jnp.where(lane == STEPS - 2, most, codes))


def put_sources(table, slot, chunk):
    left = iota(chunk.shape, 1) < 64
    other = swap_halves(chunk)
    table[slot] = jnp.where(left, chunk, other)
    table[slot + 1] = jnp.where(left, other, chunk)


def start_of(group):
    return 8.0 * group if isinstance(group, int) else (8 * group).astype(F32)


def put_targets(columns, chunk, fields, rank, groups):
    parts = jnp.concatenate([part.astype(F32) for part in split3(fields)], axis=0)
    parts = jnp.concatenate([parts, jnp.zeros((128 - parts.shape[0], 128), F32)], axis=0).astype(BF16)
    wide = jnp.broadcast_to(rank, (8, 128))
    left = iota((8, 128), 1) < 64
    sub = iota((8, 128), 0).astype(F32)
    ours = jnp.where(left, wide, -1.0), jnp.where(left, -1.0, wide)
    pick = jnp.concatenate(
        [jnp.where(our == sub + start_of(g), 1.0, 0.0) for g in groups for our in ours], axis=0
    ).astype(BF16)
    rows = dot_nt(pick, parts)
    for n, g in enumerate(groups):
        columns[pl.ds(pl.multiple_of(g * 1024 + chunk * 16, 16), 16), :] = rows[16 * n : 16 * n + 16]


def widener(fields, stride):
    k, n = iota((128, 128 * fields), 0), iota((128, 128 * fields), 1)
    return ((k % stride == n // 128) & (k < 3 * stride)).astype(F32).astype(BF16)


def gather_sums(totals, tile, rank, groups):
    left = iota((8, 128), 1) < 64
    wide = jnp.broadcast_to(rank, (8, 128))
    sub = iota((8, 128), 0).astype(F32)
    out = [jnp.zeros((8, 128), F32) for _ in totals]
    for g in groups:
        hit = wide == sub + start_of(g)
        for n, total in enumerate(totals):
            one = jnp.sum(total[pl.ds(pl.multiple_of(g * 1024 + tile * 8, 8), 8), :], axis=1, keepdims=True)
            two = jnp.sum(total[pl.ds(pl.multiple_of(g * 1024 + tile * 8 + 8, 8), 8), :], axis=1, keepdims=True)
            out[n] = out[n] + jnp.where(hit, jnp.where(left, one, two), 0.0)
    return [jnp.sum(o, axis=0, keepdims=True) for o in out]


def wrapped(a, b):
    s = a - b
    return s - jnp.floor(s + 0.5)


def decode(code):
    return code & 1023, (code >> 10) & 511, code >> 19


def density_item(mine, other):
    dx = wrapped(mine[0], other[0:1])
    dy = wrapped(mine[1], other[1:2])
    dz = wrapped(mine[2], other[2:3])
    rsq = jnp.maximum(dx * dx + dy * dy + dz * dz, other[3:4])
    q = rsq * lax.rsqrt(rsq) * mine[3]
    t = jnp.maximum(2.0 - q, 0.0)
    u = jnp.maximum(1.0 - q, 0.0)
    return (t * t * t - 4.0 * (u * u * u),)


def force_item(mine, other):
    dx = wrapped(mine[0], other[0:1])
    dy = wrapped(mine[1], other[1:2])
    dz = wrapped(mine[2], other[2:3])
    rsq = jnp.maximum(dx * dx + dy * dy + dz * dz, other[10:11])
    inv = lax.rsqrt(rsq)
    r = rsq * inv

    def profile(h, hinv):
        q = r * hinv
        t = jnp.maximum(2.0 - q, 0.0)
        return jnp.where(q < 1.0, 4.0 - 3.0 * q, t * t * (h * inv))

    slope = profile(mine[6], mine[8]) * mine[9] + profile(other[6:7], other[8:9]) * other[9:10]
    w = (mine[7] + other[7:8]) * slope
    gap = (mine[3] - other[3:4]) * dx + (mine[4] - other[4:5]) * dy + (mine[5] - other[5:6]) * dz
    return (w * dx, w * dy, w * dz, w * gap)


def for_all_groups(most, body):
    body(range(FEW), False)

    @pl.loop(FEW, jnp.maximum(most, FEW))
    def _(g):
        body([g], True)


def run_items(number, codes, columns, sources, spread, fields, item, totals):
    def steps(first, count):
        for late in range(0, count, 2):
            places = [decode(codes[way, first + late + n]) for n in range(2) for way in range(WAYS)]
            rows = [pl.multiple_of(place * 8, 8) for place, _, _ in places]
            mine = jnp.concatenate([columns[pl.ds(row, 8), :] for row in rows], axis=0).astype(BF16)
            wide = dot(mine, spread[...])
            for n, (_, one, two) in enumerate(places):
                first_tile, second_tile = sources[one], sources[two]
                other = jnp.where(iota(first_tile.shape, 1) < 64, first_tile, second_tile)
                own = [wide[8 * n : 8 * n + 8, 128 * f : 128 * f + 128] for f in range(fields)]
                for total, term in zip(totals, item(own, other)):
                    total[pl.ds(rows[n], 8), :] += term

    spans = number // (SPAN * WAYS)

    @pl.loop(0, spans)
    def _(span):
        steps(SPAN * span, SPAN)

    rest = number - spans * (SPAN * WAYS)

    @pl.loop(0, (rest + TAIL * WAYS - 1) // (TAIL * WAYS))
    def _(tail):
        steps(SPAN * spans + TAIL * tail, TAIL)


def density_kernel(cols_ref, own_ref, extra_ref, ghost_ref, result_ref, dens_ref, code_ref, rank_ref,
                   sources, columns, spread, total, sums, smooth, codes_s, sem):
    active = extra_ref[pl.ds(1, 64, stride=2), :]
    spread[...] = widener(4, 8)
    rank_ref[...] = ranks_of(active)
    code_ref[...] = item_codes(cols_ref[...], tile_groups(active))
    copy = pltpu.make_async_copy(code_ref, codes_s, sem)
    copy.start()

    def fields(block):
        sub = iota((8, 128), 0)
        return jnp.where(sub < 3, block, jnp.where(sub == 3, NEAR, 0.0))

    def targets(block):
        sub = iota((8, 128), 0)
        return jnp.where(sub < 3, block, jnp.where(sub == 3, 1.0 / block[6:7], 0.0))

    @pl.loop(0, 16)
    def _(step):
        for part in range(4):
            chunk = step * 4 + part
            lanes = pl.ds(pl.multiple_of(step * 512, 512) + 128 * part, 128)
            block = own_ref[:, lanes]
            smooth[pl.ds(chunk, 1), :] = block[6:7]
            put_sources(sources, chunk * 2, fields(block))
            put_sources(sources, chunk * 2 + 128, fields(ghost_ref[:, lanes]))

    sources[256] = jnp.where(iota((8, 128), 0) == 3, FAR, 0.0)
    copy.wait()
    number, most = codes_s[0, STEPS - 1], codes_s[0, STEPS - 2]

    def prepare(groups, again):
        per = 16 if again else 4

        @pl.loop(0, 64 // per)
        def _(step):
            for part in range(per):
                chunk = step * per + part
                lanes = pl.ds(pl.multiple_of(step * (128 * per), 128 * per) + 128 * part, 128)
                put_targets(columns, chunk, targets(own_ref[:, lanes]), rank_ref[pl.ds(chunk, 1), :], groups)
                for g in groups:
                    total[pl.ds(pl.multiple_of(g * 1024 + chunk * 16, 16), 16), :] = jnp.zeros((16, 128), F32)

    for_all_groups(most, prepare)

    run_items(number, codes_s, columns, sources, spread, 4, density_item, (total,))

    def collect(groups, again):
        per = 16 if again else 4

        @pl.loop(0, 64 // per)
        def _(step):
            for part in range(per):
                chunk = step * per + part
                (got,) = gather_sums([total], chunk * 2, rank_ref[pl.ds(chunk, 1), :], groups)
                at = pl.ds(chunk, 1)
                sums[at, :] = sums[at, :] + got if again else got

    for_all_groups(most, collect)
    h = smooth[...]
    fresh = MASS / math.pi / (h * h * h) * (1.0 + 0.25 * sums[...])
    fresh = jnp.where(rank_ref[...] >= 0.0, fresh, extra_ref[pl.ds(0, 64, stride=2), :])
    dens_ref[...] = fresh
    result_ref[...] = fresh


def force_kernel(code_ref, own_ref, ghost_ref, dens_ref, gdens_ref, rank_ref, acc_ref, heat_ref,
                 sources, columns, spread, ax, ay, az, heat):
    number, most = code_ref[0, STEPS - 1], code_ref[0, STEPS - 2]
    spread[...] = widener(10, 16)

    def fields(block, density):
        h = block[6:7]
        press = (5.0 / 3.0 - 1.0) * block[7:8] / density
        hinv = 1.0 / h
        scale = (0.375 * MASS / math.pi) / (h * h * h * h * h)
        near = jnp.full((1, 128), NEAR, F32)
        return jnp.concatenate([block[0:7], press, hinv, scale, near, jnp.zeros((5, 128), F32)], axis=0)

    def own_fields(step, part, per):
        lanes = pl.ds(pl.multiple_of(step * (128 * per), 128 * per) + 128 * part, 128)
        return fields(own_ref[:, lanes], dens_ref[pl.ds(step * per + part, 1), :])

    @pl.loop(0, 16)
    def _(step):
        for part in range(4):
            chunk = step * 4 + part
            lanes = pl.ds(pl.multiple_of(step * 512, 512) + 128 * part, 128)
            put_sources(sources, chunk * 2, own_fields(step, part, 4))
            put_sources(sources, chunk * 2 + 128, fields(ghost_ref[:, lanes], gdens_ref[pl.ds(chunk, 1), :]))

    def prepare(groups, again):
        per = 16 if again else 4

        @pl.loop(0, 64 // per)
        def _(step):
            for part in range(per):
                chunk = step * per + part
                put_targets(columns, chunk, own_fields(step, part, per), rank_ref[pl.ds(chunk, 1), :], groups)
                for g in groups:
                    for total in (ax, ay, az, heat):
                        total[pl.ds(pl.multiple_of(g * 1024 + chunk * 16, 16), 16), :] = jnp.zeros((16, 128), F32)

    for_all_groups(most, prepare)
    sub = iota((16, 128), 0)
    sources[256] = jnp.where(sub == 10, FAR, jnp.where((sub == 6) | (sub == 8), 1.0, 0.0))

    run_items(number, code_ref, columns, sources, spread, 10, force_item, (ax, ay, az, heat))

    def collect(groups, again):
        per = 16 if again else 4

        @pl.loop(0, 64 // per)
        def _(step):
            for part in range(per):
                chunk = step * per + part
                got = gather_sums([ax, ay, az, heat], chunk * 2, rank_ref[pl.ds(chunk, 1), :], groups)
                lanes = pl.ds(pl.multiple_of(step * (128 * per), 128 * per) + 128 * part, 128)
                at = pl.ds(chunk, 1)
                for n in range(3):
                    acc_ref[n : n + 1, lanes] = acc_ref[n : n + 1, lanes] + got[n] if again else got[n]
                heat_ref[at, :] = heat_ref[at, :] - 0.5 * got[3] if again else -0.5 * got[3]

    for_all_groups(most, collect)


VM = pl.BlockSpec(memory_space=pltpu.VMEM)
SM = pl.BlockSpec(memory_space=pltpu.SMEM)


def density_step(columns, own, extra, ghost):
    return pl.pallas_call(
        density_kernel,
        name="density",
        out_shape=(
            jax.ShapeDtypeStruct((64, 128), F32),
            jax.ShapeDtypeStruct((64, 128), F32),
            jax.ShapeDtypeStruct((WAYS, STEPS), I32),
            jax.ShapeDtypeStruct((64, 128), F32),
        ),
        in_specs=[VM, VM, VM, VM],
        out_specs=(VM, VM, VM, VM),
        scratch_shapes=[
            pltpu.VMEM((257, 8, 128), F32),
            pltpu.VMEM((8192, 128), F32),
            pltpu.VMEM((128, 512), BF16),
            pltpu.VMEM((8192, 128), F32),
            pltpu.VMEM((64, 128), F32),
            pltpu.VMEM((64, 128), F32),
            pltpu.SMEM((WAYS, STEPS), I32),
            pltpu.SemaphoreType.DMA,
        ],
        compiler_params=pltpu.CompilerParams(vmem_limit_bytes=24 << 20),
    )(columns, own, extra, ghost)


def force_step(codes, own, ghost, density, ghost_density, rank):
    return pl.pallas_call(
        force_kernel,
        name="force",
        out_shape=(jax.ShapeDtypeStruct((3, 8192), F32), jax.ShapeDtypeStruct((64, 128), F32)),
        in_specs=[SM, VM, VM, VM, VM, VM],
        out_specs=(VM, VM),
        scratch_shapes=[pltpu.VMEM((257, 16, 128), F32), pltpu.VMEM((8192, 128), F32), pltpu.VMEM((128, 1280), BF16)]
        + [pltpu.VMEM((8192, 128), F32)] * 4,
        compiler_params=pltpu.CompilerParams(vmem_limit_bytes=40 << 20),
    )(codes, own, ghost, density, ghost_density, rank)


LEVELS = 4
SEND = 2048
PIECE = 512
BLOCK = 1024
DENSE = 512
DENSE_X = 512
PIECES = SEND // PIECE
GHOSTS = 1024
MESH = pl.DeviceIdType.MESH


def flipped(index, bit):
    step = 1 << bit
    return index + step - 2 * step * ((index // step) % 2)


def neighbour(number, sign, count_x, count_y):
    cell = number + number // 4
    i = (lax.axis_index("gx") + sign * (cell // 3 - 1) + count_x) % count_x
    j = (lax.axis_index("gy") + sign * (cell % 3 - 1) + count_y) % count_y
    return i, j


def spread_state(own, parts):
    for h in range(0, own.shape[1] // 256, 2):
        pair = jnp.concatenate([own[:, h * 256 : h * 256 + 256], own[:, h * 256 + 256 : h * 256 + 512]], axis=0)
        for n, part in enumerate(split3(pair)):
            parts[n, h * 8 : h * 8 + 16, :] = part


def permuted(value, lanes):
    return jnp.take_along_axis(value, lanes, axis=1, mode="promise_in_bounds")


def one_hot(index_row):
    low = jnp.bitwise_and(index_row, 255)
    return jnp.where(iota((256, index_row.shape[1]), 0) == low, 1.0, 0.0).astype(BF16)


def chosen(read, bits, first, count):
    if count == 1:
        return read(first)
    half = count // 2
    low = chosen(read, bits, first, half)
    high = chosen(read, bits, first + half, half)
    return jnp.where(bits[half.bit_length() - 1], high, low)


def digits_of(value, count):
    return [jnp.bitwise_and(value, 1 << n) != 0 for n in range(count)]


def rows_at(state, index):
    index = jnp.broadcast_to(index, (8, 128))
    low = jnp.bitwise_and(index, 127)
    return chosen(lambda c: permuted(state[:, 128 * c : 128 * c + 128], low), digits_of(index >> 7, 6), 0, 64)


def rows_by_matmul(parts, index):
    blocks = parts.shape[1] // 8
    hot = one_hot(index)
    found = dot(parts[2], hot) + dot(parts[1], hot) + dot(parts[0], hot)
    bits = digits_of(jnp.broadcast_to(index, (8, 256)) >> 8, blocks.bit_length() - 1)
    return chosen(lambda h: found[8 * h : 8 * h + 8], bits, 0, blocks)


def pairs_at(extra, index, groups):
    index = jnp.broadcast_to(index, (8, 128))
    low = jnp.bitwise_and(index, 127)
    bits = digits_of(index >> 9, groups.bit_length() - 1)
    out = chosen(lambda g: permuted(extra[8 * g : 8 * g + 8, :], low), bits, 0, groups)
    out = jnp.where(iota((8, 128), 0) >> 1 == jnp.bitwise_and(index >> 7, 3), out, 0.0)
    out = out + pltpu.roll(out, 4, 0)
    return out + pltpu.roll(out, 2, 0)


def cells_at(table, index):
    index = jnp.broadcast_to(index, (8, 128))
    low, high = jnp.bitwise_and(index, 127), (index >> 7) - iota((8, 128), 0)
    out = jnp.zeros((8, 128), table.dtype)
    for v in range(8):
        out = jnp.where(high == 8 * v, permuted(table[8 * v : 8 * v + 8, :], low), out)
    return jnp.sum(out, axis=0, keepdims=True)


def landed(read, slot, old):
    low = jnp.bitwise_and(slot, 127)
    new = chosen(lambda c: permuted(read(c), low), digits_of(slot >> 7, 4), 0, 16)
    return jnp.where(slot >= 0, new, old)


def exchange_kernel(count_x, count_y, used, counts_h, particles_h, old_h, active_h, rows_h, exports_h, pairs_h,
                    own, extra, ghost, columns, exports_3,
                    loads, counts, old, active, rows, exports, pairs, parts, parts_in, hot, inverse, inverse_wide, slots, slots_x, base_main, base_extra,
                    send_main, send_extra, recv_main, recv_extra, recv_wide,
                    send_ghost, send_sems, recv_sems, ghost_send, ghost_recv):
    i, j = lax.axis_index("gx"), lax.axis_index("gy")
    bits_x, bits_y = count_x.bit_length() - 1, count_y.bit_length() - 1
    partners = [
        (flipped(i, bits_x - 1), j),
        (flipped(i, bits_x - 2), j),
        (i, flipped(j, bits_y - 1)),
        (i, flipped(j, bits_y - 2)),
    ]
    copies = [
        pltpu.make_async_copy(source, target, loads.at[n])
        for n, (source, target) in enumerate(
            ((rows_h, rows), (counts_h, counts), (particles_h, own), (old_h, old), (active_h, active), (exports_h, exports), (pairs_h, pairs))
        )
    ]
    for copy in copies:
        copy.start()
    barrier = pltpu.get_barrier_semaphore()
    for partner in partners:
        pl.semaphore_signal(barrier, inc=1, device_id=partner, device_id_type=MESH)
    for number in range(8):
        pl.semaphore_signal(barrier, inc=1, device_id=neighbour(number, 1, count_x, count_y), device_id_type=MESH)

    def invert(level):
        slot = iota((32, SEND), 1)
        index = rows[level : level + 1, :]
        high = jnp.where(slot < counts[0:1, level : level + 1], jnp.broadcast_to(index >> 8, (32, SEND)), 64)
        here = iota((32, SEND), 0) == high
        digits = jnp.concatenate(
            [
                jnp.where(here, ((slot >> 7) + 1).astype(F32), 0.0),
                jnp.where(here, jnp.bitwise_and(slot, 127).astype(F32), 0.0),
            ],
            axis=0,
        ).astype(BF16)
        for piece in range(PIECES):
            hot[:, piece * PIECE : piece * PIECE + PIECE] = one_hot(index[:, piece * PIECE : piece * PIECE + PIECE])
        found = dot_nt(digits, hot[...])
        found = (128.0 * (found[0:32] - 1.0) + found[32:64]).astype(I32)
        for part in range(2):
            value = found[:, 128 * part : 128 * part + 128]
            inverse[pl.ds(part, 32, stride=2), :] = value
            for field in range(2):
                inverse_wide[level, pl.ds(2 * part + field, 32, stride=4), :] = value

    def main_copy(level, piece):
        lanes = pl.ds(pl.multiple_of(piece * PIECE, PIECE), PIECE)
        return pltpu.make_async_remote_copy(
            src_ref=send_main.at[level, :, lanes],
            dst_ref=recv_main.at[level, :, lanes],
            send_sem=send_sems.at[level, piece],
            recv_sem=recv_sems.at[level, piece],
            device_id=partners[level],
            device_id_type=MESH,
        )

    def extra_copy(level):
        return pltpu.make_async_remote_copy(
            src_ref=send_extra.at[level],
            dst_ref=recv_extra.at[level],
            send_sem=send_sems.at[level, PIECES],
            recv_sem=recv_sems.at[level, PIECES],
            device_id=partners[level],
            device_id_type=MESH,
        )

    def ghost_copy(number):
        lanes = pl.ds(pl.multiple_of(number * GHOSTS, GHOSTS), GHOSTS)
        return pltpu.make_async_remote_copy(
            src_ref=send_ghost.at[:, lanes],
            dst_ref=ghost.at[:, lanes],
            send_sem=ghost_send.at[number],
            recv_sem=ghost_recv.at[number],
            device_id=neighbour(number, 1, count_x, count_y),
            device_id_type=MESH,
        )

    def gather(level, out):
        spread_state(own, parts)

        @pl.loop(0, SEND // BLOCK)
        def _(block):
            at = pl.multiple_of(block * BLOCK, BLOCK)
            for k in range(0, DENSE, 256):
                out[:, pl.ds(at + k, 256)] = rows_by_matmul(parts, rows[level : level + 1, pl.ds(at + k, 256)])
            for k in range(0, BLOCK, 128):
                index = rows[level : level + 1, pl.ds(at + k, 128)]
                base_extra[:, pl.ds(at + k, 128)] = pairs_at(extra, index, 16)
                if k >= DENSE:
                    out[:, pl.ds(at + k, 128)] = rows_at(own, index)

    def compose(level):
        @pl.loop(0, PIECES)
        def _(piece):
            for k in range(PIECE // 128):
                at = pl.multiple_of(piece * PIECE + 128 * k, 128)
                slots[:, pl.ds(at, 128)] = cells_at(inverse, rows[level : level + 1, pl.ds(at, 128)])

    def send(level):
        for piece in range(PIECES):
            for k in range(PIECE // 128):
                c = piece * (PIECE // 128) + k
                lanes = slice(128 * c, 128 * c + 128)
                both = base_extra[:, lanes]
                if level > 0:
                    slot = jnp.broadcast_to(slots[:, lanes], (8, 128))
                    send_main[level, :, lanes] = landed(
                        lambda n: recv_main[level - 1, :, 128 * n : 128 * n + 128], slot, base_main[:, lanes]
                    )
                    fresh = pairs_at(recv_extra.at[level - 1], jnp.maximum(slots[:, lanes], 0), 4)
                    both = jnp.where(slot >= 0, fresh, both)
                send_extra[level, 2 * c : 2 * c + 2, :] = both[0:2]
            main_copy(level, piece).start()
        extra_copy(level).start()

    def arrive(level):
        extra_copy(level).wait()
        for piece in range(PIECES):
            main_copy(level, piece).wait()

    def settle(level):
        spread_state(recv_main.at[level], parts_in)
        for c in range(16):
            wide = jnp.concatenate([recv_extra[level, 2 * c : 2 * c + 2, :]] * 4, axis=0)
            recv_wide[:, 128 * c : 128 * c + 128] = wide

        @pl.loop(0, 4)
        def _(step):
            for late in range(4):
                g = step * 4 + late
                at = pl.multiple_of(g * 8, 8)
                slot = inverse_wide[level, pl.ds(at, 8), :]
                extra[pl.ds(at, 8), :] = landed(
                    lambda c: recv_wide[:, 128 * c : 128 * c + 128], slot, extra[pl.ds(at, 8), :]
                )
                first = pl.multiple_of(g * 512, 512)
                for b in range(0, 2):
                    lanes = pl.ds(first + 128 * b, 128)
                    slot_b = jnp.broadcast_to(slot[2 * b : 2 * b + 1], (8, 128))
                    own[:, lanes] = landed(
                        lambda c: recv_main[level, :, 128 * c : 128 * c + 128], slot_b, own[:, lanes]
                    )
                lanes = pl.ds(first + 256, 256)
                slot_row = jnp.concatenate([slot[4:5], slot[6:7]], axis=1)
                fresh = rows_by_matmul(parts_in, slot_row)
                own[:, lanes] = jnp.where(jnp.broadcast_to(slot_row, (8, 256)) >= 0, fresh, own[:, lanes])

    for copy in copies:
        copy.wait()
    extra[pl.ds(0, 64, stride=2), :] = old[...]
    extra[pl.ds(1, 64, stride=2), :] = active[...].astype(F32)
    for number in range(8):
        exports_3[number] = exports[number : number + 1, :]
    gather(0, send_main.at[0])
    pl.semaphore_wait(barrier, 12)

    for level in range(LEVELS):
        send(level)
        if level == 0:
            columns[...] = pair_columns(pairs[...].astype(F32), used[0])
        invert(level)
        if level > 0:
            settle(level - 1)
        if level + 1 < LEVELS:
            compose(level + 1)
            gather(level + 1, base_main)
        else:

            spread_state(own, parts)

            @pl.loop(0, 8)
            def _(number):
                at = pl.multiple_of(number * GHOSTS, GHOSTS)
                for k in range(0, DENSE_X, 256):
                    send_ghost[:, pl.ds(at + k, 256)] = rows_by_matmul(parts, exports_3[number, :, k : k + 256])
                for k in range(0, GHOSTS, 128):
                    index = exports_3[number, :, k : k + 128]
                    slots_x[number, :, k : k + 128] = cells_at(inverse, index)
                    if k >= DENSE_X:
                        send_ghost[:, pl.ds(at + k, 128)] = rows_at(own, index)

        arrive(level)

    @pl.loop(0, 8)
    def _(number):
        for k in range(8):
            lanes = pl.ds(pl.multiple_of(number * GHOSTS, GHOSTS) + 128 * k, 128)
            slot = jnp.broadcast_to(slots_x[number, :, 128 * k : 128 * k + 128], (8, 128))
            send_ghost[:, lanes] = landed(
                lambda n: recv_main[LEVELS - 1, :, 128 * n : 128 * n + 128], slot, send_ghost[:, lanes]
            )
        ghost_copy(number).start()

    settle(LEVELS - 1)
    for number in range(8):
        ghost_copy(number).wait()


HB = pl.BlockSpec(memory_space=pltpu.HBM)


def exchange(mesh, send_count, pair_count, particles, old, active, send_rows, export_rows, pair_tiles):
    count_x, count_y = mesh.shape["gx"], mesh.shape["gy"]
    return pl.pallas_call(
        functools.partial(exchange_kernel, count_x, count_y),
        name="exchange",
        out_shape=(
            jax.ShapeDtypeStruct((8, 8192), F32),
            jax.ShapeDtypeStruct((128, 128), F32),
            jax.ShapeDtypeStruct((8, 8192), F32),
            jax.ShapeDtypeStruct((8, COLS), F32),
            jax.ShapeDtypeStruct((8, 1, GHOSTS), I32),
        ),
        in_specs=[SM, HB, HB, HB, HB, HB, HB, HB],
        out_specs=(VM, VM, VM, VM, VM),
        scratch_shapes=[
            pltpu.SemaphoreType.DMA((7,)),
            pltpu.VMEM((1, 4), I32),
            pltpu.VMEM((64, 128), F32),
            pltpu.VMEM((64, 128), I32),
            pltpu.VMEM((LEVELS, SEND), I32),
            pltpu.VMEM((8, GHOSTS), I32),
            pltpu.VMEM((2, 512), I32),
            pltpu.VMEM((3, 256, 256), BF16),
            pltpu.VMEM((3, SEND // 32, 256), BF16),
            pltpu.VMEM((256, SEND), BF16),
            pltpu.VMEM((64, 128), I32),
            pltpu.VMEM((LEVELS, 128, 128), I32),
            pltpu.VMEM((1, SEND), I32),
            pltpu.VMEM((8, 1, GHOSTS), I32),
            pltpu.VMEM((8, SEND), F32),
            pltpu.VMEM((8, SEND), F32),
            pltpu.VMEM((LEVELS, 8, SEND), F32),
            pltpu.VMEM((LEVELS, 32, 128), F32),
            pltpu.VMEM((LEVELS, 8, SEND), F32),
            pltpu.VMEM((LEVELS, 32, 128), F32),
            pltpu.VMEM((8, SEND), F32),
            pltpu.VMEM((8, 8 * GHOSTS), F32),
            pltpu.SemaphoreType.DMA((LEVELS, PIECES + 1)),
            pltpu.SemaphoreType.DMA((LEVELS, PIECES + 1)),
            pltpu.SemaphoreType.DMA((8,)),
            pltpu.SemaphoreType.DMA((8,)),
        ],
        compiler_params=pltpu.CompilerParams(
            collective_id=0, has_side_effects=True, vmem_limit_bytes=24 << 20
        ),
    )(
        pair_count,
        *[
            pltpu.with_memory_space_constraint(x, pltpu.HBM)
            for x in (send_count, particles, old, active, send_rows, export_rows, pair_tiles)
        ],
    )


def ghost_density_kernel(count_x, count_y, density, exports_3, out, send, send_sems, recv_sems):
    barrier = pltpu.get_barrier_semaphore()
    for number in range(8):
        pl.semaphore_signal(barrier, inc=1, device_id=neighbour(number, 1, count_x, count_y), device_id_type=MESH)

    def copy(number):
        return pltpu.make_async_remote_copy(
            src_ref=send.at[number],
            dst_ref=out.at[number],
            send_sem=send_sems.at[number],
            recv_sem=recv_sems.at[number],
            device_id=neighbour(number, 1, count_x, count_y),
            device_id_type=MESH,
        )

    def gathered(number):
        for k in range(8):
            send[number, k : k + 1, :] = cells_at(density, exports_3[number, :, 128 * k : 128 * k + 128])

    @pl.loop(0, 2)
    def _(half):
        for n in range(4):
            gathered(half * 4 + n)

    pl.semaphore_wait(barrier, 8)
    for number in range(8):
        copy(number).start()

    for number in range(8):
        copy(number).wait()


def ghost_density_step(mesh, density, export_rows):
    return pl.pallas_call(
        functools.partial(ghost_density_kernel, mesh.shape["gx"], mesh.shape["gy"]),
        name="ghost_density",
        out_shape=jax.ShapeDtypeStruct((8, 8, 128), F32),
        in_specs=[VM, VM],
        out_specs=VM,
        scratch_shapes=[
            pltpu.VMEM((8, 8, 128), F32),
            pltpu.SemaphoreType.DMA((8,)),
            pltpu.SemaphoreType.DMA((8,)),
        ],
        compiler_params=pltpu.CompilerParams(collective_id=1, has_side_effects=True, vmem_limit_bytes=8 << 20),
    )(density, export_rows)


def on_device(
    mesh, particles, old_density, active, send_rows, send_count, export_rows, pair_tiles, pair_count
):
    own, extra, ghost, columns, exports = exchange(
        mesh,
        send_count.T,
        pair_count,
        particles,
        old_density.reshape(64, 128),
        active.reshape(64, 128),
        send_rows,
        export_rows,
        pair_tiles,
    )
    result, density, codes, rank = density_step(columns, own, extra, ghost)
    ghost_density = ghost_density_step(mesh, density, exports).reshape(64, 128)
    acceleration, heating = force_step(codes, own, ghost, density, ghost_density, rank)
    return result.reshape(8192), acceleration, heating.reshape(8192)


def solution(mesh):
    in_specs = (
        P(None, ("gx", "gy")),
        P(("gx", "gy")),
        P(("gx", "gy")),
        P(None, ("gx", "gy")),
        P(None, ("gx", "gy")),
        P(None, ("gx", "gy")),
        P(None, ("gx", "gy")),
        P(("gx", "gy")),
    )
    out_specs = (P(("gx", "gy")), P(None, ("gx", "gy")), P(("gx", "gy")))
    return jax.shard_map(
        functools.partial(on_device, mesh), mesh=mesh, in_specs=in_specs, out_specs=out_specs, check_vma=False
    )
```

```python
import functools
import math

import jax
import jax.numpy as jnp
from jax import lax
from jax.experimental import pallas as pl
from jax.experimental.pallas import tpu as pltpu
from jax.sharding import PartitionSpec as P

F32 = jnp.float32
BF16 = jnp.bfloat16
I32 = jnp.int32
MASS = 1.0 / 512.0
NEAR = 1e-30
FAR = 1e36
NT_DIMS = (((1,), (1,)), ((), ()))
COLS = 320
STEPS = 384
WAYS = 8
SPAN = 16
TAIL = 4
FEW = 4


def iota(shape, axis):
    return lax.broadcasted_iota(I32, shape, axis)


def split3(x):
    a = x.astype(BF16)
    r = x - a.astype(F32)
    b = r.astype(BF16)
    c = (r - b.astype(F32)).astype(BF16)
    return a, b, c


def dot(a, b):
    return jnp.dot(a, b, preferred_element_type=F32)


def dot_nt(a, b):
    return lax.dot_general(a, b, NT_DIMS, preferred_element_type=F32)


def swap_halves(x):
    return pltpu.roll(x, 64, x.ndim - 1)


def ranks_of(active):
    rows, cols = iota((128, 128), 0), iota((128, 128), 1)
    before = ((rows // 64 == cols // 64) & (rows < cols)).astype(F32).astype(BF16)
    rank = dot(active.astype(BF16), before)
    return jnp.where(active > 0.5, rank, -1.0)


def tile_groups(active):
    rows, cols = iota((128, 128), 0), iota((128, 128), 1)
    pick = (rows // 64 == cols % 2).astype(F32).astype(BF16)
    count = dot(active.astype(BF16), pick)
    own = iota((64, 128), 0) == iota((64, 128), 1) // 2
    total = jnp.sum(jnp.where(own, count, 0.0), axis=0, keepdims=True)
    return jnp.floor((total + 7.0) * 0.125)


def pair_columns(pairs, used):
    target, source = pairs[0:1], pairs[1:2]
    count = pairs.shape[1]
    target_col = jnp.broadcast_to(target, (8, count)).T[:, 0:1]
    used_row = iota((1, count), 1) < used
    q, p = iota((count, count), 0), iota((count, count), 1)
    same = (target_col == target) & (q < p) & (q < used)
    order = jnp.sum(jnp.where(same, 1.0, 0.0), axis=0, keepdims=True)
    at = (iota((128, count), 0).astype(F32) == target) & used_row
    at_f = jnp.where(at, 1.0, 0.0)
    number = jnp.sum(at_f, axis=1, keepdims=True)
    columns = jnp.floor((number + 1.0) * 0.5)
    below = (iota((128, 128), 0) > iota((128, 128), 1)).astype(F32).astype(BF16)
    first = dot(below, jnp.broadcast_to(columns, (128, 128)).astype(BF16))[:, 0:1]
    first_row = jnp.sum(at_f * first, axis=0, keepdims=True)
    half = jnp.floor(order * 0.5)
    column = first_row + half
    second = jnp.where(order - 2.0 * half > 0.5, 1.0, 0.0)
    use = jnp.where(used_row, 1.0, 0.0)
    lead = use * (1.0 - second)
    trail = use * second
    zero = lead * 0.0
    values = jnp.concatenate(
        [target * lead, source * lead, source * trail, lead, trail, zero, zero, zero], axis=0
    ).astype(BF16)
    match = jnp.where((iota((COLS, count), 0).astype(F32) == column) & used_row, 1.0, 0.0).astype(BF16)
    found = dot_nt(values, match)
    alone = 256.0 * (1.0 - found[4:5])
    return jnp.where(iota(found.shape, 0) == 2, found + alone, found)


def item_codes(in_row, groups):
    tile = jnp.where(iota((128, COLS), 0).astype(F32) == in_row[0:1], 1.0, 0.0).astype(BF16)
    size = dot(jnp.broadcast_to(groups, (8, 128)).astype(BF16), tile) * in_row[3:4]
    upper = (iota((COLS, COLS), 0) < iota((COLS, COLS), 1)).astype(F32).astype(BF16)
    lower = (iota((COLS, COLS), 0) > iota((COLS, COLS), 1)).astype(F32).astype(BF16)
    start_row = dot(size.astype(BF16), upper)[0:1]
    start_col = dot_nt(lower, size.astype(BF16))[:, 0:1]
    total = jnp.sum(size[0:1], axis=1, keepdims=True)
    high = jnp.floor(start_row * (1.0 / 256.0))
    table = jnp.concatenate(
        [in_row[0:3], high, start_row - 256.0 * high, high * 0.0, high * 0.0, high * 0.0], axis=0
    )
    table = jnp.concatenate([table, jnp.zeros((8, 128 * ((COLS + 127) // 128) - COLS), F32)], axis=1)
    before = jnp.where(iota(table.shape, 1) == 0, 0.0, pltpu.roll(table, 1, 1))
    steps = (table - before)[:, 0:COLS].astype(BF16)
    at = iota((1, WAYS * STEPS), 1)
    item = (at % STEPS * WAYS + at // STEPS).astype(F32)
    found = dot(steps, jnp.where(item >= start_col, 1.0, 0.0).astype(BF16))
    beyond = item >= total
    group = item - 256.0 * found[3:4] - found[4:5]
    place = jnp.where(beyond, 0.0, group * 128.0 + found[0:1]).astype(I32)
    first_source = jnp.where(beyond, 256.0, found[1:2]).astype(I32)
    other = jnp.where(beyond, 256.0, found[2:3]).astype(I32)
    codes = place + first_source * 1024 + other * (1 << 19)
    codes = jnp.concatenate([codes[:, STEPS * w : STEPS * w + STEPS] for w in range(WAYS)], axis=0)
    most = jnp.max(groups, axis=1, keepdims=True).astype(I32)
    lane = iota(codes.shape, 1)
    return jnp.where(lane == STEPS - 1, total.astype(I32), jnp.where(lane == STEPS - 2, most, codes))


def put_sources(table, slot, chunk):
    left = iota(chunk.shape, 1) < 64
    other = swap_halves(chunk)
    table[slot] = jnp.where(left, chunk, other)
    table[slot + 1] = jnp.where(left, other, chunk)


def start_of(group):
    return 8.0 * group if isinstance(group, int) else (8 * group).astype(F32)


def put_targets(columns, chunk, fields, rank, groups):
    parts = jnp.concatenate([part.astype(F32) for part in split3(fields)], axis=0)
    parts = jnp.concatenate([parts, jnp.zeros((128 - parts.shape[0], 128), F32)], axis=0).astype(BF16)
    wide = jnp.broadcast_to(rank, (8, 128))
    left = iota((8, 128), 1) < 64
    sub = iota((8, 128), 0).astype(F32)
    ours = jnp.where(left, wide, -1.0), jnp.where(left, -1.0, wide)
    pick = jnp.concatenate(
        [jnp.where(our == sub + start_of(g), 1.0, 0.0) for g in groups for our in ours], axis=0
    ).astype(BF16)
    rows = dot_nt(pick, parts)
    for n, g in enumerate(groups):
        columns[pl.ds(pl.multiple_of(g * 1024 + chunk * 16, 16), 16), :] = rows[16 * n : 16 * n + 16]


def widener(fields, stride):
    k, n = iota((128, 128 * fields), 0), iota((128, 128 * fields), 1)
    return ((k % stride == n // 128) & (k < 3 * stride)).astype(F32).astype(BF16)


def gather_sums(totals, tile, rank, groups):
    left = iota((8, 128), 1) < 64
    wide = jnp.broadcast_to(rank, (8, 128))
    sub = iota((8, 128), 0).astype(F32)
    out = [jnp.zeros((8, 128), F32) for _ in totals]
    for g in groups:
        hit = wide == sub + start_of(g)
        for n, total in enumerate(totals):
            one = jnp.sum(total[pl.ds(pl.multiple_of(g * 1024 + tile * 8, 8), 8), :], axis=1, keepdims=True)
            two = jnp.sum(total[pl.ds(pl.multiple_of(g * 1024 + tile * 8 + 8, 8), 8), :], axis=1, keepdims=True)
            out[n] = out[n] + jnp.where(hit, jnp.where(left, one, two), 0.0)
    return [jnp.sum(o, axis=0, keepdims=True) for o in out]


def wrapped(a, b):
    s = a - b
    return s - jnp.floor(s + 0.5)


def decode(code):
    return code & 1023, (code >> 10) & 511, code >> 19


def density_item(mine, other):
    dx = wrapped(mine[0], other[0:1])
    dy = wrapped(mine[1], other[1:2])
    dz = wrapped(mine[2], other[2:3])
    rsq = jnp.maximum(dx * dx + dy * dy + dz * dz, other[3:4])
    q = rsq * lax.rsqrt(rsq) * mine[3]
    t = jnp.maximum(2.0 - q, 0.0)
    u = jnp.maximum(1.0 - q, 0.0)
    return (t * t * t - 4.0 * (u * u * u),)


def force_item(mine, other):
    dx = wrapped(mine[0], other[0:1])
    dy = wrapped(mine[1], other[1:2])
    dz = wrapped(mine[2], other[2:3])
    rsq = jnp.maximum(dx * dx + dy * dy + dz * dz, other[10:11])
    inv = lax.rsqrt(rsq)
    r = rsq * inv

    def profile(h, hinv):
        q = r * hinv
        t = jnp.maximum(2.0 - q, 0.0)
        return jnp.where(q < 1.0, 4.0 - 3.0 * q, t * t * (h * inv))

    slope = profile(mine[6], mine[8]) * mine[9] + profile(other[6:7], other[8:9]) * other[9:10]
    w = (mine[7] + other[7:8]) * slope
    gap = (mine[3] - other[3:4]) * dx + (mine[4] - other[4:5]) * dy + (mine[5] - other[5:6]) * dz
    return (w * dx, w * dy, w * dz, w * gap)


def for_all_groups(most, body):
    body(range(FEW), False)

    @pl.loop(FEW, jnp.maximum(most, FEW))
    def _(g):
        body([g], True)


def run_items(number, codes, columns, sources, spread, fields, item, totals):
    def steps(first, count):
        for late in range(0, count, 2):
            places = [decode(codes[way, first + late + n]) for n in range(2) for way in range(WAYS)]
            rows = [pl.multiple_of(place * 8, 8) for place, _, _ in places]
            mine = jnp.concatenate([columns[pl.ds(row, 8), :] for row in rows], axis=0).astype(BF16)
            wide = dot(mine, spread[...])
            for n, (_, one, two) in enumerate(places):
                first_tile, second_tile = sources[one], sources[two]
                other = jnp.where(iota(first_tile.shape, 1) < 64, first_tile, second_tile)
                own = [wide[8 * n : 8 * n + 8, 128 * f : 128 * f + 128] for f in range(fields)]
                for total, term in zip(totals, item(own, other)):
                    total[pl.ds(rows[n], 8), :] += term

    spans = number // (SPAN * WAYS)

    @pl.loop(0, spans)
    def _(span):
        steps(SPAN * span, SPAN)

    rest = number - spans * (SPAN * WAYS)

    @pl.loop(0, (rest + TAIL * WAYS - 1) // (TAIL * WAYS))
    def _(tail):
        steps(SPAN * spans + TAIL * tail, TAIL)


def density_kernel(cols_ref, own_ref, extra_ref, ghost_ref, result_ref, dens_ref, code_ref, rank_ref,
                   sources, columns, spread, total, sums, smooth, codes_s, sem):
    active = extra_ref[pl.ds(1, 64, stride=2), :]
    spread[...] = widener(4, 8)
    rank_ref[...] = ranks_of(active)
    code_ref[...] = item_codes(cols_ref[...], tile_groups(active))
    copy = pltpu.make_async_copy(code_ref, codes_s, sem)
    copy.start()

    def fields(block):
        sub = iota((8, 128), 0)
        return jnp.where(sub < 3, block, jnp.where(sub == 3, NEAR, 0.0))

    def targets(block):
        sub = iota((8, 128), 0)
        return jnp.where(sub < 3, block, jnp.where(sub == 3, 1.0 / block[6:7], 0.0))

    @pl.loop(0, 16)
    def _(step):
        for part in range(4):
            chunk = step * 4 + part
            lanes = pl.ds(pl.multiple_of(step * 512, 512) + 128 * part, 128)
            block = own_ref[:, lanes]
            smooth[pl.ds(chunk, 1), :] = block[6:7]
            put_sources(sources, chunk * 2, fields(block))
            put_sources(sources, chunk * 2 + 128, fields(ghost_ref[:, lanes]))

    sources[256] = jnp.where(iota((8, 128), 0) == 3, FAR, 0.0)
    copy.wait()
    number, most = codes_s[0, STEPS - 1], codes_s[0, STEPS - 2]

    def prepare(groups, again):
        per = 16 if again else 8

        @pl.loop(0, 64 // per)
        def _(step):
            for part in range(per):
                chunk = step * per + part
                lanes = pl.ds(pl.multiple_of(step * (128 * per), 128 * per) + 128 * part, 128)
                put_targets(columns, chunk, targets(own_ref[:, lanes]), rank_ref[pl.ds(chunk, 1), :], groups)
                for g in groups:
                    total[pl.ds(pl.multiple_of(g * 1024 + chunk * 16, 16), 16), :] = jnp.zeros((16, 128), F32)

    for_all_groups(most, prepare)

    run_items(number, codes_s, columns, sources, spread, 4, density_item, (total,))

    def collect(groups, again):
        per = 16 if again else 8

        @pl.loop(0, 64 // per)
        def _(step):
            for part in range(per):
                chunk = step * per + part
                (got,) = gather_sums([total], chunk * 2, rank_ref[pl.ds(chunk, 1), :], groups)
                at = pl.ds(chunk, 1)
                sums[at, :] = sums[at, :] + got if again else got

    for_all_groups(most, collect)
    h = smooth[...]
    fresh = MASS / math.pi / (h * h * h) * (1.0 + 0.25 * sums[...])
    fresh = jnp.where(rank_ref[...] >= 0.0, fresh, extra_ref[pl.ds(0, 64, stride=2), :])
    dens_ref[...] = fresh
    result_ref[...] = fresh


def force_kernel(code_ref, own_ref, ghost_ref, dens_ref, gdens_ref, rank_ref, acc_ref, heat_ref,
                 sources, columns, spread, ax, ay, az, heat):
    number, most = code_ref[0, STEPS - 1], code_ref[0, STEPS - 2]
    spread[...] = widener(10, 16)

    def fields(block, density):
        h = block[6:7]
        press = (5.0 / 3.0 - 1.0) * block[7:8] / density
        hinv = 1.0 / h
        scale = (0.375 * MASS / math.pi) / (h * h * h * h * h)
        near = jnp.full((1, 128), NEAR, F32)
        return jnp.concatenate([block[0:7], press, hinv, scale, near, jnp.zeros((5, 128), F32)], axis=0)

    def own_fields(step, part, per):
        lanes = pl.ds(pl.multiple_of(step * (128 * per), 128 * per) + 128 * part, 128)
        return fields(own_ref[:, lanes], dens_ref[pl.ds(step * per + part, 1), :])

    @pl.loop(0, 16)
    def _(step):
        for part in range(4):
            chunk = step * 4 + part
            lanes = pl.ds(pl.multiple_of(step * 512, 512) + 128 * part, 128)
            put_sources(sources, chunk * 2, own_fields(step, part, 4))
            put_sources(sources, chunk * 2 + 128, fields(ghost_ref[:, lanes], gdens_ref[pl.ds(chunk, 1), :]))

    def prepare(groups, again):
        per = 16 if again else 8

        @pl.loop(0, 64 // per)
        def _(step):
            for part in range(per):
                chunk = step * per + part
                put_targets(columns, chunk, own_fields(step, part, per), rank_ref[pl.ds(chunk, 1), :], groups)
                for g in groups:
                    for total in (ax, ay, az, heat):
                        total[pl.ds(pl.multiple_of(g * 1024 + chunk * 16, 16), 16), :] = jnp.zeros((16, 128), F32)

    for_all_groups(most, prepare)
    sub = iota((16, 128), 0)
    sources[256] = jnp.where(sub == 10, FAR, jnp.where((sub == 6) | (sub == 8), 1.0, 0.0))

    run_items(number, code_ref, columns, sources, spread, 10, force_item, (ax, ay, az, heat))

    def collect(groups, again):
        per = 16 if again else 8

        @pl.loop(0, 64 // per)
        def _(step):
            for part in range(per):
                chunk = step * per + part
                got = gather_sums([ax, ay, az, heat], chunk * 2, rank_ref[pl.ds(chunk, 1), :], groups)
                lanes = pl.ds(pl.multiple_of(step * (128 * per), 128 * per) + 128 * part, 128)
                at = pl.ds(chunk, 1)
                for n in range(3):
                    acc_ref[n : n + 1, lanes] = acc_ref[n : n + 1, lanes] + got[n] if again else got[n]
                heat_ref[at, :] = heat_ref[at, :] - 0.5 * got[3] if again else -0.5 * got[3]

    for_all_groups(most, collect)


VM = pl.BlockSpec(memory_space=pltpu.VMEM)
SM = pl.BlockSpec(memory_space=pltpu.SMEM)


def density_step(columns, own, extra, ghost):
    return pl.pallas_call(
        density_kernel,
        name="density",
        out_shape=(
            jax.ShapeDtypeStruct((64, 128), F32),
            jax.ShapeDtypeStruct((64, 128), F32),
            jax.ShapeDtypeStruct((WAYS, STEPS), I32),
            jax.ShapeDtypeStruct((64, 128), F32),
        ),
        in_specs=[VM, VM, VM, VM],
        out_specs=(VM, VM, VM, VM),
        scratch_shapes=[
            pltpu.VMEM((257, 8, 128), F32),
            pltpu.VMEM((8192, 128), F32),
            pltpu.VMEM((128, 512), BF16),
            pltpu.VMEM((8192, 128), F32),
            pltpu.VMEM((64, 128), F32),
            pltpu.VMEM((64, 128), F32),
            pltpu.SMEM((WAYS, STEPS), I32),
            pltpu.SemaphoreType.DMA,
        ],
        compiler_params=pltpu.CompilerParams(vmem_limit_bytes=24 << 20),
    )(columns, own, extra, ghost)


def force_step(codes, own, ghost, density, ghost_density, rank):
    return pl.pallas_call(
        force_kernel,
        name="force",
        out_shape=(jax.ShapeDtypeStruct((3, 8192), F32), jax.ShapeDtypeStruct((64, 128), F32)),
        in_specs=[SM, VM, VM, VM, VM, VM],
        out_specs=(VM, VM),
        scratch_shapes=[pltpu.VMEM((257, 16, 128), F32), pltpu.VMEM((8192, 128), F32), pltpu.VMEM((128, 1280), BF16)]
        + [pltpu.VMEM((8192, 128), F32)] * 4,
        compiler_params=pltpu.CompilerParams(vmem_limit_bytes=40 << 20),
    )(codes, own, ghost, density, ghost_density, rank)


LEVELS = 4
SEND = 2048
PIECE = 512
BLOCK = 1024
DENSE = 512
DENSE_X = 512
PIECES = SEND // PIECE
GHOSTS = 1024
MESH = pl.DeviceIdType.MESH


def flipped(index, bit):
    step = 1 << bit
    return index + step - 2 * step * ((index // step) % 2)


def neighbour(number, sign, count_x, count_y):
    cell = number + number // 4
    i = (lax.axis_index("gx") + sign * (cell // 3 - 1) + count_x) % count_x
    j = (lax.axis_index("gy") + sign * (cell % 3 - 1) + count_y) % count_y
    return i, j


def spread_state(own, parts):
    for h in range(0, own.shape[1] // 256, 2):
        pair = jnp.concatenate([own[:, h * 256 : h * 256 + 256], own[:, h * 256 + 256 : h * 256 + 512]], axis=0)
        for n, part in enumerate(split3(pair)):
            parts[n, h * 8 : h * 8 + 16, :] = part


def permuted(value, lanes):
    return jnp.take_along_axis(value, lanes, axis=1, mode="promise_in_bounds")


def one_hot(index_row):
    low = jnp.bitwise_and(index_row, 255)
    return jnp.where(iota((256, index_row.shape[1]), 0) == low, 1.0, 0.0).astype(BF16)


def chosen(read, bits, first, count):
    if count == 1:
        return read(first)
    half = count // 2
    low = chosen(read, bits, first, half)
    high = chosen(read, bits, first + half, half)
    return jnp.where(bits[half.bit_length() - 1], high, low)


def digits_of(value, count):
    return [jnp.bitwise_and(value, 1 << n) != 0 for n in range(count)]


def rows_at(state, index):
    index = jnp.broadcast_to(index, (8, 128))
    low = jnp.bitwise_and(index, 127)
    return chosen(lambda c: permuted(state[:, 128 * c : 128 * c + 128], low), digits_of(index >> 7, 6), 0, 64)


def rows_by_matmul(parts, index):
    blocks = parts.shape[1] // 8
    hot = one_hot(index)
    found = dot(parts[2], hot) + dot(parts[1], hot) + dot(parts[0], hot)
    bits = digits_of(jnp.broadcast_to(index, (8, 256)) >> 8, blocks.bit_length() - 1)
    return chosen(lambda h: found[8 * h : 8 * h + 8], bits, 0, blocks)


def pairs_at(extra, index, groups):
    index = jnp.broadcast_to(index, (8, 128))
    low = jnp.bitwise_and(index, 127)
    bits = digits_of(index >> 9, groups.bit_length() - 1)
    out = chosen(lambda g: permuted(extra[8 * g : 8 * g + 8, :], low), bits, 0, groups)
    out = jnp.where(iota((8, 128), 0) >> 1 == jnp.bitwise_and(index >> 7, 3), out, 0.0)
    out = out + pltpu.roll(out, 4, 0)
    return out + pltpu.roll(out, 2, 0)


def cells_at(table, index):
    index = jnp.broadcast_to(index, (8, 128))
    low, high = jnp.bitwise_and(index, 127), (index >> 7) - iota((8, 128), 0)
    out = jnp.zeros((8, 128), table.dtype)
    for v in range(8):
        out = jnp.where(high == 8 * v, permuted(table[8 * v : 8 * v + 8, :], low), out)
    return jnp.sum(out, axis=0, keepdims=True)


def landed(read, slot, old):
    low = jnp.bitwise_and(slot, 127)
    new = chosen(lambda c: permuted(read(c), low), digits_of(slot >> 7, 4), 0, 16)
    return jnp.where(slot >= 0, new, old)


def exchange_kernel(count_x, count_y, used, counts_h, particles_h, old_h, active_h, rows_h, exports_h, pairs_h,
                    own, extra, ghost, columns, exports_3,
                    loads, counts, old, active, rows, exports, pairs, parts, parts_in, hot, inverse, inverse_wide, slots, slots_x, base_main, base_extra,
                    send_main, send_extra, recv_main, recv_extra, recv_wide,
                    send_ghost, send_sems, recv_sems, ghost_send, ghost_recv):
    i, j = lax.axis_index("gx"), lax.axis_index("gy")
    bits_x, bits_y = count_x.bit_length() - 1, count_y.bit_length() - 1
    partners = [
        (flipped(i, bits_x - 1), j),
        (flipped(i, bits_x - 2), j),
        (i, flipped(j, bits_y - 1)),
        (i, flipped(j, bits_y - 2)),
    ]
    copies = [
        pltpu.make_async_copy(source, target, loads.at[n])
        for n, (source, target) in enumerate(
            ((rows_h, rows), (counts_h, counts), (particles_h, own), (old_h, old), (active_h, active), (exports_h, exports), (pairs_h, pairs))
        )
    ]
    for copy in copies:
        copy.start()
    barrier = pltpu.get_barrier_semaphore()
    for partner in partners:
        pl.semaphore_signal(barrier, inc=1, device_id=partner, device_id_type=MESH)
    for number in range(8):
        pl.semaphore_signal(barrier, inc=1, device_id=neighbour(number, 1, count_x, count_y), device_id_type=MESH)

    def invert(level):
        slot = iota((32, SEND), 1)
        index = rows[level : level + 1, :]
        high = jnp.where(slot < counts[0:1, level : level + 1], jnp.broadcast_to(index >> 8, (32, SEND)), 64)
        here = iota((32, SEND), 0) == high
        digits = jnp.concatenate(
            [
                jnp.where(here, ((slot >> 7) + 1).astype(F32), 0.0),
                jnp.where(here, jnp.bitwise_and(slot, 127).astype(F32), 0.0),
            ],
            axis=0,
        ).astype(BF16)
        for piece in range(PIECES):
            hot[:, piece * PIECE : piece * PIECE + PIECE] = one_hot(index[:, piece * PIECE : piece * PIECE + PIECE])
        found = dot_nt(digits, hot[...])
        found = (128.0 * (found[0:32] - 1.0) + found[32:64]).astype(I32)
        for part in range(2):
            value = found[:, 128 * part : 128 * part + 128]
            inverse[pl.ds(part, 32, stride=2), :] = value
            for field in range(2):
                inverse_wide[level, pl.ds(2 * part + field, 32, stride=4), :] = value

    def main_copy(level, piece):
        lanes = pl.ds(pl.multiple_of(piece * PIECE, PIECE), PIECE)
        return pltpu.make_async_remote_copy(
            src_ref=send_main.at[level, :, lanes],
            dst_ref=recv_main.at[level, :, lanes],
            send_sem=send_sems.at[level, piece],
            recv_sem=recv_sems.at[level, piece],
            device_id=partners[level],
            device_id_type=MESH,
        )

    def extra_copy(level):
        return pltpu.make_async_remote_copy(
            src_ref=send_extra.at[level],
            dst_ref=recv_extra.at[level],
            send_sem=send_sems.at[level, PIECES],
            recv_sem=recv_sems.at[level, PIECES],
            device_id=partners[level],
            device_id_type=MESH,
        )

    def ghost_copy(number):
        lanes = pl.ds(pl.multiple_of(number * GHOSTS, GHOSTS), GHOSTS)
        return pltpu.make_async_remote_copy(
            src_ref=send_ghost.at[:, lanes],
            dst_ref=ghost.at[:, lanes],
            send_sem=ghost_send.at[number],
            recv_sem=ghost_recv.at[number],
            device_id=neighbour(number, 1, count_x, count_y),
            device_id_type=MESH,
        )

    def gather(level, out):
        spread_state(own, parts)

        @pl.loop(0, SEND // BLOCK)
        def _(block):
            at = pl.multiple_of(block * BLOCK, BLOCK)
            for k in range(0, DENSE, 256):
                out[:, pl.ds(at + k, 256)] = rows_by_matmul(parts, rows[level : level + 1, pl.ds(at + k, 256)])
            for k in range(0, BLOCK, 128):
                index = rows[level : level + 1, pl.ds(at + k, 128)]
                base_extra[:, pl.ds(at + k, 128)] = pairs_at(extra, index, 16)
                if k >= DENSE:
                    out[:, pl.ds(at + k, 128)] = rows_at(own, index)

    def compose(level):
        @pl.loop(0, PIECES)
        def _(piece):
            for k in range(PIECE // 128):
                at = pl.multiple_of(piece * PIECE + 128 * k, 128)
                slots[:, pl.ds(at, 128)] = cells_at(inverse, rows[level : level + 1, pl.ds(at, 128)])

    def send(level):
        for piece in range(PIECES):
            for k in range(PIECE // 128):
                c = piece * (PIECE // 128) + k
                lanes = slice(128 * c, 128 * c + 128)
                both = base_extra[:, lanes]
                if level > 0:
                    slot = jnp.broadcast_to(slots[:, lanes], (8, 128))
                    send_main[level, :, lanes] = landed(
                        lambda n: recv_main[level - 1, :, 128 * n : 128 * n + 128], slot, base_main[:, lanes]
                    )
                    fresh = pairs_at(recv_extra.at[level - 1], jnp.maximum(slots[:, lanes], 0), 4)
                    both = jnp.where(slot >= 0, fresh, both)
                send_extra[level, 2 * c : 2 * c + 2, :] = both[0:2]
            main_copy(level, piece).start()
        extra_copy(level).start()

    def arrive(level):
        extra_copy(level).wait()
        for piece in range(PIECES):
            main_copy(level, piece).wait()

    def settle(level):
        spread_state(recv_main.at[level], parts_in)
        for c in range(16):
            wide = jnp.concatenate([recv_extra[level, 2 * c : 2 * c + 2, :]] * 4, axis=0)
            recv_wide[:, 128 * c : 128 * c + 128] = wide

        @pl.loop(0, 4)
        def _(step):
            for late in range(4):
                g = step * 4 + late
                at = pl.multiple_of(g * 8, 8)
                slot = inverse_wide[level, pl.ds(at, 8), :]
                extra[pl.ds(at, 8), :] = landed(
                    lambda c: recv_wide[:, 128 * c : 128 * c + 128], slot, extra[pl.ds(at, 8), :]
                )
                first = pl.multiple_of(g * 512, 512)
                for b in range(0, 2):
                    lanes = pl.ds(first + 128 * b, 128)
                    slot_b = jnp.broadcast_to(slot[2 * b : 2 * b + 1], (8, 128))
                    own[:, lanes] = landed(
                        lambda c: recv_main[level, :, 128 * c : 128 * c + 128], slot_b, own[:, lanes]
                    )
                lanes = pl.ds(first + 256, 256)
                slot_row = jnp.concatenate([slot[4:5], slot[6:7]], axis=1)
                fresh = rows_by_matmul(parts_in, slot_row)
                own[:, lanes] = jnp.where(jnp.broadcast_to(slot_row, (8, 256)) >= 0, fresh, own[:, lanes])

    for copy in copies:
        copy.wait()
    extra[pl.ds(0, 64, stride=2), :] = old[...]
    extra[pl.ds(1, 64, stride=2), :] = active[...].astype(F32)
    for number in range(8):
        exports_3[number] = exports[number : number + 1, :]
    gather(0, send_main.at[0])
    pl.semaphore_wait(barrier, 12)

    for level in range(LEVELS):
        send(level)
        if level == 0:
            columns[...] = pair_columns(pairs[...].astype(F32), used[0])
        invert(level)
        if level > 0:
            settle(level - 1)
        if level + 1 < LEVELS:
            compose(level + 1)
            gather(level + 1, base_main)
        else:

            spread_state(own, parts)

            @pl.loop(0, 8)
            def _(number):
                at = pl.multiple_of(number * GHOSTS, GHOSTS)
                for k in range(0, DENSE_X, 256):
                    send_ghost[:, pl.ds(at + k, 256)] = rows_by_matmul(parts, exports_3[number, :, k : k + 256])
                for k in range(0, GHOSTS, 128):
                    index = exports_3[number, :, k : k + 128]
                    slots_x[number, :, k : k + 128] = cells_at(inverse, index)
                    if k >= DENSE_X:
                        send_ghost[:, pl.ds(at + k, 128)] = rows_at(own, index)

        arrive(level)

    @pl.loop(0, 8)
    def _(number):
        for k in range(8):
            lanes = pl.ds(pl.multiple_of(number * GHOSTS, GHOSTS) + 128 * k, 128)
            slot = jnp.broadcast_to(slots_x[number, :, 128 * k : 128 * k + 128], (8, 128))
            send_ghost[:, lanes] = landed(
                lambda n: recv_main[LEVELS - 1, :, 128 * n : 128 * n + 128], slot, send_ghost[:, lanes]
            )
        ghost_copy(number).start()

    settle(LEVELS - 1)
    for number in range(8):
        ghost_copy(number).wait()


HB = pl.BlockSpec(memory_space=pltpu.HBM)


def exchange(mesh, send_count, pair_count, particles, old, active, send_rows, export_rows, pair_tiles):
    count_x, count_y = mesh.shape["gx"], mesh.shape["gy"]
    return pl.pallas_call(
        functools.partial(exchange_kernel, count_x, count_y),
        name="exchange",
        out_shape=(
            jax.ShapeDtypeStruct((8, 8192), F32),
            jax.ShapeDtypeStruct((128, 128), F32),
            jax.ShapeDtypeStruct((8, 8192), F32),
            jax.ShapeDtypeStruct((8, COLS), F32),
            jax.ShapeDtypeStruct((8, 1, GHOSTS), I32),
        ),
        in_specs=[SM, HB, HB, HB, HB, HB, HB, HB],
        out_specs=(VM, VM, VM, VM, VM),
        scratch_shapes=[
            pltpu.SemaphoreType.DMA((7,)),
            pltpu.VMEM((1, 4), I32),
            pltpu.VMEM((64, 128), F32),
            pltpu.VMEM((64, 128), I32),
            pltpu.VMEM((LEVELS, SEND), I32),
            pltpu.VMEM((8, GHOSTS), I32),
            pltpu.VMEM((2, 512), I32),
            pltpu.VMEM((3, 256, 256), BF16),
            pltpu.VMEM((3, SEND // 32, 256), BF16),
            pltpu.VMEM((256, SEND), BF16),
            pltpu.VMEM((64, 128), I32),
            pltpu.VMEM((LEVELS, 128, 128), I32),
            pltpu.VMEM((1, SEND), I32),
            pltpu.VMEM((8, 1, GHOSTS), I32),
            pltpu.VMEM((8, SEND), F32),
            pltpu.VMEM((8, SEND), F32),
            pltpu.VMEM((LEVELS, 8, SEND), F32),
            pltpu.VMEM((LEVELS, 32, 128), F32),
            pltpu.VMEM((LEVELS, 8, SEND), F32),
            pltpu.VMEM((LEVELS, 32, 128), F32),
            pltpu.VMEM((8, SEND), F32),
            pltpu.VMEM((8, 8 * GHOSTS), F32),
            pltpu.SemaphoreType.DMA((LEVELS, PIECES + 1)),
            pltpu.SemaphoreType.DMA((LEVELS, PIECES + 1)),
            pltpu.SemaphoreType.DMA((8,)),
            pltpu.SemaphoreType.DMA((8,)),
        ],
        compiler_params=pltpu.CompilerParams(
            collective_id=0, has_side_effects=True, vmem_limit_bytes=24 << 20
        ),
    )(
        pair_count,
        *[
            pltpu.with_memory_space_constraint(x, pltpu.HBM)
            for x in (send_count, particles, old, active, send_rows, export_rows, pair_tiles)
        ],
    )


def ghost_density_kernel(count_x, count_y, density, exports_3, out, send, send_sems, recv_sems):
    barrier = pltpu.get_barrier_semaphore()
    for number in range(8):
        pl.semaphore_signal(barrier, inc=1, device_id=neighbour(number, 1, count_x, count_y), device_id_type=MESH)

    def copy(number):
        return pltpu.make_async_remote_copy(
            src_ref=send.at[number],
            dst_ref=out.at[number],
            send_sem=send_sems.at[number],
            recv_sem=recv_sems.at[number],
            device_id=neighbour(number, 1, count_x, count_y),
            device_id_type=MESH,
        )

    def gathered(number):
        for k in range(8):
            send[number, k : k + 1, :] = cells_at(density, exports_3[number, :, 128 * k : 128 * k + 128])

    @pl.loop(0, 2)
    def _(half):
        for n in range(4):
            gathered(half * 4 + n)

    pl.semaphore_wait(barrier, 8)
    for number in range(8):
        copy(number).start()

    for number in range(8):
        copy(number).wait()


def ghost_density_step(mesh, density, export_rows):
    return pl.pallas_call(
        functools.partial(ghost_density_kernel, mesh.shape["gx"], mesh.shape["gy"]),
        name="ghost_density",
        out_shape=jax.ShapeDtypeStruct((8, 8, 128), F32),
        in_specs=[VM, VM],
        out_specs=VM,
        scratch_shapes=[
            pltpu.VMEM((8, 8, 128), F32),
            pltpu.SemaphoreType.DMA((8,)),
            pltpu.SemaphoreType.DMA((8,)),
        ],
        compiler_params=pltpu.CompilerParams(collective_id=1, has_side_effects=True, vmem_limit_bytes=8 << 20),
    )(density, export_rows)


def on_device(
    mesh, particles, old_density, active, send_rows, send_count, export_rows, pair_tiles, pair_count
):
    own, extra, ghost, columns, exports = exchange(
        mesh,
        send_count.T,
        pair_count,
        particles,
        old_density.reshape(64, 128),
        active.reshape(64, 128),
        send_rows,
        export_rows,
        pair_tiles,
    )
    result, density, codes, rank = density_step(columns, own, extra, ghost)
    ghost_density = ghost_density_step(mesh, density, exports).reshape(64, 128)
    acceleration, heating = force_step(codes, own, ghost, density, ghost_density, rank)
    return result.reshape(8192), acceleration, heating.reshape(8192)


def solution(mesh):
    in_specs = (
        P(None, ("gx", "gy")),
        P(("gx", "gy")),
        P(("gx", "gy")),
        P(None, ("gx", "gy")),
        P(None, ("gx", "gy")),
        P(None, ("gx", "gy")),
        P(None, ("gx", "gy")),
        P(("gx", "gy")),
    )
    out_specs = (P(("gx", "gy")), P(None, ("gx", "gy")), P(("gx", "gy")))
    return jax.shard_map(
        functools.partial(on_device, mesh), mesh=mesh, in_specs=in_specs, out_specs=out_specs, check_vma=False
    )
```
